256 devices in a mesh: row: 8 (over x, core), col: 32 (over y, z).
Axes of the slice: x: 4, y: 4, z: 8, core: 2. Of those that a mesh axis runs over, the one named last changes fastest.
Arguments:
- matrix: float32 [16384, 16384], P('row', 'col'), may hold values from 0 to 2, as said below
Outputs:
- factored: float32 [16384, 16384], P('row', 'col')
The draws below stay inside these ranges and needn't reach their ends.
Inputs may be any that keep to these rules, and one draw needn't show every extreme that they name: In grid order, the matrix is the leading 16384 columns of a symmetric positive definite matrix of order 16384.
All inputs are finite; a program needn't handle non-finite values.
Results may differ from the reference program's by a relative error of at most 0.0011.
Values may be sent and summed in bfloat16 or wider, within the bound.
No kernel may reach another device: no remote copies, remote signals or barrier semaphores. Data moves between devices by JAX's collectives and lax.ppermute only.
A program may use at most 64 MiB of HBM per device.

```python
import jax
import jax.numpy as jnp
from jax import lax

TILE = 256
TR = 8
TC = 2
PANELS = 3
N_ROW = 8
N_COL = 32


def draw_matrix(key, part):
    point_key = jax.random.fold_in(key, 11)
    total_rows = TR * TILE * N_ROW
    total_cols = TC * TILE * N_COL
    stored_row = jnp.arange(total_rows, dtype=jnp.int32)
    row_device = stored_row // (TR * TILE)
    row_rest = stored_row % (TR * TILE)
    grid_row = (row_rest // TILE * N_ROW + row_device) * TILE + row_rest % TILE
    stored_col = jnp.arange(total_cols, dtype=jnp.int32)
    col_device = stored_col // (TC * TILE)
    col_rest = stored_col % (TC * TILE)
    grid_col = (col_rest // TILE * N_COL + col_device) * TILE + col_rest % TILE
    extents = jnp.array([1.0, 1.0, 1.0], dtype=jnp.float32)
    coordinates = jax.random.uniform(point_key, (3, total_rows), jnp.float32, 0.0, 1.0) * extents[:, None]
    row_points = coordinates[:, grid_row]
    col_points = coordinates[:, grid_col]
    squared = jnp.zeros((total_rows, total_cols), jnp.float32)
    for axis_number in range(3):
        offset = row_points[axis_number][:, None] - col_points[axis_number][None, :]
        squared = squared + offset * offset
    distance = jnp.sqrt(squared)
    on_diagonal = grid_row[:, None] == grid_col[None, :]
    values = jnp.exp(-distance / 0.25)
    nugget = 0.5
    return values + jnp.where(on_diagonal, jnp.float32(nugget), jnp.float32(0.0))


def setup_inputs(seed: int = 0) -> dict:
    splits = jax.random.split(jax.random.key(seed), 2)
    matrix = draw_matrix(jax.random.fold_in(splits[1], 71), 0)
    return {"matrix": matrix}


def factor_tile(square):
    factor = jnp.linalg.cholesky(square)
    eye_tile = jnp.eye(square.shape[0], dtype=square.dtype)
    inverse = jax.scipy.linalg.solve_triangular(factor, eye_tile, lower=True)
    return (factor, inverse)

def to_columns(stored):
    shaped = stored.reshape(N_ROW, TR, TILE, N_COL, TC, TILE)
    return shaped.transpose(4, 3, 1, 0, 2, 5).reshape(TC * N_COL, TR * N_ROW * TILE, TILE)

def from_columns(columns):
    shaped = columns.reshape(TC, N_COL, TR, N_ROW, TILE, TILE)
    return shaped.transpose(3, 2, 4, 1, 0, 5).reshape(N_ROW * TR * TILE, N_COL * TC * TILE)

def reference(matrix):
    grid_tiles = to_columns(matrix)
    total_rows = grid_tiles.shape[1]
    total_tiles = grid_tiles.shape[0]
    row_tile = jnp.arange(total_rows, dtype=jnp.int32) // TILE
    for panel_step in range(PANELS):
        first_row = panel_step * TILE
        column_old = grid_tiles[panel_step]
        factor, inverse = factor_tile(column_old[first_row:first_row + TILE])
        solved = jnp.dot(column_old.astype(jnp.float32), inverse.T.astype(jnp.float32), precision=lax.Precision.HIGHEST, preferred_element_type=jnp.float32)
        below_step = (row_tile > panel_step)[:, None]
        solved = jnp.where(below_step, solved, jnp.float32(0.0))
        rounded = solved.astype(jnp.bfloat16)

        def update_tile(operands):
            column_block, tile_index = operands
            partner = lax.dynamic_slice_in_dim(rounded, tile_index * TILE, TILE, 0)
            product = jnp.dot(rounded.astype(jnp.float32), partner.T.astype(jnp.float32), preferred_element_type=jnp.float32)
            keep_tile = jnp.logical_and(row_tile >= tile_index, tile_index > panel_step)
            return column_block - jnp.where(keep_tile[:, None], product, jnp.float32(0.0))
        grid_tiles = lax.map(update_tile, (grid_tiles, jnp.arange(total_tiles, dtype=jnp.int32)))
        new_column = column_old.at[first_row:first_row + TILE].set(factor)
        new_column = jnp.where(below_step, solved, new_column)
        grid_tiles = grid_tiles.at[panel_step].set(new_column)
    return from_columns(grid_tiles)
```

```python
import jax
import jax.numpy as jnp
from jax import lax
from jax.experimental import pallas as pl
from jax.experimental.pallas import tpu as pltpu
from jax.sharding import PartitionSpec as P

TILE = 256
PANELS = 3
NB = 64
PIV = 8
N_ROW = 8
N_Y = 4
N_Z = 8
SUB = TILE // 8
HALVES = 2
F32 = jnp.float32
BF16 = jnp.bfloat16
HIGHEST = lax.Precision.HIGHEST
LOWER = [(0, 0), (1, 0), (1, 1), (2, 0), (2, 1), (2, 2)]


def dot_nn(a, b):
    return lax.dot_general(a, b, (((1,), (0,)), ((), ())), precision=HIGHEST, preferred_element_type=F32)


def dot_nt(a, b):
    return lax.dot_general(a, b, (((1,), (1,)), ((), ())), precision=HIGHEST, preferred_element_type=F32)


def dot_bf(a, b):
    return lax.dot_general(a, b, (((1,), (1,)), ((), ())), preferred_element_type=F32)


def y_shift(x, s):
    pairs = [(y * N_Z + z, (y + s) % N_Y * N_Z + z) for y in range(N_Y) for z in range(N_Z)]
    return lax.ppermute(x, "col", pairs)


def z_shift(x, s):
    pairs = [(y * N_Z + z, y * N_Z + (z + s) % N_Z) for y in range(N_Y) for z in range(N_Z)]
    return lax.ppermute(x, "col", pairs)


def row_shift(x, s):
    return lax.ppermute(x, "row", [(r, (r + s) % N_ROW) for r in range(N_ROW)])


def row_z_swap(x):
    n_col = N_Y * N_Z
    pairs = [
        (r * n_col + y * N_Z + z, z * n_col + y * N_Z + r)
        for r in range(N_ROW)
        for y in range(N_Y)
        for z in range(N_Z)
    ]
    return lax.ppermute(x, ("row", "col"), pairs)


SMEM = pl.BlockSpec(memory_space=pltpu.SMEM)
ANY = pl.BlockSpec(memory_space=pl.ANY)
VMEM = pl.BlockSpec(memory_space=pltpu.VMEM)


def pack_top_kernel(idx, tile, *outs):
    r = idx[0]
    for s in range(N_ROW):
        base = pl.multiple_of((r + s) % N_ROW * SUB, SUB)
        outs[s][...] = tile[pl.ds(base, SUB), :]


def pack_top(idx, matrix):
    return pl.pallas_call(
        pack_top_kernel,
        grid=(1,),
        out_shape=[jax.ShapeDtypeStruct((SUB, TILE), F32)] * N_ROW,
        in_specs=[SMEM, pl.BlockSpec((TILE, TILE), lambda i: (0, 0))],
        out_specs=[pl.BlockSpec((SUB, TILE), lambda i: (0, 0))] * N_ROW,
        name="pack_top",
    )(idx, matrix)


def pack_y_kernel(idx, matrix, *rest):
    outs, sem = rest[:N_Y], rest[N_Y]
    y = idx[1]
    copies = []
    for s in range(N_Y):
        for h in range(HALVES):
            base = pl.multiple_of(((y + s) % N_Y + h * N_Y) * TILE, TILE)
            copies.append(
                pltpu.make_async_copy(
                    matrix.at[pl.ds(base, TILE), pl.ds(0, TILE)], outs[s].at[h], sem.at[s * HALVES + h]
                )
            )
    for copy in copies:
        copy.start()
    for copy in copies:
        copy.wait()


def pack_y(idx, matrix):
    return pl.pallas_call(
        pack_y_kernel,
        out_shape=[jax.ShapeDtypeStruct((HALVES, TILE, TILE), F32)] * N_Y,
        in_specs=[SMEM, ANY],
        out_specs=[ANY] * N_Y,
        scratch_shapes=[pltpu.SemaphoreType.DMA((N_Y * HALVES,))],
        name="pack_y",
    )(idx, matrix)


def pack_z_kernel(idx, own, *rest):
    got, outs = rest[: N_Y - 1], rest[N_Y - 1 :]
    y, z = idx[1], idx[2]
    for source, ref in enumerate((own,) + tuple(got)):

        @pl.when(y == source)
        def _():
            for s in range(N_Z):
                base = pl.multiple_of((z + s) % N_Z * SUB, SUB)
                outs[s][...] = ref[:, pl.ds(base, SUB), :]


def pack_z(idx, own, got):
    return pl.pallas_call(
        pack_z_kernel,
        out_shape=[jax.ShapeDtypeStruct((HALVES, SUB, TILE), F32)] * N_Z,
        in_specs=[SMEM] + [VMEM] * N_Y,
        out_specs=[VMEM] * N_Z,
        name="pack_z",
    )(idx, own, *got)


def pick_kernel(which, count, idx, *rest):
    got, out = rest[:-1], rest[-1]
    for s, ref in enumerate(got):
        source = (idx[which] + len(got) - s) % len(got)

        @pl.when(source < count)
        def _():
            out[source] = ref[...]


def pick(idx, which, count, got):
    shape = (count,) + got[0].shape
    return pl.pallas_call(
        lambda *refs: pick_kernel(which, count, *refs),
        out_shape=jax.ShapeDtypeStruct(shape, got[0].dtype),
        in_specs=[SMEM] + [VMEM] * len(got),
        out_specs=VMEM,
        name="pick",
    )(idx, *got)


def pick_lower_kernel(idx, *rest):
    got, out = rest[:-1], rest[-1]
    for s, ref in enumerate(got):
        source = (idx[2] + len(got) - s) % len(got)
        for k in range(PANELS):

            @pl.when(source == k)
            def _():
                for n, (i, kk) in enumerate(LOWER):
                    if kk == k:
                        out[n] = ref[i]


def pick_lower(idx, got):
    return pl.pallas_call(
        pick_lower_kernel,
        out_shape=jax.ShapeDtypeStruct((len(LOWER), SUB, TILE), F32),
        in_specs=[SMEM] + [VMEM] * len(got),
        out_specs=VMEM,
        name="pick_lower",
    )(idx, *got)


def eliminate(block):
    sub = lax.broadcasted_iota(jnp.int32, (8, 2 * NB), 0)
    lane = lax.broadcasted_iota(jnp.int32, (8, 2 * NB), 1)
    groups = NB // 8

    def spread(x):
        return jnp.broadcast_to(x, (8, 2 * NB))

    m = []
    for g in range(groups):
        eye = jnp.where(lane == sub + (8 * g + NB), F32(1), F32(0))
        m.append(jnp.concatenate([block[8 * g : 8 * g + 8], eye[:, NB:]], axis=1))
    scale = []
    for g0 in range(groups):
        j = g0 * PIV
        cols = [[spread(m[g][:, j + q : j + q + 1]) for g in range(g0, groups)] for q in range(PIV)]
        rows = [spread(m[g0][q : q + 1, :]) for q in range(PIV)]
        a = {}
        for q in range(PIV):
            for i in range(q, PIV):
                a[i, q] = spread(cols[q][0][i : i + 1, :])
        low = {}
        inv = []
        pivots = None
        for q in range(PIV):
            inv.append(1.0 / a[q, q])
            pivots = a[q, q] if pivots is None else jnp.where(sub >= q, a[q, q], pivots)
            for i in range(q + 1, PIV):
                low[i, q] = a[i, q] * inv[q]
            for jj in range(q + 1, PIV):
                for i in range(jj, PIV):
                    a[i, jj] = a[i, jj] - low[i, q] * a[jj, q]
        scale.append(lax.rsqrt(pivots))
        scaled = []
        for q in range(PIV):
            for i in range(q + 1, PIV):
                rows[i] = rows[i] - low[i, q] * rows[q]
            scaled.append(rows[q] * inv[q])
        for g in range(g0, groups):
            x = [cols[q][g - g0] for q in range(PIV)]
            updated = m[g]
            for q in range(PIV):
                for i in range(q + 1, PIV):
                    x[i] = x[i] - low[i, q] * x[q]
                part = x[q]
                if g == g0:
                    part = jnp.where(sub > q, part, F32(0))
                updated = updated - part * scaled[q]
            m[g] = updated
    return jnp.concatenate([m[g] * scale[g] for g in range(groups)], axis=0)


def chol_inv(w, lc):
    blocks = TILE // NB
    rows = lax.broadcasted_iota(jnp.int32, (2 * TILE, NB), 0)
    r64 = lax.broadcasted_iota(jnp.int32, (NB, NB), 0)
    c64 = lax.broadcasted_iota(jnp.int32, (NB, NB), 1)

    def step(b, carry):
        base = pl.multiple_of(b * NB, NB)
        m = eliminate(w[b, pl.ds(base, NB), :]).T
        lower = jnp.where(r64 >= c64, m[:NB], F32(0))
        inv_t = jnp.where(r64 <= c64, m[NB:], F32(0))
        p = jnp.where(rows >= base + NB, dot_nn(w[b], inv_t), F32(0))
        lc[b] = p
        lc[b, pl.ds(base, NB), :] = lower
        for bj in range(1, blocks):

            @pl.when(bj > b)
            def _():
                w[bj] = w[bj] - dot_nt(p, p[bj * NB : (bj + 1) * NB])

        return carry

    lax.fori_loop(0, blocks, step, 0)


def factor_kernel(idx, *rest):
    got = rest[:N_ROW]
    l_ref, it_ref, lb_ref, top, w, lc, sb = rest[N_ROW:]
    blocks = TILE // NB
    for s in range(N_ROW):
        base = pl.multiple_of((idx[0] + N_ROW - s) % N_ROW * SUB, SUB)
        for n, (i, k) in enumerate(LOWER):
            top[i, k, pl.ds(base, SUB), :] = got[s][n]
    r = lax.broadcasted_iota(jnp.int32, (TILE, NB), 0)
    c = lax.broadcasted_iota(jnp.int32, (TILE, NB), 1)

    def panel(k, carry):
        tile = top[k, k]
        for b in range(blocks):
            w[b, :TILE, :] = tile[:, b * NB : (b + 1) * NB]
            w[b, TILE:, :] = jnp.where(r == c + b * NB, F32(1), F32(0))
        chol_inv(w, lc)
        l_ref[k] = jnp.concatenate([lc[b, :TILE, :] for b in range(blocks)], axis=1)
        inv_t = jnp.concatenate([lc[b, TILE:, :] for b in range(blocks)], axis=1)
        it_ref[k] = inv_t
        for i in range(1, PANELS):

            @pl.when(i > k)
            def _():
                solved = dot_nn(top[i, k], inv_t).astype(BF16)
                sb[i] = solved
                lb_ref[i, k] = solved

        for i in range(1, PANELS):
            for j in range(1, i + 1):

                @pl.when(j > k)
                def _():
                    top[i, j] = top[i, j] - dot_bf(sb[i], sb[j])

        return carry

    lax.fori_loop(0, PANELS, panel, 0)


def factor(idx, got):
    square = (PANELS, TILE, TILE)
    return pl.pallas_call(
        factor_kernel,
        out_shape=[
            jax.ShapeDtypeStruct(square, F32),
            jax.ShapeDtypeStruct(square, F32),
            jax.ShapeDtypeStruct((PANELS, PANELS, TILE, TILE), BF16),
        ],
        in_specs=[SMEM] + [VMEM] * N_ROW,
        out_specs=[VMEM] * 3,
        scratch_shapes=[
            pltpu.VMEM((PANELS, PANELS, TILE, TILE), F32),
            pltpu.VMEM((TILE // NB, 2 * TILE, NB), F32),
            pltpu.VMEM((TILE // NB, 2 * TILE, NB), F32),
            pltpu.VMEM((PANELS, TILE, TILE), BF16),
        ],
        name="factor",
    )(idx, *got)


def solve_kernel(idx, it_ref, lb_ref, *rest):
    got = rest[:N_Z]
    out, rows = rest[N_Z:]
    r, y, z = idx[0], idx[1], idx[2]
    for s in range(N_Z):
        source = (z + N_Z - s) % N_Z

        @pl.when(source < PANELS)
        def _():
            rows[source] = got[s][...]

    chunk = HALVES * SUB
    half = lax.broadcasted_iota(jnp.int32, (chunk, TILE), 0) // SUB
    tile_row = (half * N_Y + y) * N_ROW + r
    done = []
    for k in range(PANELS):
        left = rows[k].reshape(chunk, TILE)
        for j in range(k):
            left = left - dot_bf(done[j], lb_ref[k, j])
        solved = dot_nn(left, it_ref[k])
        done.append(jnp.where(tile_row > k, solved, F32(0)).astype(BF16))
    for k in range(PANELS):
        out[:, :, k * TILE : (k + 1) * TILE] = done[k].reshape(HALVES, SUB, TILE)


def solve(idx, inv_t, low, got):
    return pl.pallas_call(
        solve_kernel,
        out_shape=jax.ShapeDtypeStruct((HALVES, SUB, PANELS * TILE), BF16),
        in_specs=[SMEM] + [VMEM] * (2 + N_Z),
        out_specs=VMEM,
        scratch_shapes=[pltpu.VMEM((PANELS, HALVES, SUB, TILE), F32)],
        name="solve",
    )(idx, inv_t, low, *got)


def join_z_kernel(idx, *rest):
    got, out = rest[:-1], rest[-1]
    for s in range(N_Z):
        base = pl.multiple_of((idx[2] + N_Z - s) % N_Z * SUB, SUB)
        out[:, pl.ds(base, SUB), :] = got[s][...]


def join_z(idx, got):
    return pl.pallas_call(
        join_z_kernel,
        out_shape=jax.ShapeDtypeStruct((HALVES, TILE, PANELS * TILE), BF16),
        in_specs=[SMEM] + [VMEM] * N_Z,
        out_specs=VMEM,
        name="join_z",
    )(idx, *got)


def update_kernel(idx, a_ref, l_ref, it_ref, *rest):
    row_parts, col_parts = rest[:N_Y], rest[N_Y : N_Y + N_ROW]
    out, s_all, c_all, l_own, it_own, row_sem, col_sem, own_sem = rest[N_Y + N_ROW :]
    r, y, c = idx[0], idx[1], idx[3]
    t = pl.program_id(0)
    n_col = N_Y * N_Z

    def row_copy(s, h):
        slot = h * N_Y + (y + N_Y - s) % N_Y
        return pltpu.make_async_copy(row_parts[s].at[h], s_all.at[slot], row_sem.at[slot])

    def col_copy(s, h):
        base = pl.multiple_of((r + N_ROW - s) % N_ROW * SUB, SUB)
        return pltpu.make_async_copy(
            col_parts[s].at[h], c_all.at[h, pl.ds(base, SUB), :], col_sem.at[s * HALVES + h]
        )

    def own_copies():
        return (
            pltpu.make_async_copy(l_ref.at[c], l_own, own_sem.at[0]),
            pltpu.make_async_copy(it_ref.at[c], it_own, own_sem.at[1]),
        )

    @pl.when(t == 0)
    def _():
        for s in range(N_ROW):
            for h in range(HALVES):
                col_copy(s, h).start()
        for h in range(HALVES):
            for s in range(N_Y):
                row_copy(s, h).start()

        @pl.when(c < PANELS)
        def _():
            for copy in own_copies():
                copy.start()
            for copy in own_copies():
                copy.wait()

        for s in range(N_ROW):
            for h in range(HALVES):
                col_copy(s, h).wait()

    pltpu.make_async_copy(row_parts[0].at[0], s_all.at[t], row_sem.at[t]).wait()
    i = t * N_ROW + r
    for u in range(HALVES):
        lanes = slice(u * TILE, (u + 1) * TILE)
        j = c + u * n_col

        @pl.when(i >= j)
        def _():
            out[:, lanes] = a_ref[:, lanes] - dot_bf(s_all[t], c_all[u])

        @pl.when(i < j)
        def _():
            out[:, lanes] = a_ref[:, lanes]

    @pl.when(jnp.logical_and(c < PANELS, i > c))
    def _():
        out[:, :TILE] = dot_nn(out[:, :TILE], it_own[...])

    @pl.when(jnp.logical_and(c < PANELS, i == c))
    def _():
        out[:, :TILE] = l_own[...]


def update(idx, matrix, l_all, inv_t, row_parts, col_parts):
    rows, cols = matrix.shape
    width = PANELS * TILE
    block = pl.BlockSpec((TILE, cols), lambda t: (t, 0))
    return pl.pallas_call(
        update_kernel,
        grid=(rows // TILE,),
        out_shape=jax.ShapeDtypeStruct(matrix.shape, F32),
        in_specs=[SMEM, block] + [ANY] * (2 + N_Y + N_ROW),
        out_specs=block,
        scratch_shapes=[
            pltpu.VMEM((rows // TILE, TILE, width), BF16),
            pltpu.VMEM((HALVES, TILE, width), BF16),
            pltpu.VMEM((TILE, TILE), F32),
            pltpu.VMEM((TILE, TILE), F32),
            pltpu.SemaphoreType.DMA((rows // TILE,)),
            pltpu.SemaphoreType.DMA((N_ROW * HALVES,)),
            pltpu.SemaphoreType.DMA((2,)),
        ],
        name="update",
    )(idx, matrix, l_all, inv_t, *row_parts, *col_parts)


def on_device(matrix):
    row_index = lax.axis_index("row")
    col_index = lax.axis_index("col")
    y_index, z_index = col_index // N_Z, col_index % N_Z
    idx = jnp.stack([row_index, y_index, z_index, col_index]).astype(jnp.int32)

    sent = pack_top(idx, matrix)
    got = [sent[0]] + [row_shift(sent[s], s) for s in range(1, N_ROW)]
    slices = pick(idx, 0, PANELS, got)
    over_y = [slices] + [y_shift(slices, s) for s in range(1, N_Y)]
    slices = lax.select_n(y_index, *over_y)
    lower = pick_lower(idx, [slices] + [z_shift(slices, s) for s in range(1, N_Z)])
    top_parts = [lower] + [row_shift(lower, s) for s in range(1, N_ROW)]

    sent = pack_y(idx, matrix)
    got = [y_shift(sent[s], s) for s in range(1, N_Y)]
    sent = pack_z(idx, sent[0], got)
    panel_parts = [sent[0]] + [z_shift(sent[s], s) for s in range(1, N_Z)]

    l_all, inv_t, low = factor(idx, top_parts)
    solved = solve(idx, inv_t, low, panel_parts)

    swapped = row_z_swap(solved)
    col_parts = [swapped] + [row_shift(swapped, s) for s in range(1, N_ROW)]
    joined = join_z(idx, [solved] + [z_shift(solved, s) for s in range(1, N_Z)])
    row_parts = [joined] + [y_shift(joined, s) for s in range(1, N_Y)]
    return update(idx, matrix, l_all, inv_t, row_parts, col_parts)


def solution(mesh):
    return jax.shard_map(
        on_device, mesh=mesh, in_specs=(P("row", "col"),), out_specs=P("row", "col"), check_vma=False
    )
```

```python
import jax
import jax.numpy as jnp
from jax import lax
from jax.experimental import pallas as pl
from jax.experimental.pallas import tpu as pltpu
from jax.sharding import PartitionSpec as P

TILE = 256
PANELS = 3
NB = 64
PIV = 8
N_ROW = 8
N_Y = 4
N_Z = 8
SUB = TILE // 8
HALVES = 2
F32 = jnp.float32
BF16 = jnp.bfloat16
HIGHEST = lax.Precision.HIGHEST
LOWER = [(0, 0), (1, 0), (1, 1), (2, 0), (2, 1), (2, 2)]


def dot_nn(a, b):
    return lax.dot_general(a, b, (((1,), (0,)), ((), ())), precision=HIGHEST, preferred_element_type=F32)


def dot_nt(a, b):
    return lax.dot_general(a, b, (((1,), (1,)), ((), ())), precision=HIGHEST, preferred_element_type=F32)


def dot_bf(a, b):
    return lax.dot_general(a, b, (((1,), (1,)), ((), ())), preferred_element_type=F32)


def y_shift(x, s):
    pairs = [(y * N_Z + z, (y + s) % N_Y * N_Z + z) for y in range(N_Y) for z in range(N_Z)]
    return lax.ppermute(x, "col", pairs)


def z_shift(x, s):
    pairs = [(y * N_Z + z, y * N_Z + (z + s) % N_Z) for y in range(N_Y) for z in range(N_Z)]
    return lax.ppermute(x, "col", pairs)


def row_shift(x, s):
    return lax.ppermute(x, "row", [(r, (r + s) % N_ROW) for r in range(N_ROW)])


def row_z_swap(x):
    n_col = N_Y * N_Z
    pairs = [
        (r * n_col + y * N_Z + z, z * n_col + y * N_Z + r)
        for r in range(N_ROW)
        for y in range(N_Y)
        for z in range(N_Z)
    ]
    return lax.ppermute(x, ("row", "col"), pairs)


SMEM = pl.BlockSpec(memory_space=pltpu.SMEM)
ANY = pl.BlockSpec(memory_space=pl.ANY)
VMEM = pl.BlockSpec(memory_space=pltpu.VMEM)


def pack_top_kernel(idx, tile, *outs):
    r = idx[0]
    for s in range(N_ROW):
        base = pl.multiple_of((r + s) % N_ROW * SUB, SUB)
        outs[s][...] = tile[pl.ds(base, SUB), :]


def pack_top(idx, matrix):
    return pl.pallas_call(
        pack_top_kernel,
        grid=(1,),
        out_shape=[jax.ShapeDtypeStruct((SUB, TILE), F32)] * N_ROW,
        in_specs=[SMEM, pl.BlockSpec((TILE, TILE), lambda i: (0, 0))],
        out_specs=[pl.BlockSpec((SUB, TILE), lambda i: (0, 0))] * N_ROW,
        name="pack_top",
    )(idx, matrix)


def pack_y_kernel(*refs):
    for s in range(N_Y):
        refs[N_Y + s][...] = refs[s][...]


def pack_y(matrix):
    return pl.pallas_call(
        pack_y_kernel,
        grid=(HALVES,),
        out_shape=[jax.ShapeDtypeStruct((HALVES, TILE, TILE), F32)] * N_Y,
        in_specs=[pl.BlockSpec((TILE, TILE), lambda h, s=s: (h * N_Y + s, 0)) for s in range(N_Y)],
        out_specs=[pl.BlockSpec((None, TILE, TILE), lambda h: (h, 0, 0))] * N_Y,
        name="pack_y",
    )(*[matrix] * N_Y)


def pack_z_kernel(idx, own, *rest):
    got, outs = rest[: N_Y - 1], rest[N_Y - 1 :]
    y, z = idx[1], idx[2]
    for source, ref in enumerate((own,) + tuple(got)):

        @pl.when(y == source)
        def _():
            for s in range(N_Z):
                base = pl.multiple_of((z + s) % N_Z * SUB, SUB)
                outs[s][...] = ref[:, pl.ds(base, SUB), :]


def pack_z(idx, own, got):
    return pl.pallas_call(
        pack_z_kernel,
        out_shape=[jax.ShapeDtypeStruct((HALVES, SUB, TILE), F32)] * N_Z,
        in_specs=[SMEM] + [VMEM] * N_Y,
        out_specs=[VMEM] * N_Z,
        name="pack_z",
    )(idx, own, *got)


def pick_kernel(which, count, idx, *rest):
    got, out = rest[:-1], rest[-1]
    for s, ref in enumerate(got):
        source = (idx[which] + len(got) - s) % len(got)

        @pl.when(source < count)
        def _():
            out[source] = ref[...]


def pick(idx, which, count, got):
    shape = (count,) + got[0].shape
    return pl.pallas_call(
        lambda *refs: pick_kernel(which, count, *refs),
        out_shape=jax.ShapeDtypeStruct(shape, got[0].dtype),
        in_specs=[SMEM] + [VMEM] * len(got),
        out_specs=VMEM,
        name="pick",
    )(idx, *got)


def pick_lower_kernel(idx, *rest):
    got, out = rest[:-1], rest[-1]
    for s, ref in enumerate(got):
        source = (idx[2] + len(got) - s) % len(got)
        for k in range(PANELS):

            @pl.when(source == k)
            def _():
                for n, (i, kk) in enumerate(LOWER):
                    if kk == k:
                        out[n] = ref[i]


def pick_lower(idx, got):
    return pl.pallas_call(
        pick_lower_kernel,
        out_shape=jax.ShapeDtypeStruct((len(LOWER), SUB, TILE), F32),
        in_specs=[SMEM] + [VMEM] * len(got),
        out_specs=VMEM,
        name="pick_lower",
    )(idx, *got)


def eliminate(block):
    sub = lax.broadcasted_iota(jnp.int32, (8, 2 * NB), 0)
    lane = lax.broadcasted_iota(jnp.int32, (8, 2 * NB), 1)
    groups = NB // 8

    def spread(x):
        return jnp.broadcast_to(x, (8, 2 * NB))

    m = []
    for g in range(groups):
        eye = jnp.where(lane == sub + (8 * g + NB), F32(1), F32(0))
        m.append(jnp.concatenate([block[8 * g : 8 * g + 8], eye[:, NB:]], axis=1))
    scale = []
    for g0 in range(groups):
        j = g0 * PIV
        cols = [[spread(m[g][:, j + q : j + q + 1]) for g in range(g0, groups)] for q in range(PIV)]
        rows = [spread(m[g0][q : q + 1, :]) for q in range(PIV)]
        a = {}
        for q in range(PIV):
            for i in range(q, PIV):
                a[i, q] = spread(cols[q][0][i : i + 1, :])
        low = {}
        inv = []
        pivots = None
        for q in range(PIV):
            inv.append(1.0 / a[q, q])
            pivots = a[q, q] if pivots is None else jnp.where(sub >= q, a[q, q], pivots)
            for i in range(q + 1, PIV):
                low[i, q] = a[i, q] * inv[q]
            for jj in range(q + 1, PIV):
                for i in range(jj, PIV):
                    a[i, jj] = a[i, jj] - low[i, q] * a[jj, q]
        scale.append(lax.rsqrt(pivots))
        scaled = []
        for q in range(PIV):
            for i in range(q + 1, PIV):
                rows[i] = rows[i] - low[i, q] * rows[q]
            scaled.append(rows[q] * inv[q])
        for g in range(g0, groups):
            x = [cols[q][g - g0] for q in range(PIV)]
            updated = m[g]
            for q in range(PIV):
                for i in range(q + 1, PIV):
                    x[i] = x[i] - low[i, q] * x[q]
                part = x[q]
                if g == g0:
                    part = jnp.where(sub > q, part, F32(0))
                updated = updated - part * scaled[q]
            m[g] = updated
    return jnp.concatenate([m[g] * scale[g] for g in range(groups)], axis=0)


def chol_inv(w, lc):
    blocks = TILE // NB
    rows = lax.broadcasted_iota(jnp.int32, (2 * TILE, NB), 0)
    r64 = lax.broadcasted_iota(jnp.int32, (NB, NB), 0)
    c64 = lax.broadcasted_iota(jnp.int32, (NB, NB), 1)

    def step(b, carry):
        base = pl.multiple_of(b * NB, NB)
        m = eliminate(w[b, pl.ds(base, NB), :]).T
        lower = jnp.where(r64 >= c64, m[:NB], F32(0))
        inv_t = jnp.where(r64 <= c64, m[NB:], F32(0))
        p = jnp.where(rows >= base + NB, dot_nn(w[b], inv_t), F32(0))
        lc[b] = p
        lc[b, pl.ds(base, NB), :] = lower
        for bj in range(1, blocks):

            @pl.when(bj > b)
            def _():
                w[bj] = w[bj] - dot_nt(p, p[bj * NB : (bj + 1) * NB])

        return carry

    lax.fori_loop(0, blocks, step, 0)


def factor_kernel(idx, *rest):
    got = rest[:N_ROW]
    l_ref, it_ref, lb_ref, top, w, lc, sb = rest[N_ROW:]
    blocks = TILE // NB
    for s in range(N_ROW):
        base = pl.multiple_of((idx[0] + N_ROW - s) % N_ROW * SUB, SUB)
        for n, (i, k) in enumerate(LOWER):
            top[i, k, pl.ds(base, SUB), :] = got[s][n]
    r = lax.broadcasted_iota(jnp.int32, (TILE, NB), 0)
    c = lax.broadcasted_iota(jnp.int32, (TILE, NB), 1)

    def panel(k, carry):
        tile = top[k, k]
        for b in range(blocks):
            w[b, :TILE, :] = tile[:, b * NB : (b + 1) * NB]
            w[b, TILE:, :] = jnp.where(r == c + b * NB, F32(1), F32(0))
        chol_inv(w, lc)
        l_ref[k] = jnp.concatenate([lc[b, :TILE, :] for b in range(blocks)], axis=1)
        inv_t = jnp.concatenate([lc[b, TILE:, :] for b in range(blocks)], axis=1)
        it_ref[k] = inv_t
        for i in range(1, PANELS):

            @pl.when(i > k)
            def _():
                solved = dot_nn(top[i, k], inv_t).astype(BF16)
                sb[i] = solved
                lb_ref[i, k] = solved

        for i in range(1, PANELS):
            for j in range(1, i + 1):

                @pl.when(j > k)
                def _():
                    top[i, j] = top[i, j] - dot_bf(sb[i], sb[j])

        return carry

    lax.fori_loop(0, PANELS, panel, 0)


def factor(idx, got):
    square = (PANELS, TILE, TILE)
    return pl.pallas_call(
        factor_kernel,
        out_shape=[
            jax.ShapeDtypeStruct(square, F32),
            jax.ShapeDtypeStruct(square, F32),
            jax.ShapeDtypeStruct((PANELS, PANELS, TILE, TILE), BF16),
        ],
        in_specs=[SMEM] + [VMEM] * N_ROW,
        out_specs=[VMEM] * 3,
        scratch_shapes=[
            pltpu.VMEM((PANELS, PANELS, TILE, TILE), F32),
            pltpu.VMEM((TILE // NB, 2 * TILE, NB), F32),
            pltpu.VMEM((TILE // NB, 2 * TILE, NB), F32),
            pltpu.VMEM((PANELS, TILE, TILE), BF16),
        ],
        name="factor",
    )(idx, *got)


def pick_panel_kernel(idx, *rest):
    got, out = rest[:-1], rest[-1]
    for s in range(N_Z):
        source = (idx[2] + N_Z - s) % N_Z
        for k in range(PANELS):

            @pl.when(source == k)
            def _():
                out[:, :, k * TILE : (k + 1) * TILE] = got[s][...]


def pick_panel(idx, got):
    return pl.pallas_call(
        pick_panel_kernel,
        out_shape=jax.ShapeDtypeStruct((HALVES, SUB, PANELS * TILE), F32),
        in_specs=[SMEM] + [VMEM] * N_Z,
        out_specs=VMEM,
        name="pick_panel",
    )(idx, *got)


def solve_rows(left, tile_row, it_ref, lb_ref):
    solved, rounded = [], []
    for k in range(PANELS):
        rest = left[:, k * TILE : (k + 1) * TILE]
        for j in range(k):
            rest = rest - dot_bf(rounded[j], lb_ref[k, j])
        full = jnp.where(tile_row > k, dot_nn(rest, it_ref[k]), F32(0))
        solved.append(full)
        rounded.append(full.astype(BF16))
    return solved, rounded


def update_kernel(idx, a_ref, p_ref, l_ref, it_ref, lb_ref, *rest):
    col_parts = rest[:N_ROW]
    out, c_all, s_now = rest[N_ROW:]
    r, y, z, c = idx[0], idx[1], idx[2], idx[3]
    t = pl.program_id(0)
    n_col = N_Y * N_Z
    rows = HALVES * SUB

    @pl.when(t == 0)
    def _():
        half = lax.broadcasted_iota(jnp.int32, (rows, TILE), 0) // SUB
        for s in range(N_ROW):
            base = pl.multiple_of((r + N_ROW - s) % N_ROW * SUB, SUB)
            left = col_parts[s][...].reshape(rows, PANELS * TILE)
            _, rounded = solve_rows(left, c + half * n_col, it_ref, lb_ref)
            for k in range(PANELS):
                for h in range(HALVES):
                    c_all[h, pl.ds(base, SUB), k * TILE : (k + 1) * TILE] = rounded[k][h * SUB : (h + 1) * SUB]

    i = t * N_ROW + r
    solved, rounded = solve_rows(p_ref[...].reshape(TILE, PANELS * TILE), i, it_ref, lb_ref)
    for k in range(PANELS):
        s_now[:, k * TILE : (k + 1) * TILE] = rounded[k]
    for u in range(HALVES):
        lanes = slice(u * TILE, (u + 1) * TILE)
        j = c + u * n_col

        @pl.when(i >= j)
        def _():
            out[:, lanes] = a_ref[:, lanes] - dot_bf(s_now[...], c_all[u])

        @pl.when(i < j)
        def _():
            out[:, lanes] = a_ref[:, lanes]

    for k in range(PANELS):

        @pl.when(jnp.logical_and(c == k, i > k))
        def _():
            out[:, :TILE] = solved[k]

        @pl.when(jnp.logical_and(c == k, i == k))
        def _():
            out[:, :TILE] = l_ref[k]


def update(idx, matrix, panel, l_all, inv_t, low, col_parts):
    rows, cols = matrix.shape
    width = PANELS * TILE
    block = pl.BlockSpec((TILE, cols), lambda t: (t, 0))
    return pl.pallas_call(
        update_kernel,
        grid=(rows // TILE,),
        out_shape=jax.ShapeDtypeStruct(matrix.shape, F32),
        in_specs=[
            SMEM,
            block,
            pl.BlockSpec((None, N_Z, None, SUB, width), lambda t: (t % N_Y, 0, t // N_Y, 0, 0)),
        ]
        + [VMEM] * (3 + N_ROW),
        out_specs=block,
        scratch_shapes=[pltpu.VMEM((HALVES, TILE, width), BF16), pltpu.VMEM((TILE, width), BF16)],
        name="update",
    )(idx, matrix, panel, l_all, inv_t, low, *col_parts)


def on_device(matrix):
    row_index = lax.axis_index("row")
    col_index = lax.axis_index("col")
    y_index, z_index = col_index // N_Z, col_index % N_Z
    idx = jnp.stack([row_index, y_index, z_index, col_index]).astype(jnp.int32)

    sent = pack_y(matrix)
    got = [y_shift(sent[s], s) for s in range(1, N_Y)]
    sent = pack_z(idx, sent[0], got)
    mine = pick_panel(idx, [sent[0]] + [z_shift(sent[s], s) for s in range(1, N_Z)])
    panel = lax.all_gather(mine, "col").reshape(N_Y, N_Z, HALVES, SUB, PANELS * TILE)
    swapped = row_z_swap(mine)
    col_parts = [swapped] + [row_shift(swapped, s) for s in range(1, N_ROW)]

    sent = pack_top(idx, matrix)
    got = [sent[0]] + [row_shift(sent[s], s) for s in range(1, N_ROW)]
    slices = pick(idx, 0, PANELS, got)
    slices, _ = lax.optimization_barrier((slices, mine))
    over_y = [slices] + [y_shift(slices, s) for s in range(1, N_Y)]
    slices = lax.select_n(y_index, *over_y)
    lower = pick_lower(idx, [slices] + [z_shift(slices, s) for s in range(1, N_Z)])
    top_parts = [lower] + [row_shift(lower, s) for s in range(1, N_ROW)]
    l_all, inv_t, low = factor(idx, top_parts)

    return update(idx, matrix, panel, l_all, inv_t, low, col_parts)


def solution(mesh):
    return jax.shard_map(
        on_device, mesh=mesh, in_specs=(P("row", "col"),), out_specs=P("row", "col"), check_vma=False
    )
```

```python
import jax
import jax.numpy as jnp
from jax import lax
from jax.experimental import pallas as pl
from jax.experimental.pallas import tpu as pltpu
from jax.sharding import PartitionSpec as P

TILE = 256
PANELS = 3
NB = 64
PIV = 8
N_ROW = 8
N_Y = 4
N_Z = 8
SUB = TILE // 8
HALVES = 2
F32 = jnp.float32
BF16 = jnp.bfloat16
HIGHEST = lax.Precision.HIGHEST
N_X = 4
Z_GROUP = 4
EARLY = (PANELS - 1) * TILE


def dot_nn(a, b):
    return lax.dot_general(a, b, (((1,), (0,)), ((), ())), precision=HIGHEST, preferred_element_type=F32)


def dot_nt(a, b):
    return lax.dot_general(a, b, (((1,), (1,)), ((), ())), precision=HIGHEST, preferred_element_type=F32)


def dot_bf(a, b):
    return lax.dot_general(a, b, (((1,), (1,)), ((), ())), preferred_element_type=F32)


def y_shift(x, s):
    pairs = [(y * N_Z + z, (y + s) % N_Y * N_Z + z) for y in range(N_Y) for z in range(N_Z)]
    return lax.ppermute(x, "col", pairs)


def z_shift(x, s):
    pairs = [(y * N_Z + z, y * N_Z + (z + s) % N_Z) for y in range(N_Y) for z in range(N_Z)]
    return lax.ppermute(x, "col", pairs)


def row_shift(x, s):
    return lax.ppermute(x, "row", [(r, (r + s) % N_ROW) for r in range(N_ROW)])


def z_group_shift(x, s):
    pairs = [
        (y * N_Z + z, y * N_Z + z // Z_GROUP * Z_GROUP + (z % Z_GROUP + s) % Z_GROUP)
        for y in range(N_Y)
        for z in range(N_Z)
    ]
    return lax.ppermute(x, "col", pairs)


def x_shift(x, s):
    return lax.ppermute(x, "row", [(r, (r + 2 * s) % N_ROW) for r in range(N_ROW)])


def core_swap(x):
    return lax.ppermute(x, "row", [(r, r ^ 1) for r in range(N_ROW)])


def row_z_swap(x):
    n_col = N_Y * N_Z
    pairs = [
        (r * n_col + y * N_Z + z, z * n_col + y * N_Z + r)
        for r in range(N_ROW)
        for y in range(N_Y)
        for z in range(N_Z)
    ]
    return lax.ppermute(x, ("row", "col"), pairs)


SMEM = pl.BlockSpec(memory_space=pltpu.SMEM)
ANY = pl.BlockSpec(memory_space=pl.ANY)
VMEM = pl.BlockSpec(memory_space=pltpu.VMEM)


def pack_top_kernel(idx, tile, *outs):
    r = idx[0]
    for s in range(N_ROW):
        base = pl.multiple_of((r + s) % N_ROW * SUB, SUB)
        outs[s][...] = tile[pl.ds(base, SUB), :]


def pack_top(idx, matrix):
    return pl.pallas_call(
        pack_top_kernel,
        grid=(1,),
        out_shape=[jax.ShapeDtypeStruct((SUB, TILE), F32)] * N_ROW,
        in_specs=[SMEM, pl.BlockSpec((TILE, TILE), lambda i: (0, 0))],
        out_specs=[pl.BlockSpec((SUB, TILE), lambda i: (0, 0))] * N_ROW,
        name="pack_top",
    )(idx, matrix)


def pack_y_kernel(*refs):
    for s in range(N_Y):
        refs[N_Y + s][...] = refs[s][...]


def pack_y(matrix):
    return pl.pallas_call(
        pack_y_kernel,
        grid=(HALVES,),
        out_shape=[jax.ShapeDtypeStruct((HALVES, TILE, TILE), F32)] * N_Y,
        in_specs=[pl.BlockSpec((TILE, TILE), lambda h, s=s: (h * N_Y + s, 0)) for s in range(N_Y)],
        out_specs=[pl.BlockSpec((None, TILE, TILE), lambda h: (h, 0, 0))] * N_Y,
        name="pack_y",
    )(*[matrix] * N_Y)


def pack_z_kernel(idx, own, *rest):
    got, outs = rest[: N_Y - 1], rest[N_Y - 1 :]
    y, z = idx[1], idx[2]
    for source, ref in enumerate((own,) + tuple(got)):

        @pl.when(y == source)
        def _():
            for s in range(N_Z):
                base = pl.multiple_of((z + s) % N_Z * SUB, SUB)
                outs[s][0] = ref[:, pl.ds(base, SUB), :]
                other = pl.multiple_of((z + s + N_Z // 2) % N_Z * SUB, SUB)
                outs[s][1] = ref[:, pl.ds(other, SUB), :]


def pack_z(idx, own, got):
    return pl.pallas_call(
        pack_z_kernel,
        out_shape=[jax.ShapeDtypeStruct((2, HALVES, SUB, TILE), F32)] * N_Z,
        in_specs=[SMEM] + [VMEM] * N_Y,
        out_specs=[VMEM] * N_Z,
        name="pack_z",
    )(idx, own, *got)


def pick_row_kernel(idx, *rest):
    got, out = rest[:-1], rest[-1]
    first = idx[3] % PANELS
    for s, ref in enumerate(got):
        source = (idx[0] + N_ROW - s) % N_ROW
        for n in range(2):

            @pl.when(source == (first + n) % PANELS)
            def _():
                out[n] = ref[...]


def pick_row(idx, got):
    return pl.pallas_call(
        pick_row_kernel,
        out_shape=jax.ShapeDtypeStruct((2, SUB, TILE), F32),
        in_specs=[SMEM] + [VMEM] * N_ROW,
        out_specs=VMEM,
        name="pick_row",
    )(idx, *got)


def pick_top_kernel(idx, *rest):
    got, out = rest[:-1], rest[-1]
    for s, ref in enumerate(got):
        source = (idx[2] + N_Z - s) % N_Z

        @pl.when(source < PANELS)
        def _():
            out[source] = ref[...]


def pick_top(idx, got):
    return pl.pallas_call(
        pick_top_kernel,
        out_shape=jax.ShapeDtypeStruct((PANELS, 2, SUB, TILE), F32),
        in_specs=[SMEM] + [VMEM] * N_Z,
        out_specs=VMEM,
        name="pick_top",
    )(idx, *got)


def eliminate(block):
    sub = lax.broadcasted_iota(jnp.int32, (8, 2 * NB), 0)
    lane = lax.broadcasted_iota(jnp.int32, (8, 2 * NB), 1)
    groups = NB // 8

    def spread(x):
        return jnp.broadcast_to(x, (8, 2 * NB))

    m = []
    for g in range(groups):
        eye = jnp.where(lane == sub + (8 * g + NB), F32(1), F32(0))
        m.append(jnp.concatenate([block[8 * g : 8 * g + 8], eye[:, NB:]], axis=1))
    scale = []
    for g0 in range(groups):
        j = g0 * PIV
        cols = [[spread(m[g][:, j + q : j + q + 1]) for g in range(g0, groups)] for q in range(PIV)]
        rows = [spread(m[g0][q : q + 1, :]) for q in range(PIV)]
        a = {}
        for q in range(PIV):
            for i in range(q, PIV):
                a[i, q] = spread(cols[q][0][i : i + 1, :])
        low = {}
        inv = []
        pivots = None
        for q in range(PIV):
            inv.append(1.0 / a[q, q])
            pivots = a[q, q] if pivots is None else jnp.where(sub >= q, a[q, q], pivots)
            for i in range(q + 1, PIV):
                low[i, q] = a[i, q] * inv[q]
            for jj in range(q + 1, PIV):
                for i in range(jj, PIV):
                    a[i, jj] = a[i, jj] - low[i, q] * a[jj, q]
        scale.append(lax.rsqrt(pivots))
        scaled = []
        for q in range(PIV):
            for i in range(q + 1, PIV):
                rows[i] = rows[i] - low[i, q] * rows[q]
            scaled.append(rows[q] * inv[q])
        for g in range(g0, groups):
            x = [cols[q][g - g0] for q in range(PIV)]
            updated = m[g]
            for q in range(PIV):
                for i in range(q + 1, PIV):
                    x[i] = x[i] - low[i, q] * x[q]
                part = x[q]
                if g == g0:
                    part = jnp.where(sub > q, part, F32(0))
                updated = updated - part * scaled[q]
            m[g] = updated
    return jnp.concatenate([m[g] * scale[g] for g in range(groups)], axis=0)


def chol_inv(w, lc):
    blocks = TILE // NB
    rows = lax.broadcasted_iota(jnp.int32, (2 * TILE, NB), 0)
    r64 = lax.broadcasted_iota(jnp.int32, (NB, NB), 0)
    c64 = lax.broadcasted_iota(jnp.int32, (NB, NB), 1)

    def step(b, carry):
        base = pl.multiple_of(b * NB, NB)
        m = eliminate(w[b, pl.ds(base, NB), :]).T
        lower = jnp.where(r64 >= c64, m[:NB], F32(0))
        inv_t = jnp.where(r64 <= c64, m[NB:], F32(0))
        p = jnp.where(rows >= base + NB, dot_nn(w[b], inv_t), F32(0))
        lc[b] = p
        lc[b, pl.ds(base, NB), :] = lower
        for bj in range(1, blocks):

            @pl.when(bj > b)
            def _():
                w[bj] = w[bj] - dot_nt(p, p[bj * NB : (bj + 1) * NB])

        return carry

    lax.fori_loop(0, blocks, step, 0)


def factor_tile(tile, l_ref, it_ref, w, lc):
    blocks = TILE // NB
    r = lax.broadcasted_iota(jnp.int32, (TILE, NB), 0)
    c = lax.broadcasted_iota(jnp.int32, (TILE, NB), 1)
    for b in range(blocks):
        w[b, :TILE, :] = tile[:, b * NB : (b + 1) * NB]
        w[b, TILE:, :] = jnp.where(r == c + b * NB, F32(1), F32(0))
    chol_inv(w, lc)
    l_ref[...] = jnp.concatenate([lc[b, :TILE, :] for b in range(blocks)], axis=1)
    inv_t = jnp.concatenate([lc[b, TILE:, :] for b in range(blocks)], axis=1)
    it_ref[...] = inv_t
    return inv_t


def factor0_kernel(idx, *rest):
    got = rest[:N_ROW]
    l_ref, it_ref, lb_ref, t11, t21, t22, top, w, lc = rest[N_ROW:]
    x, core = idx[0] // 2, idx[0] % 2
    for s in range(N_X):
        for other in range(2):
            source = (x + N_X - s) % N_X * 2 + (core + other) % 2
            base = pl.multiple_of(source * SUB, SUB)
            top[:, :, pl.ds(base, SUB), :] = got[2 * s + other][...]
    inv_t = factor_tile(top[0, 0], l_ref, it_ref, w, lc)
    low1 = dot_nn(top[0, 1], inv_t).astype(BF16)
    low2 = dot_nn(top[2, 1].T, inv_t).astype(BF16)
    lb_ref[0] = low1
    lb_ref[1] = low2
    t11[...] = top[1, 0] - dot_bf(low1, low1)
    t21[...] = top[1, 1] - dot_bf(low2, low1)
    t22[...] = top[2, 0] - dot_bf(low2, low2)


def factor1_kernel(t11, t21, t22, l_ref, it_ref, lb_ref, rest_ref, w, lc):
    inv_t = factor_tile(t11[...], l_ref, it_ref, w, lc)
    low = dot_nn(t21[...], inv_t).astype(BF16)
    lb_ref[...] = low
    rest_ref[...] = t22[...] - dot_bf(low, low)


def factor2_kernel(t22, l_ref, it_ref, w, lc):
    factor_tile(t22[...], l_ref, it_ref, w, lc)


SQUARE = jax.ShapeDtypeStruct((TILE, TILE), F32)
FACTOR_COST = pl.CostEstimate(flops=15_000_000_000, transcendentals=0, bytes_accessed=2_000_000)
WORK = [pltpu.VMEM((TILE // NB, 2 * TILE, NB), F32)] * 2


def factor0(idx, got):
    return pl.pallas_call(
        factor0_kernel,
        out_shape=[SQUARE, SQUARE, jax.ShapeDtypeStruct((2, TILE, TILE), BF16), SQUARE, SQUARE, SQUARE],
        in_specs=[SMEM] + [VMEM] * N_ROW,
        out_specs=[VMEM] * 6,
        scratch_shapes=[pltpu.VMEM((PANELS, 2, TILE, TILE), F32)] + WORK,
        cost_estimate=FACTOR_COST,
        name="factor0",
    )(idx, *got)


def factor1(t11, t21, t22):
    return pl.pallas_call(
        factor1_kernel,
        out_shape=[SQUARE, SQUARE, jax.ShapeDtypeStruct((TILE, TILE), BF16), SQUARE],
        in_specs=[VMEM] * 3,
        out_specs=[VMEM] * 4,
        scratch_shapes=WORK,
        cost_estimate=FACTOR_COST,
        name="factor1",
    )(t11, t21, t22)


def factor2(t22):
    return pl.pallas_call(
        factor2_kernel,
        out_shape=[SQUARE, SQUARE],
        in_specs=[VMEM],
        out_specs=[VMEM] * 2,
        scratch_shapes=WORK,
        cost_estimate=FACTOR_COST,
        name="factor2",
    )(t22)


def pick_panel_kernel(idx, *rest):
    got, own, pair = rest[:-2], rest[-2], rest[-1]
    for s in range(N_Z):
        source = (idx[2] + N_Z - s) % N_Z
        for k in range(PANELS):

            @pl.when(source == k)
            def _():
                own[:, :, k * TILE : (k + 1) * TILE] = got[s][0]
                pair[:, :, :, k * TILE : (k + 1) * TILE] = got[s][...]


def pick_panel(idx, got):
    width = PANELS * TILE
    return pl.pallas_call(
        pick_panel_kernel,
        out_shape=[
            jax.ShapeDtypeStruct((HALVES, SUB, width), F32),
            jax.ShapeDtypeStruct((2, HALVES, SUB, width), F32),
        ],
        in_specs=[SMEM] + [VMEM] * N_Z,
        out_specs=[VMEM] * 2,
        name="pick_panel",
    )(idx, *got)


def keep_rows(tile_row, k, solved):
    return jnp.where(tile_row > k, solved, F32(0)).astype(BF16)


def row_tiles(idx):
    half = lax.broadcasted_iota(jnp.int32, (HALVES * TILE, TILE), 0) // TILE
    return (half * N_Y + idx[1]) * N_ROW + idx[0]


def col_tiles(idx):
    half = lax.broadcasted_iota(jnp.int32, (HALVES * N_X * SUB, TILE), 0) // (N_X * SUB)
    return half * (N_Y * N_Z) + idx[3]


def solve_early_kernel(idx, it0, it1, lb0, lb1, *rest):
    row_parts, col_parts = rest[:Z_GROUP], rest[Z_GROUP : Z_GROUP + N_X]
    row_out, row_left, col_out, col_left, rows, cols = rest[Z_GROUP + N_X :]
    z, x = idx[2], idx[0] // 2
    for s in range(Z_GROUP):
        source = z // Z_GROUP * Z_GROUP + (z % Z_GROUP + Z_GROUP - s) % Z_GROUP
        for p in range(2):
            base = pl.multiple_of((source + p * (N_Z // 2)) % N_Z * SUB, SUB)
            rows[:, pl.ds(base, SUB), :] = row_parts[s][p]
    for s in range(N_X):
        base = pl.multiple_of((x + N_X - s) % N_X * SUB, SUB)
        cols[:, pl.ds(base, SUB), :] = col_parts[s][...]
    for src, tile_row, out, left_out in (
        (rows, row_tiles(idx), row_out, row_left),
        (cols, col_tiles(idx), col_out, col_left),
    ):
        count = src.shape[0] * src.shape[1]

        def panel(k, src=src, count=count):
            return src[:, :, k * TILE : (k + 1) * TILE].reshape(count, TILE)

        s0 = keep_rows(tile_row, 0, dot_nn(panel(0), it0[...]))
        s1 = keep_rows(tile_row, 1, dot_nn(panel(1) - dot_bf(s0, lb0[0]), it1[...]))
        out[:, :, :TILE] = s0.reshape(src.shape[0], src.shape[1], TILE)
        out[:, :, TILE:EARLY] = s1.reshape(src.shape[0], src.shape[1], TILE)
        left_out[...] = panel(2) - dot_bf(s0, lb0[1]) - dot_bf(s1, lb1[...])


def solve_early(idx, it0, it1, lb0, lb1, row_parts, col_parts):
    width = PANELS * TILE
    n_rows, n_cols = HALVES * TILE, HALVES * N_X * SUB
    return pl.pallas_call(
        solve_early_kernel,
        out_shape=[
            jax.ShapeDtypeStruct((HALVES, TILE, EARLY), BF16),
            jax.ShapeDtypeStruct((n_rows, TILE), F32),
            jax.ShapeDtypeStruct((HALVES, N_X * SUB, EARLY), BF16),
            jax.ShapeDtypeStruct((n_cols, TILE), F32),
        ],
        in_specs=[SMEM] + [VMEM] * (4 + Z_GROUP + N_X),
        out_specs=[VMEM] * 4,
        scratch_shapes=[pltpu.VMEM((HALVES, TILE, width), F32), pltpu.VMEM((HALVES, N_X * SUB, width), F32)],
        name="solve_early",
    )(idx, it0, it1, lb0, lb1, *row_parts, *col_parts)


def solve_last_kernel(idx, it2, row_left, col_left, row_out, col_out):
    k = PANELS - 1
    rows = keep_rows(row_tiles(idx), k, dot_nn(row_left[...], it2[...]))
    cols = keep_rows(col_tiles(idx), k, dot_nn(col_left[...], it2[...]))
    row_out[...] = rows.reshape(row_out.shape)
    col_out[...] = cols.reshape(col_out.shape)


def solve_last(idx, it2, row_left, col_left):
    return pl.pallas_call(
        solve_last_kernel,
        out_shape=[
            jax.ShapeDtypeStruct((HALVES, TILE, TILE), BF16),
            jax.ShapeDtypeStruct((HALVES, N_X * SUB, TILE), BF16),
        ],
        in_specs=[SMEM] + [VMEM] * 3,
        out_specs=[VMEM] * 2,
        name="solve_last",
    )(idx, it2, row_left, col_left)


def update_kernel(idx, a_ref, *rest):
    early_rows, last_rows = rest[:N_Y], rest[N_Y : 2 * N_Y]
    rest = rest[2 * N_Y :]
    early_cols, last_cols = rest[:2], rest[2:4]
    factors, inverses = rest[4 : 4 + PANELS], rest[4 + PANELS : 4 + 2 * PANELS]
    out, s_all, c_all, l_own, it_own, row_sem, own_sem = rest[4 + 2 * PANELS :]
    r, y, c = idx[0], idx[1], idx[3]
    core = r % 2
    t = pl.program_id(0)
    n_col = N_Y * N_Z

    def row_copies(s, h):
        slot = h * N_Y + (y + N_Y - s) % N_Y
        return (
            pltpu.make_async_copy(early_rows[s].at[h], s_all.at[slot, :, pl.ds(0, EARLY)], row_sem.at[slot, 0]),
            pltpu.make_async_copy(last_rows[s].at[h], s_all.at[slot, :, pl.ds(EARLY, TILE)], row_sem.at[slot, 1]),
        )

    def own_copies(k):
        return (
            pltpu.make_async_copy(factors[k], l_own, own_sem.at[0]),
            pltpu.make_async_copy(inverses[k], it_own, own_sem.at[1]),
        )

    @pl.when(t == 0)
    def _():
        for h in range(HALVES):
            for s in range(N_Y):
                for copy in row_copies(s, h):
                    copy.start()
        for k in range(PANELS):

            @pl.when(c == k)
            def _():
                for copy in own_copies(k):
                    copy.start()
                for copy in own_copies(k):
                    copy.wait()

        for other in range(2):
            for slot in range(N_X):
                base = pl.multiple_of((2 * slot + (core + other) % 2) * SUB, SUB)
                piece = slice(slot * SUB, (slot + 1) * SUB)
                c_all[:, pl.ds(base, SUB), :EARLY] = early_cols[other][:, piece, :]
                c_all[:, pl.ds(base, SUB), EARLY:] = last_cols[other][:, piece, :]

    pltpu.make_async_copy(early_rows[0].at[0], s_all.at[t, :, pl.ds(0, EARLY)], row_sem.at[t, 0]).wait()
    pltpu.make_async_copy(last_rows[0].at[0], s_all.at[t, :, pl.ds(EARLY, TILE)], row_sem.at[t, 1]).wait()
    i = t * N_ROW + r
    for u in range(HALVES):
        lanes = slice(u * TILE, (u + 1) * TILE)
        j = c + u * n_col

        @pl.when(i >= j)
        def _():
            out[:, lanes] = a_ref[:, lanes] - dot_bf(s_all[t], c_all[u])

        @pl.when(i < j)
        def _():
            out[:, lanes] = a_ref[:, lanes]

    @pl.when(jnp.logical_and(c < PANELS, i > c))
    def _():
        out[:, :TILE] = dot_nn(out[:, :TILE], it_own[...])

    @pl.when(jnp.logical_and(c < PANELS, i == c))
    def _():
        out[:, :TILE] = l_own[...]


def update(idx, matrix, early_rows, last_rows, early_cols, last_cols, factors, inverses):
    rows, cols = matrix.shape
    width = PANELS * TILE
    block = pl.BlockSpec((TILE, cols), lambda t: (t, 0))
    return pl.pallas_call(
        update_kernel,
        grid=(rows // TILE,),
        out_shape=jax.ShapeDtypeStruct(matrix.shape, F32),
        in_specs=[SMEM, block] + [ANY] * (2 * N_Y) + [VMEM] * 4 + [ANY] * (2 * PANELS),
        out_specs=block,
        scratch_shapes=[
            pltpu.VMEM((rows // TILE, TILE, width), BF16),
            pltpu.VMEM((HALVES, TILE, width), BF16),
            pltpu.VMEM((TILE, TILE), F32),
            pltpu.VMEM((TILE, TILE), F32),
            pltpu.SemaphoreType.DMA((rows // TILE, 2)),
            pltpu.SemaphoreType.DMA((2,)),
        ],
        name="update",
    )(idx, matrix, *early_rows, *last_rows, *early_cols, *last_cols, *factors, *inverses)


def on_device(matrix):
    row_index = lax.axis_index("row")
    col_index = lax.axis_index("col")
    y_index, z_index = col_index // N_Z, col_index % N_Z
    idx = jnp.stack([row_index, y_index, z_index, col_index]).astype(jnp.int32)
    barrier = lax.optimization_barrier

    sent = pack_top(idx, matrix)
    tiles = pack_y(matrix)
    slices = pick_row(idx, [sent[0]] + [row_shift(sent[s], s) for s in range(1, N_ROW)])
    slices = lax.select_n(y_index, slices, *[y_shift(slices, s) for s in range(1, N_Y)])
    slices, tiles = barrier((slices, tiles))
    shifted = [y_shift(tiles[s], s) for s in range(1, N_Y)]
    top = pick_top(idx, [slices] + [z_shift(slices, s) for s in range(1, N_Z)])
    top_parts = []
    for s in range(N_X):
        part = x_shift(top, s) if s else top
        top_parts += [part, core_swap(part)]

    sent = pack_z(idx, tiles[0], shifted)
    own, pair = pick_panel(idx, [sent[0]] + [z_shift(sent[s], s) for s in range(1, N_Z)])
    swapped = row_z_swap(own)
    row_parts = [pair] + [z_group_shift(pair, s) for s in range(1, Z_GROUP)]
    top_parts, pair, swapped = barrier((top_parts, pair, swapped))
    col_parts = [swapped] + [x_shift(swapped, s) for s in range(1, N_X)]

    l0, it0, lb0, t11, t21, t22 = factor0(idx, top_parts)
    l1, it1, lb1, t22 = factor1(t11, t21, t22)
    row_early, row_left, col_early, col_left = solve_early(idx, it0, it1, lb0, lb1, row_parts, col_parts)
    t22, row_early = barrier((t22, row_early))
    early_rows = [row_early] + [y_shift(row_early, s) for s in range(1, N_Y)]
    early_cols = [col_early, core_swap(col_early)]
    l2, it2 = factor2(t22)
    row_left, early_rows, early_cols = barrier((row_left, early_rows, early_cols))
    row_last, col_last = solve_last(idx, it2, row_left, col_left)
    last_rows = [row_last] + [y_shift(row_last, s) for s in range(1, N_Y)]
    last_cols = [col_last, core_swap(col_last)]
    return update(idx, matrix, early_rows, last_rows, early_cols, last_cols, [l0, l1, l2], [it0, it1, it2])


def solution(mesh):
    return jax.shard_map(
        on_device, mesh=mesh, in_specs=(P("row", "col"),), out_specs=P("row", "col"), check_vma=False
    )
```

```python
import jax
import jax.numpy as jnp
from jax import lax
from jax.experimental import pallas as pl
from jax.experimental.pallas import tpu as pltpu
from jax.sharding import PartitionSpec as P

TILE = 256
PANELS = 3
NB = 64
PIV = 8
N_ROW = 8
N_Y = 4
N_Z = 8
SUB = TILE // 8
HALVES = 2
F32 = jnp.float32
BF16 = jnp.bfloat16
HIGHEST = lax.Precision.HIGHEST
N_X = 4


def dot_nn(a, b):
    return lax.dot_general(a, b, (((1,), (0,)), ((), ())), precision=HIGHEST, preferred_element_type=F32)


def dot_nt(a, b):
    return lax.dot_general(a, b, (((1,), (1,)), ((), ())), precision=HIGHEST, preferred_element_type=F32)


def dot_bf(a, b):
    return lax.dot_general(a, b, (((1,), (1,)), ((), ())), preferred_element_type=F32)


def y_shift(x, s):
    pairs = [(y * N_Z + z, (y + s) % N_Y * N_Z + z) for y in range(N_Y) for z in range(N_Z)]
    return lax.ppermute(x, "col", pairs)


def z_shift(x, s):
    pairs = [(y * N_Z + z, y * N_Z + (z + s) % N_Z) for y in range(N_Y) for z in range(N_Z)]
    return lax.ppermute(x, "col", pairs)


def row_shift(x, s):
    return lax.ppermute(x, "row", [(r, (r + s) % N_ROW) for r in range(N_ROW)])


def x_shift(x, s):
    return lax.ppermute(x, "row", [(r, (r + 2 * s) % N_ROW) for r in range(N_ROW)])


def core_swap(x):
    return lax.ppermute(x, "row", [(r, r ^ 1) for r in range(N_ROW)])


def row_z_swap(x):
    n_col = N_Y * N_Z
    pairs = [
        (r * n_col + y * N_Z + z, z * n_col + y * N_Z + r)
        for r in range(N_ROW)
        for y in range(N_Y)
        for z in range(N_Z)
    ]
    return lax.ppermute(x, ("row", "col"), pairs)


SMEM = pl.BlockSpec(memory_space=pltpu.SMEM)
ANY = pl.BlockSpec(memory_space=pl.ANY)
VMEM = pl.BlockSpec(memory_space=pltpu.VMEM)


def pack_top_kernel(idx, tile, *outs):
    r = idx[0]
    for s in range(N_ROW):
        base = pl.multiple_of((r + s) % N_ROW * SUB, SUB)
        outs[s][...] = tile[pl.ds(base, SUB), :]


def pack_top(idx, matrix):
    return pl.pallas_call(
        pack_top_kernel,
        grid=(1,),
        out_shape=[jax.ShapeDtypeStruct((SUB, TILE), F32)] * N_ROW,
        in_specs=[SMEM, pl.BlockSpec((TILE, TILE), lambda i: (0, 0))],
        out_specs=[pl.BlockSpec((SUB, TILE), lambda i: (0, 0))] * N_ROW,
        name="pack_top",
    )(idx, matrix)


def pack_y_kernel(*refs):
    for s in range(N_Y):
        refs[N_Y + s][...] = refs[s][...]


def pack_y(matrix):
    return pl.pallas_call(
        pack_y_kernel,
        grid=(HALVES,),
        out_shape=[jax.ShapeDtypeStruct((HALVES, TILE, TILE), F32)] * N_Y,
        in_specs=[pl.BlockSpec((TILE, TILE), lambda h, s=s: (h * N_Y + s, 0)) for s in range(N_Y)],
        out_specs=[pl.BlockSpec((None, TILE, TILE), lambda h: (h, 0, 0))] * N_Y,
        name="pack_y",
    )(*[matrix] * N_Y)


def pack_z_kernel(idx, own, *rest):
    got, outs = rest[: N_Y - 1], rest[N_Y - 1 :]
    y, z = idx[1], idx[2]
    for source, ref in enumerate((own,) + tuple(got)):

        @pl.when(y == source)
        def _():
            for s in range(N_Z):
                base = pl.multiple_of((z + s) % N_Z * SUB, SUB)
                outs[s][...] = ref[:, pl.ds(base, SUB), :]


def pack_z(idx, own, got):
    return pl.pallas_call(
        pack_z_kernel,
        out_shape=[jax.ShapeDtypeStruct((HALVES, SUB, TILE), F32)] * N_Z,
        in_specs=[SMEM] + [VMEM] * N_Y,
        out_specs=[VMEM] * N_Z,
        name="pack_z",
    )(idx, own, *got)


def pick_row_kernel(idx, *rest):
    got, out = rest[:-1], rest[-1]
    first = idx[3] % PANELS
    for s, ref in enumerate(got):
        source = (idx[0] + N_ROW - s) % N_ROW
        for n in range(2):

            @pl.when(source == (first + n) % PANELS)
            def _():
                out[n] = ref[...]


def pick_row(idx, got):
    return pl.pallas_call(
        pick_row_kernel,
        out_shape=jax.ShapeDtypeStruct((2, SUB, TILE), F32),
        in_specs=[SMEM] + [VMEM] * N_ROW,
        out_specs=VMEM,
        name="pick_row",
    )(idx, *got)


def pick_top_kernel(idx, *rest):
    got, out = rest[:-1], rest[-1]
    for s, ref in enumerate(got):
        source = (idx[2] + N_Z - s) % N_Z

        @pl.when(source < PANELS)
        def _():
            out[source] = ref[...]


def pick_top(idx, got):
    return pl.pallas_call(
        pick_top_kernel,
        out_shape=jax.ShapeDtypeStruct((PANELS, 2, SUB, TILE), F32),
        in_specs=[SMEM] + [VMEM] * N_Z,
        out_specs=VMEM,
        name="pick_top",
    )(idx, *got)


def eliminate(block):
    sub = lax.broadcasted_iota(jnp.int32, (8, 2 * NB), 0)
    lane = lax.broadcasted_iota(jnp.int32, (8, 2 * NB), 1)
    groups = NB // 8

    def spread(x):
        return jnp.broadcast_to(x, (8, 2 * NB))

    m = []
    for g in range(groups):
        eye = jnp.where(lane == sub + (8 * g + NB), F32(1), F32(0))
        m.append(jnp.concatenate([block[8 * g : 8 * g + 8], eye[:, NB:]], axis=1))
    scale = []
    for g0 in range(groups):
        j = g0 * PIV
        cols = [[spread(m[g][:, j + q : j + q + 1]) for g in range(g0, groups)] for q in range(PIV)]
        rows = [spread(m[g0][q : q + 1, :]) for q in range(PIV)]
        a = {}
        for q in range(PIV):
            for i in range(q, PIV):
                a[i, q] = spread(cols[q][0][i : i + 1, :])
        low = {}
        inv = []
        pivots = None
        for q in range(PIV):
            inv.append(1.0 / a[q, q])
            pivots = a[q, q] if pivots is None else jnp.where(sub >= q, a[q, q], pivots)
            for i in range(q + 1, PIV):
                low[i, q] = a[i, q] * inv[q]
            for jj in range(q + 1, PIV):
                for i in range(jj, PIV):
                    a[i, jj] = a[i, jj] - low[i, q] * a[jj, q]
        scale.append(lax.rsqrt(pivots))
        scaled = []
        for q in range(PIV):
            for i in range(q + 1, PIV):
                rows[i] = rows[i] - low[i, q] * rows[q]
            scaled.append(rows[q] * inv[q])
        for g in range(g0, groups):
            x = [cols[q][g - g0] for q in range(PIV)]
            updated = m[g]
            for q in range(PIV):
                for i in range(q + 1, PIV):
                    x[i] = x[i] - low[i, q] * x[q]
                part = x[q]
                if g == g0:
                    part = jnp.where(sub > q, part, F32(0))
                updated = updated - part * scaled[q]
            m[g] = updated
    return jnp.concatenate([m[g] * scale[g] for g in range(groups)], axis=0)


def chol_inv(w, lc):
    blocks = TILE // NB
    rows = lax.broadcasted_iota(jnp.int32, (2 * TILE, NB), 0)
    r64 = lax.broadcasted_iota(jnp.int32, (NB, NB), 0)
    c64 = lax.broadcasted_iota(jnp.int32, (NB, NB), 1)

    def step(b, carry):
        base = pl.multiple_of(b * NB, NB)
        m = eliminate(w[b, pl.ds(base, NB), :]).T
        lower = jnp.where(r64 >= c64, m[:NB], F32(0))
        inv_t = jnp.where(r64 <= c64, m[NB:], F32(0))
        p = jnp.where(rows >= base + NB, dot_nn(w[b], inv_t), F32(0))
        lc[b] = p
        lc[b, pl.ds(base, NB), :] = lower
        for bj in range(1, blocks):

            @pl.when(bj > b)
            def _():
                w[bj] = w[bj] - dot_nt(p, p[bj * NB : (bj + 1) * NB])

        return carry

    lax.fori_loop(0, blocks, step, 0)


def factor_tile(tile, l_ref, it_ref, w, lc):
    blocks = TILE // NB
    r = lax.broadcasted_iota(jnp.int32, (TILE, NB), 0)
    c = lax.broadcasted_iota(jnp.int32, (TILE, NB), 1)
    for b in range(blocks):
        w[b, :TILE, :] = tile[:, b * NB : (b + 1) * NB]
        w[b, TILE:, :] = jnp.where(r == c + b * NB, F32(1), F32(0))
    chol_inv(w, lc)
    l_ref[...] = jnp.concatenate([lc[b, :TILE, :] for b in range(blocks)], axis=1)
    inv_t = jnp.concatenate([lc[b, TILE:, :] for b in range(blocks)], axis=1)
    it_ref[...] = inv_t
    return inv_t


def factor0_kernel(idx, *rest):
    got = rest[:N_ROW]
    l_ref, it_ref, lb_ref, t11, t21, t22, top, w, lc = rest[N_ROW:]
    x, core = idx[0] // 2, idx[0] % 2
    for s in range(N_X):
        for other in range(2):
            source = (x + N_X - s) % N_X * 2 + (core + other) % 2
            base = pl.multiple_of(source * SUB, SUB)
            top[:, :, pl.ds(base, SUB), :] = got[2 * s + other][...]
    inv_t = factor_tile(top[0, 0], l_ref, it_ref, w, lc)
    low1 = dot_nn(top[0, 1], inv_t).astype(BF16)
    low2 = dot_nn(top[2, 1].T, inv_t).astype(BF16)
    lb_ref[0] = low1
    lb_ref[1] = low2
    t11[...] = top[1, 0] - dot_bf(low1, low1)
    t21[...] = top[1, 1] - dot_bf(low2, low1)
    t22[...] = top[2, 0] - dot_bf(low2, low2)


def factor1_kernel(t11, t21, t22, l_ref, it_ref, lb_ref, rest_ref, w, lc):
    inv_t = factor_tile(t11[...], l_ref, it_ref, w, lc)
    low = dot_nn(t21[...], inv_t).astype(BF16)
    lb_ref[...] = low
    rest_ref[...] = t22[...] - dot_bf(low, low)


def factor2_kernel(t22, l_ref, it_ref, w, lc):
    factor_tile(t22[...], l_ref, it_ref, w, lc)


SQUARE = jax.ShapeDtypeStruct((TILE, TILE), F32)
FACTOR_COST = pl.CostEstimate(flops=15_000_000_000, transcendentals=0, bytes_accessed=2_000_000)
WORK = [pltpu.VMEM((TILE // NB, 2 * TILE, NB), F32)] * 2


def factor0(idx, got):
    return pl.pallas_call(
        factor0_kernel,
        out_shape=[SQUARE, SQUARE, jax.ShapeDtypeStruct((2, TILE, TILE), BF16), SQUARE, SQUARE, SQUARE],
        in_specs=[SMEM] + [VMEM] * N_ROW,
        out_specs=[VMEM] * 6,
        scratch_shapes=[pltpu.VMEM((PANELS, 2, TILE, TILE), F32)] + WORK,
        cost_estimate=FACTOR_COST,
        name="factor0",
    )(idx, *got)


def factor1(t11, t21, t22):
    return pl.pallas_call(
        factor1_kernel,
        out_shape=[SQUARE, SQUARE, jax.ShapeDtypeStruct((TILE, TILE), BF16), SQUARE],
        in_specs=[VMEM] * 3,
        out_specs=[VMEM] * 4,
        scratch_shapes=WORK,
        cost_estimate=FACTOR_COST,
        name="factor1",
    )(t11, t21, t22)


def factor2(t22):
    return pl.pallas_call(
        factor2_kernel,
        out_shape=[SQUARE, SQUARE],
        in_specs=[VMEM],
        out_specs=[VMEM] * 2,
        scratch_shapes=WORK,
        cost_estimate=FACTOR_COST,
        name="factor2",
    )(t22)


def solve_kernel(idx, it0, it1, it2, lb0, lb1, *rest):
    got, out, rows = rest[:N_Z], rest[N_Z], rest[N_Z + 1]
    r, y, z = idx[0], idx[1], idx[2]
    for s in range(N_Z):
        source = (z + N_Z - s) % N_Z

        @pl.when(source < PANELS)
        def _():
            rows[source] = got[s][...]

    chunk = HALVES * SUB
    half = lax.broadcasted_iota(jnp.int32, (chunk, TILE), 0) // SUB
    tile_row = (half * N_Y + y) * N_ROW + r

    def keep(k, left, inverse):
        return jnp.where(tile_row > k, dot_nn(left, inverse[...]), F32(0)).astype(BF16)

    s0 = keep(0, rows[0].reshape(chunk, TILE), it0)
    s1 = keep(1, rows[1].reshape(chunk, TILE) - dot_bf(s0, lb0[0]), it1)
    s2 = keep(2, rows[2].reshape(chunk, TILE) - dot_bf(s0, lb0[1]) - dot_bf(s1, lb1[...]), it2)
    for k, done in enumerate((s0, s1, s2)):
        out[:, :, k * TILE : (k + 1) * TILE] = done.reshape(HALVES, SUB, TILE)


def solve(idx, inverses, lb0, lb1, got):
    return pl.pallas_call(
        solve_kernel,
        out_shape=jax.ShapeDtypeStruct((HALVES, SUB, PANELS * TILE), BF16),
        in_specs=[SMEM] + [VMEM] * (PANELS + 2 + N_Z),
        out_specs=VMEM,
        scratch_shapes=[pltpu.VMEM((PANELS, HALVES, SUB, TILE), F32)],
        name="solve",
    )(idx, *inverses, lb0, lb1, *got)


def join_z_kernel(idx, *rest):
    got, outs = rest[:N_Z], rest[N_Z:]
    for s in range(N_Z):
        base = pl.multiple_of((idx[2] + N_Z - s) % N_Z * SUB, SUB)
        for h in range(HALVES):
            outs[h][pl.ds(base, SUB), :] = got[s][h]


def join_z(idx, got):
    return pl.pallas_call(
        join_z_kernel,
        out_shape=[jax.ShapeDtypeStruct((TILE, PANELS * TILE), BF16)] * HALVES,
        in_specs=[SMEM] + [VMEM] * N_Z,
        out_specs=[VMEM] * HALVES,
        name="join_z",
    )(idx, *got)


def join_x_kernel(idx, *rest):
    got, out = rest[:-1], rest[-1]
    for s in range(N_X):
        out[(idx[0] // 2 + N_X - s) % N_X] = got[s][...]


def join_x(idx, got):
    return pl.pallas_call(
        join_x_kernel,
        out_shape=jax.ShapeDtypeStruct((N_X,) + got[0].shape, got[0].dtype),
        in_specs=[SMEM] + [VMEM] * N_X,
        out_specs=VMEM,
        name="join_x",
    )(idx, *got)


def update_kernel(idx, a_ref, *rest):
    row_parts = [rest[HALVES * s : HALVES * (s + 1)] for s in range(N_Y)]
    rest = rest[HALVES * N_Y :]
    col_parts, factors, inverses = rest[:2], rest[2 : 2 + PANELS], rest[2 + PANELS : 2 + 2 * PANELS]
    out, s_all, c_all, l_own, it_own, row_sem, own_sem = rest[2 + 2 * PANELS :]
    r, y, c = idx[0], idx[1], idx[3]
    core = r % 2
    t = pl.program_id(0)
    n_col = N_Y * N_Z

    def row_copy(s, h):
        slot = h * N_Y + (y + N_Y - s) % N_Y
        return pltpu.make_async_copy(row_parts[s][h], s_all.at[slot], row_sem.at[slot])

    def own_copies(k):
        return (
            pltpu.make_async_copy(factors[k], l_own, own_sem.at[0]),
            pltpu.make_async_copy(inverses[k], it_own, own_sem.at[1]),
        )

    @pl.when(t == 0)
    def _():
        for h in range(HALVES):
            for s in range(N_Y):
                row_copy(s, h).start()
        for k in range(PANELS):

            @pl.when(c == k)
            def _():
                for copy in own_copies(k):
                    copy.start()
                for copy in own_copies(k):
                    copy.wait()

        for other in range(2):
            for slot in range(N_X):
                base = pl.multiple_of((2 * slot + (core + other) % 2) * SUB, SUB)
                c_all[:, pl.ds(base, SUB), :] = col_parts[other][slot]

    pltpu.make_async_copy(row_parts[0][0], s_all.at[t], row_sem.at[t]).wait()
    i = t * N_ROW + r
    for u in range(HALVES):
        lanes = slice(u * TILE, (u + 1) * TILE)
        j = c + u * n_col

        @pl.when(i >= j)
        def _():
            out[:, lanes] = a_ref[:, lanes] - dot_bf(s_all[t], c_all[u])

        @pl.when(i < j)
        def _():
            out[:, lanes] = a_ref[:, lanes]

    @pl.when(jnp.logical_and(c < PANELS, i > c))
    def _():
        out[:, :TILE] = dot_nn(out[:, :TILE], it_own[...])

    @pl.when(jnp.logical_and(c < PANELS, i == c))
    def _():
        out[:, :TILE] = l_own[...]


def update(idx, matrix, row_parts, col_parts, factors, inverses):
    rows, cols = matrix.shape
    width = PANELS * TILE
    block = pl.BlockSpec((TILE, cols), lambda t: (t, 0))
    return pl.pallas_call(
        update_kernel,
        grid=(rows // TILE,),
        out_shape=jax.ShapeDtypeStruct(matrix.shape, F32),
        in_specs=[SMEM, block] + [ANY] * (HALVES * N_Y) + [VMEM] * 2 + [ANY] * (2 * PANELS),
        out_specs=block,
        scratch_shapes=[
            pltpu.VMEM((rows // TILE, TILE, width), BF16),
            pltpu.VMEM((HALVES, TILE, width), BF16),
            pltpu.VMEM((TILE, TILE), F32),
            pltpu.VMEM((TILE, TILE), F32),
            pltpu.SemaphoreType.DMA((rows // TILE,)),
            pltpu.SemaphoreType.DMA((2,)),
        ],
        name="update",
    )(idx, matrix, *row_parts, *col_parts, *factors, *inverses)


def on_device(matrix):
    row_index = lax.axis_index("row")
    col_index = lax.axis_index("col")
    y_index, z_index = col_index // N_Z, col_index % N_Z
    idx = jnp.stack([row_index, y_index, z_index, col_index]).astype(jnp.int32)
    barrier = lax.optimization_barrier

    sent = pack_top(idx, matrix)
    tiles = pack_y(matrix)
    slices = pick_row(idx, [sent[0]] + [row_shift(sent[s], s) for s in range(1, N_ROW)])
    slices = lax.select_n(y_index, slices, *[y_shift(slices, s) for s in range(1, N_Y)])
    top = pick_top(idx, [slices] + [z_shift(slices, s) for s in range(1, N_Z)])
    top_parts = []
    for s in range(N_X):
        part = x_shift(top, s) if s else top
        top_parts += [part, core_swap(part)]
    top_parts, tiles = barrier((top_parts, tiles))

    shifted = [y_shift(tiles[s], s) for s in range(1, N_Y)]
    l0, it0, lb0, t11, t21, t22 = factor0(idx, top_parts)
    l1, it1, lb1, t22 = factor1(t11, t21, t22)
    tiles, shifted, t22 = barrier((tiles, shifted, t22))
    sent = pack_z(idx, tiles[0], shifted)
    sent, t22 = barrier((sent, t22))
    scattered = [sent[0]] + [z_shift(sent[s], s) for s in range(1, N_Z)]
    l2, it2 = factor2(t22)
    solved = solve(idx, [it0, it1, it2], lb0, lb1, scattered)

    swapped = row_z_swap(solved)
    swapped, solved = barrier((swapped, solved))
    over_z = [solved] + [z_shift(solved, s) for s in range(1, N_Z)]
    over_x = [swapped] + [x_shift(swapped, s) for s in range(1, N_X)]
    low, high = join_z(idx, over_z)
    low, high, over_x = barrier((low, high, over_x))
    col_half = join_x(idx, over_x)
    low_up, high_down = y_shift(low, 1), y_shift(high, N_Y - 1)
    high_up, low_down = y_shift(high, 1), y_shift(low, N_Y - 1)
    low_far, high_far = y_shift(low_up, 1), y_shift(high_down, N_Y - 1)
    row_parts = [low, high, low_up, high_up, low_far, high_far, low_down, high_down]
    col_parts = [col_half, core_swap(col_half)]
    return update(idx, matrix, row_parts, col_parts, [l0, l1, l2], [it0, it1, it2])


def solution(mesh):
    return jax.shard_map(
        on_device, mesh=mesh, in_specs=(P("row", "col"),), out_specs=P("row", "col"), check_vma=False
    )
```

```python
import jax
import jax.numpy as jnp
from jax import lax
from jax.experimental import pallas as pl
from jax.experimental.pallas import tpu as pltpu
from jax.sharding import PartitionSpec as P

TILE = 256
PANELS = 3
NB = 64
PIV = 8
N_ROW = 8
N_Y = 4
N_Z = 8
SUB = TILE // 8
HALVES = 2
F32 = jnp.float32
BF16 = jnp.bfloat16
HIGHEST = lax.Precision.HIGHEST
N_X = 4
Z_GROUP = 4


def dot_nn(a, b):
    return lax.dot_general(a, b, (((1,), (0,)), ((), ())), precision=HIGHEST, preferred_element_type=F32)


def dot_nt(a, b):
    return lax.dot_general(a, b, (((1,), (1,)), ((), ())), precision=HIGHEST, preferred_element_type=F32)


def dot_bf(a, b):
    return lax.dot_general(a, b, (((1,), (1,)), ((), ())), preferred_element_type=F32)


def y_shift(x, s):
    pairs = [(y * N_Z + z, (y + s) % N_Y * N_Z + z) for y in range(N_Y) for z in range(N_Z)]
    return lax.ppermute(x, "col", pairs)


def z_shift(x, s):
    pairs = [(y * N_Z + z, y * N_Z + (z + s) % N_Z) for y in range(N_Y) for z in range(N_Z)]
    return lax.ppermute(x, "col", pairs)


def row_shift(x, s):
    return lax.ppermute(x, "row", [(r, (r + s) % N_ROW) for r in range(N_ROW)])


def z_group_shift(x, s):
    pairs = [
        (y * N_Z + z, y * N_Z + z // Z_GROUP * Z_GROUP + (z % Z_GROUP + s) % Z_GROUP)
        for y in range(N_Y)
        for z in range(N_Z)
    ]
    return lax.ppermute(x, "col", pairs)


def x_shift(x, s):
    return lax.ppermute(x, "row", [(r, (r + 2 * s) % N_ROW) for r in range(N_ROW)])


def core_swap(x):
    return lax.ppermute(x, "row", [(r, r ^ 1) for r in range(N_ROW)])


def row_z_swap(x):
    n_col = N_Y * N_Z
    pairs = [
        (r * n_col + y * N_Z + z, z * n_col + y * N_Z + r)
        for r in range(N_ROW)
        for y in range(N_Y)
        for z in range(N_Z)
    ]
    return lax.ppermute(x, ("row", "col"), pairs)


SMEM = pl.BlockSpec(memory_space=pltpu.SMEM)
ANY = pl.BlockSpec(memory_space=pl.ANY)
VMEM = pl.BlockSpec(memory_space=pltpu.VMEM)


def pack_top_kernel(idx, tile, *outs):
    r = idx[0]
    for s in range(N_ROW):
        base = pl.multiple_of((r + s) % N_ROW * SUB, SUB)
        outs[s][...] = tile[pl.ds(base, SUB), :]


def pack_top(idx, matrix):
    return pl.pallas_call(
        pack_top_kernel,
        grid=(1,),
        out_shape=[jax.ShapeDtypeStruct((SUB, TILE), F32)] * N_ROW,
        in_specs=[SMEM, pl.BlockSpec((TILE, TILE), lambda i: (0, 0))],
        out_specs=[pl.BlockSpec((SUB, TILE), lambda i: (0, 0))] * N_ROW,
        name="pack_top",
    )(idx, matrix)


def pack_y_kernel(*refs):
    for s in range(N_Y):
        refs[N_Y + s][...] = refs[s][...]


def pack_y(matrix):
    return pl.pallas_call(
        pack_y_kernel,
        grid=(HALVES,),
        out_shape=[jax.ShapeDtypeStruct((HALVES, TILE, TILE), F32)] * N_Y,
        in_specs=[pl.BlockSpec((TILE, TILE), lambda h, s=s: (h * N_Y + s, 0)) for s in range(N_Y)],
        out_specs=[pl.BlockSpec((None, TILE, TILE), lambda h: (h, 0, 0))] * N_Y,
        name="pack_y",
    )(*[matrix] * N_Y)


def pack_z_kernel(idx, own, *rest):
    got, outs = rest[: N_Y - 1], rest[N_Y - 1 :]
    y, z = idx[1], idx[2]
    for source, ref in enumerate((own,) + tuple(got)):

        @pl.when(y == source)
        def _():
            for s in range(N_Z):
                base = pl.multiple_of((z + s) % N_Z * SUB, SUB)
                outs[s][...] = ref[:, pl.ds(base, SUB), :]


def pack_z(idx, own, got):
    return pl.pallas_call(
        pack_z_kernel,
        out_shape=[jax.ShapeDtypeStruct((HALVES, SUB, TILE), F32)] * N_Z,
        in_specs=[SMEM] + [VMEM] * N_Y,
        out_specs=[VMEM] * N_Z,
        name="pack_z",
    )(idx, own, *got)


def pick_row_kernel(idx, *rest):
    got, out = rest[:-1], rest[-1]
    first = idx[3] % PANELS
    for s, ref in enumerate(got):
        source = (idx[0] + N_ROW - s) % N_ROW
        for n in range(2):

            @pl.when(source == (first + n) % PANELS)
            def _():
                out[n] = ref[...]


def pick_row(idx, got):
    return pl.pallas_call(
        pick_row_kernel,
        out_shape=jax.ShapeDtypeStruct((2, SUB, TILE), F32),
        in_specs=[SMEM] + [VMEM] * N_ROW,
        out_specs=VMEM,
        name="pick_row",
    )(idx, *got)


def pick_top_kernel(idx, *rest):
    got, out = rest[:-1], rest[-1]
    for s, ref in enumerate(got):
        source = (idx[2] % Z_GROUP + Z_GROUP - s) % Z_GROUP

        @pl.when(source < PANELS)
        def _():
            out[source] = ref[...]


def pick_top(idx, got):
    return pl.pallas_call(
        pick_top_kernel,
        out_shape=jax.ShapeDtypeStruct((PANELS, 2, SUB, TILE), F32),
        in_specs=[SMEM] + [VMEM] * Z_GROUP,
        out_specs=VMEM,
        name="pick_top",
    )(idx, *got)


def eliminate(block):
    sub = lax.broadcasted_iota(jnp.int32, (8, 2 * NB), 0)
    lane = lax.broadcasted_iota(jnp.int32, (8, 2 * NB), 1)
    groups = NB // 8

    def spread(x):
        return jnp.broadcast_to(x, (8, 2 * NB))

    m = []
    for g in range(groups):
        eye = jnp.where(lane == sub + (8 * g + NB), F32(1), F32(0))
        m.append(jnp.concatenate([block[8 * g : 8 * g + 8], eye[:, NB:]], axis=1))
    scale = []
    for g0 in range(groups):
        j = g0 * PIV
        cols = [[spread(m[g][:, j + q : j + q + 1]) for g in range(g0, groups)] for q in range(PIV)]
        rows = [spread(m[g0][q : q + 1, :]) for q in range(PIV)]
        a = {}
        for q in range(PIV):
            for i in range(q, PIV):
                a[i, q] = spread(cols[q][0][i : i + 1, :])
        low = {}
        inv = []
        pivots = None
        for q in range(PIV):
            inv.append(1.0 / a[q, q])
            pivots = a[q, q] if pivots is None else jnp.where(sub >= q, a[q, q], pivots)
            for i in range(q + 1, PIV):
                low[i, q] = a[i, q] * inv[q]
            for jj in range(q + 1, PIV):
                for i in range(jj, PIV):
                    a[i, jj] = a[i, jj] - low[i, q] * a[jj, q]
        scale.append(lax.rsqrt(pivots))
        scaled = []
        for q in range(PIV):
            for i in range(q + 1, PIV):
                rows[i] = rows[i] - low[i, q] * rows[q]
            scaled.append(rows[q] * inv[q])
        for g in range(g0, groups):
            x = [cols[q][g - g0] for q in range(PIV)]
            updated = m[g]
            for q in range(PIV):
                for i in range(q + 1, PIV):
                    x[i] = x[i] - low[i, q] * x[q]
                part = x[q]
                if g == g0:
                    part = jnp.where(sub > q, part, F32(0))
                updated = updated - part * scaled[q]
            m[g] = updated
    return jnp.concatenate([m[g] * scale[g] for g in range(groups)], axis=0)


def chol_inv(w, lc):
    blocks = TILE // NB
    rows = lax.broadcasted_iota(jnp.int32, (2 * TILE, NB), 0)
    r64 = lax.broadcasted_iota(jnp.int32, (NB, NB), 0)
    c64 = lax.broadcasted_iota(jnp.int32, (NB, NB), 1)

    def step(b, carry):
        base = pl.multiple_of(b * NB, NB)
        m = eliminate(w[b, pl.ds(base, NB), :]).T
        lower = jnp.where(r64 >= c64, m[:NB], F32(0))
        inv_t = jnp.where(r64 <= c64, m[NB:], F32(0))
        p = jnp.where(rows >= base + NB, dot_nn(w[b], inv_t), F32(0))
        lc[b] = p
        lc[b, pl.ds(base, NB), :] = lower
        for bj in range(1, blocks):

            @pl.when(bj > b)
            def _():
                w[bj] = w[bj] - dot_nt(p, p[bj * NB : (bj + 1) * NB])

        return carry

    lax.fori_loop(0, blocks, step, 0)


def factor_tile(tile, l_ref, it_ref, w, lc):
    blocks = TILE // NB
    r = lax.broadcasted_iota(jnp.int32, (TILE, NB), 0)
    c = lax.broadcasted_iota(jnp.int32, (TILE, NB), 1)
    for b in range(blocks):
        w[b, :TILE, :] = tile[:, b * NB : (b + 1) * NB]
        w[b, TILE:, :] = jnp.where(r == c + b * NB, F32(1), F32(0))
    chol_inv(w, lc)
    l_ref[...] = jnp.concatenate([lc[b, :TILE, :] for b in range(blocks)], axis=1)
    inv_t = jnp.concatenate([lc[b, TILE:, :] for b in range(blocks)], axis=1)
    it_ref[...] = inv_t
    return inv_t


def factor0_kernel(idx, *rest):
    got = rest[:2]
    l_ref, it_ref, lb_ref, t11, t21, t22, top, w, lc = rest[2:]
    core = idx[0] % 2
    for x in range(N_X):
        for other in range(2):
            base = pl.multiple_of((2 * x + (core + other) % 2) * SUB, SUB)
            top[:, :, pl.ds(base, SUB), :] = got[other][x]
    inv_t = factor_tile(top[0, 0], l_ref, it_ref, w, lc)
    low1 = dot_nn(top[0, 1], inv_t).astype(BF16)
    low2 = dot_nn(top[2, 1].T, inv_t).astype(BF16)
    lb_ref[0] = low1
    lb_ref[1] = low2
    t11[...] = top[1, 0] - dot_bf(low1, low1)
    t21[...] = top[1, 1] - dot_bf(low2, low1)
    t22[...] = top[2, 0] - dot_bf(low2, low2)


def factor1_kernel(t11, t21, t22, l_ref, it_ref, lb_ref, rest_ref, w, lc):
    inv_t = factor_tile(t11[...], l_ref, it_ref, w, lc)
    low = dot_nn(t21[...], inv_t).astype(BF16)
    lb_ref[...] = low
    rest_ref[...] = t22[...] - dot_bf(low, low)


def factor2_kernel(t22, l_ref, it_ref, w, lc):
    factor_tile(t22[...], l_ref, it_ref, w, lc)


SQUARE = jax.ShapeDtypeStruct((TILE, TILE), F32)
FACTOR_COST = pl.CostEstimate(flops=15_000_000_000, transcendentals=0, bytes_accessed=2_000_000)
WORK = [pltpu.VMEM((TILE // NB, 2 * TILE, NB), F32)] * 2


def factor0(idx, got):
    return pl.pallas_call(
        factor0_kernel,
        out_shape=[SQUARE, SQUARE, jax.ShapeDtypeStruct((2, TILE, TILE), BF16), SQUARE, SQUARE, SQUARE],
        in_specs=[SMEM] + [VMEM] * 2,
        out_specs=[VMEM] * 6,
        scratch_shapes=[pltpu.VMEM((PANELS, 2, TILE, TILE), F32)] + WORK,
        cost_estimate=FACTOR_COST,
        name="factor0",
    )(idx, *got)


def factor1(t11, t21, t22):
    return pl.pallas_call(
        factor1_kernel,
        out_shape=[SQUARE, SQUARE, jax.ShapeDtypeStruct((TILE, TILE), BF16), SQUARE],
        in_specs=[VMEM] * 3,
        out_specs=[VMEM] * 4,
        scratch_shapes=WORK,
        cost_estimate=FACTOR_COST,
        name="factor1",
    )(t11, t21, t22)


def factor2(t22):
    return pl.pallas_call(
        factor2_kernel,
        out_shape=[SQUARE, SQUARE],
        in_specs=[VMEM],
        out_specs=[VMEM] * 2,
        scratch_shapes=WORK,
        cost_estimate=FACTOR_COST,
        name="factor2",
    )(t22)


def solve_kernel(idx, it0, it1, it2, lb0, lb1, *rest):
    got, out, rows = rest[:N_Z], rest[N_Z], rest[N_Z + 1]
    r, y, z = idx[0], idx[1], idx[2]
    for s in range(N_Z):
        source = (z + N_Z - s) % N_Z

        @pl.when(source < PANELS)
        def _():
            rows[source] = got[s][...]

    chunk = HALVES * SUB
    half = lax.broadcasted_iota(jnp.int32, (chunk, TILE), 0) // SUB
    tile_row = (half * N_Y + y) * N_ROW + r

    def keep(k, left, inverse):
        return jnp.where(tile_row > k, dot_nn(left, inverse[...]), F32(0)).astype(BF16)

    s0 = keep(0, rows[0].reshape(chunk, TILE), it0)
    s1 = keep(1, rows[1].reshape(chunk, TILE) - dot_bf(s0, lb0[0]), it1)
    s2 = keep(2, rows[2].reshape(chunk, TILE) - dot_bf(s0, lb0[1]) - dot_bf(s1, lb1[...]), it2)
    for k, done in enumerate((s0, s1, s2)):
        out[:, :, k * TILE : (k + 1) * TILE] = done.reshape(HALVES, SUB, TILE)


def solve(idx, inverses, lb0, lb1, got):
    return pl.pallas_call(
        solve_kernel,
        out_shape=jax.ShapeDtypeStruct((HALVES, SUB, PANELS * TILE), BF16),
        in_specs=[SMEM] + [VMEM] * (PANELS + 2 + N_Z),
        out_specs=VMEM,
        scratch_shapes=[pltpu.VMEM((PANELS, HALVES, SUB, TILE), F32)],
        name="solve",
    )(idx, *inverses, lb0, lb1, *got)


def join_z_kernel(idx, *rest):
    got, outs = rest[:N_Z], rest[N_Z:]
    for s in range(N_Z):
        base = pl.multiple_of((idx[2] + N_Z - s) % N_Z * SUB, SUB)
        for h in range(HALVES):
            outs[h][pl.ds(base, SUB), :] = got[s][h]


def join_z(idx, got):
    return pl.pallas_call(
        join_z_kernel,
        out_shape=[jax.ShapeDtypeStruct((TILE, PANELS * TILE), BF16)] * HALVES,
        in_specs=[SMEM] + [VMEM] * N_Z,
        out_specs=[VMEM] * HALVES,
        name="join_z",
    )(idx, *got)


def join_x_kernel(idx, *rest):
    got, out = rest[:-1], rest[-1]
    for s in range(N_X):
        out[(idx[0] // 2 + N_X - s) % N_X] = got[s][...]


def join_x(idx, got):
    return pl.pallas_call(
        join_x_kernel,
        out_shape=jax.ShapeDtypeStruct((N_X,) + got[0].shape, got[0].dtype),
        in_specs=[SMEM] + [VMEM] * N_X,
        out_specs=VMEM,
        name="join_x",
    )(idx, *got)


def update_kernel(idx, a_ref, *rest):
    row_parts = [rest[HALVES * s : HALVES * (s + 1)] for s in range(N_Y)]
    rest = rest[HALVES * N_Y :]
    col_parts, factors, inverses = rest[:2], rest[2 : 2 + PANELS], rest[2 + PANELS : 2 + 2 * PANELS]
    out, s_all, c_all, l_own, it_own, row_sem, own_sem = rest[2 + 2 * PANELS :]
    r, y, c = idx[0], idx[1], idx[3]
    core = r % 2
    t = pl.program_id(0)
    n_col = N_Y * N_Z

    def row_copy(s, h):
        slot = h * N_Y + (y + N_Y - s) % N_Y
        return pltpu.make_async_copy(row_parts[s][h], s_all.at[slot], row_sem.at[slot])

    def own_copies(k):
        return (
            pltpu.make_async_copy(factors[k], l_own, own_sem.at[0]),
            pltpu.make_async_copy(inverses[k], it_own, own_sem.at[1]),
        )

    @pl.when(t == 0)
    def _():
        for h in range(HALVES):
            for s in range(N_Y):
                row_copy(s, h).start()
        for k in range(PANELS):

            @pl.when(c == k)
            def _():
                for copy in own_copies(k):
                    copy.start()
                for copy in own_copies(k):
                    copy.wait()

        for other in range(2):
            for slot in range(N_X):
                base = pl.multiple_of((2 * slot + (core + other) % 2) * SUB, SUB)
                c_all[:, pl.ds(base, SUB), :] = col_parts[other][slot]

    pltpu.make_async_copy(row_parts[0][0], s_all.at[t], row_sem.at[t]).wait()
    i = t * N_ROW + r
    for u in range(HALVES):
        lanes = slice(u * TILE, (u + 1) * TILE)
        j = c + u * n_col

        @pl.when(i >= j)
        def _():
            out[:, lanes] = a_ref[:, lanes] - dot_bf(s_all[t], c_all[u])

        @pl.when(i < j)
        def _():
            out[:, lanes] = a_ref[:, lanes]

    @pl.when(jnp.logical_and(c < PANELS, i > c))
    def _():
        out[:, :TILE] = dot_nn(out[:, :TILE], it_own[...])

    @pl.when(jnp.logical_and(c < PANELS, i == c))
    def _():
        out[:, :TILE] = l_own[...]


def update(idx, matrix, row_parts, col_parts, factors, inverses):
    rows, cols = matrix.shape
    width = PANELS * TILE
    block = pl.BlockSpec((TILE, cols), lambda t: (t, 0))
    return pl.pallas_call(
        update_kernel,
        grid=(rows // TILE,),
        out_shape=jax.ShapeDtypeStruct(matrix.shape, F32),
        in_specs=[SMEM, block] + [ANY] * (HALVES * N_Y) + [VMEM] * 2 + [ANY] * (2 * PANELS),
        out_specs=block,
        scratch_shapes=[
            pltpu.VMEM((rows // TILE, TILE, width), BF16),
            pltpu.VMEM((HALVES, TILE, width), BF16),
            pltpu.VMEM((TILE, TILE), F32),
            pltpu.VMEM((TILE, TILE), F32),
            pltpu.SemaphoreType.DMA((rows // TILE,)),
            pltpu.SemaphoreType.DMA((2,)),
        ],
        name="update",
    )(idx, matrix, *row_parts, *col_parts, *factors, *inverses)


def on_device(matrix):
    row_index = lax.axis_index("row")
    col_index = lax.axis_index("col")
    y_index, z_index = col_index // N_Z, col_index % N_Z
    idx = jnp.stack([row_index, y_index, z_index, col_index]).astype(jnp.int32)
    barrier = lax.optimization_barrier

    sent = pack_top(idx, matrix)
    tiles = pack_y(matrix)
    slices = pick_row(idx, [sent[0]] + [row_shift(sent[s], s) for s in range(1, N_ROW)])
    slices = lax.select_n(y_index, slices, *[y_shift(slices, s) for s in range(1, N_Y)])
    slices, tiles = barrier((slices, tiles))
    slices = jnp.where(z_index < Z_GROUP, slices, z_shift(slices, Z_GROUP))
    top = pick_top(idx, [slices] + [z_group_shift(slices, s) for s in range(1, Z_GROUP)])
    top = join_x(idx, [top] + [x_shift(top, s) for s in range(1, N_X)])
    top_parts = [top, core_swap(top)]
    top_parts, tiles = barrier((top_parts, tiles))

    shifted = [y_shift(tiles[s], s) for s in range(1, N_Y)]
    l0, it0, lb0, t11, t21, t22 = factor0(idx, top_parts)
    l1, it1, lb1, t22 = factor1(t11, t21, t22)
    tiles, shifted, t22 = barrier((tiles, shifted, t22))
    sent = pack_z(idx, tiles[0], shifted)
    sent, t22 = barrier((sent, t22))
    scattered = [sent[0]] + [z_shift(sent[s], s) for s in range(1, N_Z)]
    l2, it2 = factor2(t22)
    solved = solve(idx, [it0, it1, it2], lb0, lb1, scattered)

    swapped = row_z_swap(solved)
    over_z = [solved] + [z_shift(solved, s) for s in range(1, N_Z)]
    over_x = [swapped] + [x_shift(swapped, s) for s in range(1, N_X)]
    low, high = join_z(idx, over_z)
    low, high, over_x = barrier((low, high, over_x))
    col_half = join_x(idx, over_x)
    low_up, high_down = y_shift(low, 1), y_shift(high, N_Y - 1)
    high_up, low_down = y_shift(high, 1), y_shift(low, N_Y - 1)
    low_far, high_far = y_shift(low_up, 1), y_shift(high_down, N_Y - 1)
    row_parts = [low, high, low_up, high_up, low_far, high_far, low_down, high_down]
    col_parts = [col_half, core_swap(col_half)]
    return update(idx, matrix, row_parts, col_parts, [l0, l1, l2], [it0, it1, it2])


def solution(mesh):
    return jax.shard_map(
        on_device, mesh=mesh, in_specs=(P("row", "col"),), out_specs=P("row", "col"), check_vma=False
    )
```

```python
import jax
import jax.numpy as jnp
from jax import lax
from jax.experimental import pallas as pl
from jax.experimental.pallas import tpu as pltpu
from jax.sharding import PartitionSpec as P

TILE = 256
PANELS = 3
NB = 64
PIV = 8
N_ROW = 8
N_Y = 4
N_Z = 8
SUB = TILE // 8
HALVES = 2
F32 = jnp.float32
BF16 = jnp.bfloat16
HIGHEST = lax.Precision.HIGHEST
N_X = 4
Z_GROUP = 4


def dot_nn(a, b):
    return lax.dot_general(a, b, (((1,), (0,)), ((), ())), precision=HIGHEST, preferred_element_type=F32)


def dot_nt(a, b):
    return lax.dot_general(a, b, (((1,), (1,)), ((), ())), precision=HIGHEST, preferred_element_type=F32)


def dot_bf(a, b):
    return lax.dot_general(a, b, (((1,), (1,)), ((), ())), preferred_element_type=F32)


def y_shift(x, s):
    pairs = [(y * N_Z + z, (y + s) % N_Y * N_Z + z) for y in range(N_Y) for z in range(N_Z)]
    return lax.ppermute(x, "col", pairs)


def yz_shift(x, sy, sz):
    pairs = [
        (y * N_Z + z, (y + sy) % N_Y * N_Z + (z + sz) % N_Z) for y in range(N_Y) for z in range(N_Z)
    ]
    return lax.ppermute(x, "col", pairs)


def z_shift(x, s):
    pairs = [(y * N_Z + z, y * N_Z + (z + s) % N_Z) for y in range(N_Y) for z in range(N_Z)]
    return lax.ppermute(x, "col", pairs)


def row_shift(x, s):
    return lax.ppermute(x, "row", [(r, (r + s) % N_ROW) for r in range(N_ROW)])


def z_group_shift(x, s):
    pairs = [
        (y * N_Z + z, y * N_Z + z // Z_GROUP * Z_GROUP + (z % Z_GROUP + s) % Z_GROUP)
        for y in range(N_Y)
        for z in range(N_Z)
    ]
    return lax.ppermute(x, "col", pairs)


def x_shift(x, s):
    return lax.ppermute(x, "row", [(r, (r + 2 * s) % N_ROW) for r in range(N_ROW)])


def core_swap(x):
    return lax.ppermute(x, "row", [(r, r ^ 1) for r in range(N_ROW)])


def row_z_swap(x):
    n_col = N_Y * N_Z
    pairs = [
        (r * n_col + y * N_Z + z, z * n_col + y * N_Z + r)
        for r in range(N_ROW)
        for y in range(N_Y)
        for z in range(N_Z)
    ]
    return lax.ppermute(x, ("row", "col"), pairs)


SMEM = pl.BlockSpec(memory_space=pltpu.SMEM)
ANY = pl.BlockSpec(memory_space=pl.ANY)
VMEM = pl.BlockSpec(memory_space=pltpu.VMEM)


def pack_top_kernel(idx, tile, *outs):
    r = idx[0]
    for s in range(N_ROW):
        base = pl.multiple_of((r + s) % N_ROW * SUB, SUB)
        outs[s][...] = tile[pl.ds(base, SUB), :]


def pack_top(idx, matrix):
    return pl.pallas_call(
        pack_top_kernel,
        grid=(1,),
        out_shape=[jax.ShapeDtypeStruct((SUB, TILE), F32)] * N_ROW,
        in_specs=[SMEM, pl.BlockSpec((TILE, TILE), lambda i: (0, 0))],
        out_specs=[pl.BlockSpec((SUB, TILE), lambda i: (0, 0))] * N_ROW,
        name="pack_top",
    )(idx, matrix)


def pack_y_kernel(*refs):
    for s in range(N_Y):
        refs[N_Y + s][...] = refs[s][...]


def pack_y(matrix):
    return pl.pallas_call(
        pack_y_kernel,
        grid=(HALVES,),
        out_shape=[jax.ShapeDtypeStruct((HALVES, TILE, TILE), F32)] * N_Y,
        in_specs=[pl.BlockSpec((TILE, TILE), lambda h, s=s: (h * N_Y + s, 0)) for s in range(N_Y)],
        out_specs=[pl.BlockSpec((None, TILE, TILE), lambda h: (h, 0, 0))] * N_Y,
        name="pack_y",
    )(*[matrix] * N_Y)


def pack_z_kernel(idx, own, *rest):
    got, outs = rest[: N_Y - 1], rest[N_Y - 1 :]
    y, z = idx[1], idx[2]
    for source, ref in enumerate((own,) + tuple(got)):

        @pl.when(y == source)
        def _():
            for s in range(N_Z):
                base = pl.multiple_of((z + s) % N_Z * SUB, SUB)
                outs[s][...] = ref[:, pl.ds(base, SUB), :]


def pack_z(idx, own, got):
    return pl.pallas_call(
        pack_z_kernel,
        out_shape=[jax.ShapeDtypeStruct((HALVES, SUB, TILE), F32)] * N_Z,
        in_specs=[SMEM] + [VMEM] * N_Y,
        out_specs=[VMEM] * N_Z,
        name="pack_z",
    )(idx, own, *got)


def pick_row_kernel(idx, *rest):
    got, out = rest[:-1], rest[-1]
    first = idx[3] % PANELS
    for s, ref in enumerate(got):
        source = (idx[0] + N_ROW - s) % N_ROW
        for n in range(2):

            @pl.when(source == (first + n) % PANELS)
            def _():
                out[n] = ref[...]


def pick_row(idx, got):
    return pl.pallas_call(
        pick_row_kernel,
        out_shape=jax.ShapeDtypeStruct((2, SUB, TILE), F32),
        in_specs=[SMEM] + [VMEM] * N_ROW,
        out_specs=VMEM,
        name="pick_row",
    )(idx, *got)


def pick_top_kernel(idx, *rest):
    got, out = rest[:-1], rest[-1]
    for s, ref in enumerate(got):
        source = (idx[2] % Z_GROUP + Z_GROUP - s) % Z_GROUP

        @pl.when(source < PANELS)
        def _():
            out[source] = ref[...]


def pick_top(idx, got):
    return pl.pallas_call(
        pick_top_kernel,
        out_shape=jax.ShapeDtypeStruct((PANELS, 2, SUB, TILE), F32),
        in_specs=[SMEM] + [VMEM] * Z_GROUP,
        out_specs=VMEM,
        name="pick_top",
    )(idx, *got)


def eliminate(block):
    sub = lax.broadcasted_iota(jnp.int32, (8, 2 * NB), 0)
    lane = lax.broadcasted_iota(jnp.int32, (8, 2 * NB), 1)
    groups = NB // 8

    def spread(x):
        return jnp.broadcast_to(x, (8, 2 * NB))

    m = []
    for g in range(groups):
        eye = jnp.where(lane == sub + (8 * g + NB), F32(1), F32(0))
        m.append(jnp.concatenate([block[8 * g : 8 * g + 8], eye[:, NB:]], axis=1))
    scale = []
    for g0 in range(groups):
        j = g0 * PIV
        cols = [[spread(m[g][:, j + q : j + q + 1]) for g in range(g0, groups)] for q in range(PIV)]
        rows = [spread(m[g0][q : q + 1, :]) for q in range(PIV)]
        a = {}
        for q in range(PIV):
            for i in range(q, PIV):
                a[i, q] = spread(cols[q][0][i : i + 1, :])
        low = {}
        inv = []
        pivots = None
        for q in range(PIV):
            inv.append(1.0 / a[q, q])
            pivots = a[q, q] if pivots is None else jnp.where(sub >= q, a[q, q], pivots)
            for i in range(q + 1, PIV):
                low[i, q] = a[i, q] * inv[q]
            for jj in range(q + 1, PIV):
                for i in range(jj, PIV):
                    a[i, jj] = a[i, jj] - low[i, q] * a[jj, q]
        scale.append(lax.rsqrt(pivots))
        scaled = []
        for q in range(PIV):
            for i in range(q + 1, PIV):
                rows[i] = rows[i] - low[i, q] * rows[q]
            scaled.append(rows[q] * inv[q])
        for g in range(g0, groups):
            x = [cols[q][g - g0] for q in range(PIV)]
            updated = m[g]
            for q in range(PIV):
                for i in range(q + 1, PIV):
                    x[i] = x[i] - low[i, q] * x[q]
                part = x[q]
                if g == g0:
                    part = jnp.where(sub > q, part, F32(0))
                updated = updated - part * scaled[q]
            m[g] = updated
    return jnp.concatenate([m[g] * scale[g] for g in range(groups)], axis=0)


def chol_inv(w, lc):
    blocks = TILE // NB
    rows = lax.broadcasted_iota(jnp.int32, (2 * TILE, NB), 0)
    r64 = lax.broadcasted_iota(jnp.int32, (NB, NB), 0)
    c64 = lax.broadcasted_iota(jnp.int32, (NB, NB), 1)

    def step(b, carry):
        base = pl.multiple_of(b * NB, NB)
        m = eliminate(w[b, pl.ds(base, NB), :]).T
        lower = jnp.where(r64 >= c64, m[:NB], F32(0))
        inv_t = jnp.where(r64 <= c64, m[NB:], F32(0))
        p = jnp.where(rows >= base + NB, dot_nn(w[b], inv_t), F32(0))
        lc[b] = p
        lc[b, pl.ds(base, NB), :] = lower
        for bj in range(1, blocks):

            @pl.when(bj > b)
            def _():
                w[bj] = w[bj] - dot_nt(p, p[bj * NB : (bj + 1) * NB])

        return carry

    lax.fori_loop(0, blocks, step, 0)


def factor_tile(tile, l_ref, it_ref, w, lc):
    blocks = TILE // NB
    r = lax.broadcasted_iota(jnp.int32, (TILE, NB), 0)
    c = lax.broadcasted_iota(jnp.int32, (TILE, NB), 1)
    for b in range(blocks):
        w[b, :TILE, :] = tile[:, b * NB : (b + 1) * NB]
        w[b, TILE:, :] = jnp.where(r == c + b * NB, F32(1), F32(0))
    chol_inv(w, lc)
    l_ref[...] = jnp.concatenate([lc[b, :TILE, :] for b in range(blocks)], axis=1)
    inv_t = jnp.concatenate([lc[b, TILE:, :] for b in range(blocks)], axis=1)
    it_ref[...] = inv_t
    return inv_t


def factor0_kernel(idx, *rest):
    got = rest[:2]
    l_ref, it_ref, lb_ref, t11, t21, t22, top, w, lc = rest[2:]
    core = idx[0] % 2
    for x in range(N_X):
        for other in range(2):
            base = pl.multiple_of((2 * x + (core + other) % 2) * SUB, SUB)
            top[:, :, pl.ds(base, SUB), :] = got[other][x]
    inv_t = factor_tile(top[0, 0], l_ref, it_ref, w, lc)
    low1 = dot_nn(top[0, 1], inv_t).astype(BF16)
    low2 = dot_nn(top[2, 1].T, inv_t).astype(BF16)
    lb_ref[0] = low1
    lb_ref[1] = low2
    t11[...] = top[1, 0] - dot_bf(low1, low1)
    t21[...] = top[1, 1] - dot_bf(low2, low1)
    t22[...] = top[2, 0] - dot_bf(low2, low2)


def factor1_kernel(t11, t21, t22, l_ref, it_ref, lb_ref, rest_ref, w, lc):
    inv_t = factor_tile(t11[...], l_ref, it_ref, w, lc)
    low = dot_nn(t21[...], inv_t).astype(BF16)
    lb_ref[...] = low
    rest_ref[...] = t22[...] - dot_bf(low, low)


def factor2_kernel(t22, l_ref, it_ref, w, lc):
    factor_tile(t22[...], l_ref, it_ref, w, lc)


SQUARE = jax.ShapeDtypeStruct((TILE, TILE), F32)
FACTOR_COST = pl.CostEstimate(flops=15_000_000_000, transcendentals=0, bytes_accessed=2_000_000)
WORK = [pltpu.VMEM((TILE // NB, 2 * TILE, NB), F32)] * 2


def factor0(idx, got):
    return pl.pallas_call(
        factor0_kernel,
        out_shape=[SQUARE, SQUARE, jax.ShapeDtypeStruct((2, TILE, TILE), BF16), SQUARE, SQUARE, SQUARE],
        in_specs=[SMEM] + [VMEM] * 2,
        out_specs=[VMEM] * 6,
        scratch_shapes=[pltpu.VMEM((PANELS, 2, TILE, TILE), F32)] + WORK,
        name="factor0",
    )(idx, *got)


def factor1(t11, t21, t22):
    return pl.pallas_call(
        factor1_kernel,
        out_shape=[SQUARE, SQUARE, jax.ShapeDtypeStruct((TILE, TILE), BF16), SQUARE],
        in_specs=[VMEM] * 3,
        out_specs=[VMEM] * 4,
        scratch_shapes=WORK,
        cost_estimate=FACTOR_COST,
        name="factor1",
    )(t11, t21, t22)


def factor2(t22):
    return pl.pallas_call(
        factor2_kernel,
        out_shape=[SQUARE, SQUARE],
        in_specs=[VMEM],
        out_specs=[VMEM] * 2,
        scratch_shapes=WORK,
        cost_estimate=FACTOR_COST,
        name="factor2",
    )(t22)


def solve_kernel(idx, it0, it1, it2, lb0, lb1, *rest):
    got, out, rows = rest[:N_Z], rest[N_Z], rest[N_Z + 1]
    r, y, z = idx[0], idx[1], idx[2]
    for s in range(N_Z):
        source = (z + N_Z - s) % N_Z

        @pl.when(source < PANELS)
        def _():
            rows[source] = got[s][...]

    chunk = HALVES * SUB
    half = lax.broadcasted_iota(jnp.int32, (chunk, TILE), 0) // SUB
    tile_row = (half * N_Y + y) * N_ROW + r

    def keep(k, left, inverse):
        return jnp.where(tile_row > k, dot_nn(left, inverse[...]), F32(0)).astype(BF16)

    s0 = keep(0, rows[0].reshape(chunk, TILE), it0)
    s1 = keep(1, rows[1].reshape(chunk, TILE) - dot_bf(s0, lb0[0]), it1)
    s2 = keep(2, rows[2].reshape(chunk, TILE) - dot_bf(s0, lb0[1]) - dot_bf(s1, lb1[...]), it2)
    for k, done in enumerate((s0, s1, s2)):
        out[:, :, k * TILE : (k + 1) * TILE] = done.reshape(HALVES, SUB, TILE)


def solve(idx, inverses, lb0, lb1, got):
    return pl.pallas_call(
        solve_kernel,
        out_shape=jax.ShapeDtypeStruct((HALVES, SUB, PANELS * TILE), BF16),
        in_specs=[SMEM] + [VMEM] * (PANELS + 2 + N_Z),
        out_specs=VMEM,
        scratch_shapes=[pltpu.VMEM((PANELS, HALVES, SUB, TILE), F32)],
        name="solve",
    )(idx, *inverses, lb0, lb1, *got)


def join_z_kernel(idx, *rest):
    got, outs = rest[:N_Z], rest[N_Z:]
    for s in range(N_Z):
        base = pl.multiple_of((idx[2] + N_Z - s) % N_Z * SUB, SUB)
        for h in range(HALVES):
            outs[h][pl.ds(base, SUB), :] = got[s][h]


def join_z(idx, got):
    return pl.pallas_call(
        join_z_kernel,
        out_shape=[jax.ShapeDtypeStruct((TILE, PANELS * TILE), BF16)] * HALVES,
        in_specs=[SMEM] + [VMEM] * N_Z,
        out_specs=[VMEM] * HALVES,
        name="join_z",
    )(idx, *got)


def join_x_kernel(idx, *rest):
    got, out = rest[:-1], rest[-1]
    for s in range(N_X):
        out[(idx[0] // 2 + N_X - s) % N_X] = got[s][...]


def join_x(idx, got):
    return pl.pallas_call(
        join_x_kernel,
        out_shape=jax.ShapeDtypeStruct((N_X,) + got[0].shape, got[0].dtype),
        in_specs=[SMEM] + [VMEM] * N_X,
        out_specs=VMEM,
        name="join_x",
    )(idx, *got)


def update_kernel(idx, a_ref, *rest):
    row_parts = [rest[HALVES * s : HALVES * (s + 1)] for s in range(N_Y)]
    rest = rest[HALVES * N_Y :]
    col_parts, factors, inverses = rest[:2], rest[2 : 2 + PANELS], rest[2 + PANELS : 2 + 2 * PANELS]
    out, s_all, c_all, l_own, it_own, row_sem, own_sem = rest[2 + 2 * PANELS :]
    r, y, c = idx[0], idx[1], idx[3]
    core = r % 2
    t = pl.program_id(0)
    n_col = N_Y * N_Z

    def row_copy(s, h):
        slot = h * N_Y + (y + N_Y - s) % N_Y
        return pltpu.make_async_copy(row_parts[s][h], s_all.at[slot], row_sem.at[slot])

    def own_copies(k):
        return (
            pltpu.make_async_copy(factors[k], l_own, own_sem.at[0]),
            pltpu.make_async_copy(inverses[k], it_own, own_sem.at[1]),
        )

    @pl.when(t == 0)
    def _():
        for h in range(HALVES):
            for s in range(N_Y):
                row_copy(s, h).start()
        for k in range(PANELS):

            @pl.when(c == k)
            def _():
                for copy in own_copies(k):
                    copy.start()
                for copy in own_copies(k):
                    copy.wait()

        for other in range(2):
            for slot in range(N_X):
                base = pl.multiple_of((2 * slot + (core + other) % 2) * SUB, SUB)
                c_all[:, pl.ds(base, SUB), :] = col_parts[other][slot]

    pltpu.make_async_copy(row_parts[0][0], s_all.at[t], row_sem.at[t]).wait()
    i = t * N_ROW + r
    for u in range(HALVES):
        lanes = slice(u * TILE, (u + 1) * TILE)
        j = c + u * n_col

        @pl.when(i >= j)
        def _():
            out[:, lanes] = a_ref[:, lanes] - dot_bf(s_all[t], c_all[u])

        @pl.when(i < j)
        def _():
            out[:, lanes] = a_ref[:, lanes]

    @pl.when(jnp.logical_and(c < PANELS, i > c))
    def _():
        out[:, :TILE] = dot_nn(out[:, :TILE], it_own[...])

    @pl.when(jnp.logical_and(c < PANELS, i == c))
    def _():
        out[:, :TILE] = l_own[...]


def update(idx, matrix, row_parts, col_parts, factors, inverses):
    rows, cols = matrix.shape
    width = PANELS * TILE
    block = pl.BlockSpec((TILE, cols), lambda t: (t, 0))
    return pl.pallas_call(
        update_kernel,
        grid=(rows // TILE,),
        out_shape=jax.ShapeDtypeStruct(matrix.shape, F32),
        in_specs=[SMEM, block] + [ANY] * (HALVES * N_Y) + [VMEM] * 2 + [ANY] * (2 * PANELS),
        out_specs=block,
        scratch_shapes=[
            pltpu.VMEM((rows // TILE, TILE, width), BF16),
            pltpu.VMEM((HALVES, TILE, width), BF16),
            pltpu.VMEM((TILE, TILE), F32),
            pltpu.VMEM((TILE, TILE), F32),
            pltpu.SemaphoreType.DMA((rows // TILE,)),
            pltpu.SemaphoreType.DMA((2,)),
        ],
        name="update",
    )(idx, matrix, *row_parts, *col_parts, *factors, *inverses)


def on_device(matrix):
    row_index = lax.axis_index("row")
    col_index = lax.axis_index("col")
    y_index, z_index = col_index // N_Z, col_index % N_Z
    idx = jnp.stack([row_index, y_index, z_index, col_index]).astype(jnp.int32)
    barrier = lax.optimization_barrier

    sent = pack_top(idx, matrix)
    tiles = pack_y(matrix)
    slices = pick_row(idx, [sent[0]] + [row_shift(sent[s], s) for s in range(1, N_ROW)])
    copies = [slices]
    for g in range(N_Z // Z_GROUP):
        copies += [yz_shift(slices, s, g * Z_GROUP) for s in range(N_Y) if s or g]
    slices = lax.select_n(z_index // Z_GROUP * N_Y + y_index, *copies)
    slices, tiles = barrier((slices, tiles))
    top = pick_top(idx, [slices] + [z_group_shift(slices, s) for s in range(1, Z_GROUP)])
    over_x = [top] + [x_shift(top, s) for s in range(1, N_X)]
    over_x[1:], tiles = barrier((over_x[1:], tiles))
    top = join_x(idx, over_x)
    top_parts = [top, core_swap(top)]

    shifted = [y_shift(tiles[s], s) for s in range(1, N_Y)]
    l0, it0, lb0, t11, t21, t22 = factor0(idx, top_parts)
    tiles, shifted, t11 = barrier((tiles, shifted, t11))
    sent = pack_z(idx, tiles[0], shifted)
    sent, t11 = barrier((sent, t11))
    scattered = [sent[0]] + [z_shift(sent[s], s) for s in range(1, N_Z)]
    l1, it1, lb1, t22 = factor1(t11, t21, t22)
    l2, it2 = factor2(t22)
    solved = solve(idx, [it0, it1, it2], lb0, lb1, scattered)

    swapped = row_z_swap(solved)
    over_z = [solved] + [z_shift(solved, s) for s in range(1, N_Z) if s != N_Z // 2]
    over_z.insert(N_Z // 2, z_shift(over_z[N_Z // 2 - 1], 1))
    over_x = [swapped] + [x_shift(swapped, s) for s in range(1, N_X)]
    low, high = join_z(idx, over_z)
    low, high, over_x = barrier((low, high, over_x))
    col_half = join_x(idx, over_x)
    low_up, high_down = y_shift(low, 1), y_shift(high, N_Y - 1)
    high_up, low_down = y_shift(high, 1), y_shift(low, N_Y - 1)
    low_far, high_far = y_shift(low_up, 1), y_shift(high_down, N_Y - 1)
    row_parts = [low, high, low_up, high_up, low_far, high_far, low_down, high_down]
    col_parts = [col_half, core_swap(col_half)]
    return update(idx, matrix, row_parts, col_parts, [l0, l1, l2], [it0, it1, it2])


def solution(mesh):
    return jax.shard_map(
        on_device, mesh=mesh, in_specs=(P("row", "col"),), out_specs=P("row", "col"), check_vma=False
    )
```

```python
import jax
import jax.numpy as jnp
from jax import lax
from jax.experimental import pallas as pl
from jax.experimental.pallas import tpu as pltpu
from jax.sharding import PartitionSpec as P

TILE = 256
PANELS = 3
NB = 64
PIV = 8
N_ROW = 8
N_Y = 4
N_Z = 8
SUB = TILE // 8
HALVES = 2
F32 = jnp.float32
BF16 = jnp.bfloat16
HIGHEST = lax.Precision.HIGHEST
N_X = 4
Z_GROUP = 4


def dot_nn(a, b):
    return lax.dot_general(a, b, (((1,), (0,)), ((), ())), precision=HIGHEST, preferred_element_type=F32)


def dot_nt(a, b):
    return lax.dot_general(a, b, (((1,), (1,)), ((), ())), precision=HIGHEST, preferred_element_type=F32)


def dot_bf(a, b):
    return lax.dot_general(a, b, (((1,), (1,)), ((), ())), preferred_element_type=F32)


def y_shift(x, s):
    pairs = [(y * N_Z + z, (y + s) % N_Y * N_Z + z) for y in range(N_Y) for z in range(N_Z)]
    return lax.ppermute(x, "col", pairs)


def z_shift(x, s):
    pairs = [(y * N_Z + z, y * N_Z + (z + s) % N_Z) for y in range(N_Y) for z in range(N_Z)]
    return lax.ppermute(x, "col", pairs)


def row_shift(x, s):
    return lax.ppermute(x, "row", [(r, (r + s) % N_ROW) for r in range(N_ROW)])


def z_group_shift(x, s):
    pairs = [
        (y * N_Z + z, y * N_Z + z // Z_GROUP * Z_GROUP + (z % Z_GROUP + s) % Z_GROUP)
        for y in range(N_Y)
        for z in range(N_Z)
    ]
    return lax.ppermute(x, "col", pairs)


def x_shift(x, s):
    return lax.ppermute(x, "row", [(r, (r + 2 * s) % N_ROW) for r in range(N_ROW)])


def core_swap(x):
    return lax.ppermute(x, "row", [(r, r ^ 1) for r in range(N_ROW)])


def row_z_swap(x):
    n_col = N_Y * N_Z
    pairs = [
        (r * n_col + y * N_Z + z, z * n_col + y * N_Z + r)
        for r in range(N_ROW)
        for y in range(N_Y)
        for z in range(N_Z)
    ]
    return lax.ppermute(x, ("row", "col"), pairs)


SMEM = pl.BlockSpec(memory_space=pltpu.SMEM)
ANY = pl.BlockSpec(memory_space=pl.ANY)
VMEM = pl.BlockSpec(memory_space=pltpu.VMEM)


def pack_top_kernel(idx, tile, *outs):
    r = idx[0]
    for s in range(N_ROW):
        base = pl.multiple_of((r + s) % N_ROW * SUB, SUB)
        outs[s][...] = tile[pl.ds(base, SUB), :]


def pack_top(idx, matrix):
    return pl.pallas_call(
        pack_top_kernel,
        grid=(1,),
        out_shape=[jax.ShapeDtypeStruct((SUB, TILE), F32)] * N_ROW,
        in_specs=[SMEM, pl.BlockSpec((TILE, TILE), lambda i: (0, 0))],
        out_specs=[pl.BlockSpec((SUB, TILE), lambda i: (0, 0))] * N_ROW,
        name="pack_top",
    )(idx, matrix)


def pack_y_kernel(*refs):
    for s in range(N_Y):
        refs[N_Y + s][...] = refs[s][...]


def pack_y(matrix):
    return pl.pallas_call(
        pack_y_kernel,
        grid=(HALVES,),
        out_shape=[jax.ShapeDtypeStruct((HALVES, TILE, TILE), F32)] * N_Y,
        in_specs=[pl.BlockSpec((TILE, TILE), lambda h, s=s: (h * N_Y + s, 0)) for s in range(N_Y)],
        out_specs=[pl.BlockSpec((None, TILE, TILE), lambda h: (h, 0, 0))] * N_Y,
        name="pack_y",
    )(*[matrix] * N_Y)


def pack_z_kernel(idx, own, *rest):
    got, outs = rest[: N_Y - 1], rest[N_Y - 1 :]
    y, z = idx[1], idx[2]
    for source, ref in enumerate((own,) + tuple(got)):

        @pl.when(y == source)
        def _():
            for s in range(N_Z):
                base = pl.multiple_of((z + s) % N_Z * SUB, SUB)
                outs[s][...] = ref[:, pl.ds(base, SUB), :]


def pack_z(idx, own, got):
    return pl.pallas_call(
        pack_z_kernel,
        out_shape=[jax.ShapeDtypeStruct((HALVES, SUB, TILE), F32)] * N_Z,
        in_specs=[SMEM] + [VMEM] * N_Y,
        out_specs=[VMEM] * N_Z,
        name="pack_z",
    )(idx, own, *got)


def pick_row_kernel(idx, *rest):
    got, out = rest[:-1], rest[-1]
    first = idx[3] % PANELS
    for s, ref in enumerate(got):
        source = (idx[0] + N_ROW - s) % N_ROW
        for n in range(2):

            @pl.when(source == (first + n) % PANELS)
            def _():
                out[n] = ref[...]


def pick_row(idx, got):
    return pl.pallas_call(
        pick_row_kernel,
        out_shape=jax.ShapeDtypeStruct((2, SUB, TILE), F32),
        in_specs=[SMEM] + [VMEM] * N_ROW,
        out_specs=VMEM,
        name="pick_row",
    )(idx, *got)


def pick_top_kernel(idx, *rest):
    got, out = rest[:-1], rest[-1]
    for s, ref in enumerate(got):
        source = (idx[2] % Z_GROUP + Z_GROUP - s) % Z_GROUP

        @pl.when(source < PANELS)
        def _():
            out[source] = ref[...]


def pick_top(idx, got):
    return pl.pallas_call(
        pick_top_kernel,
        out_shape=jax.ShapeDtypeStruct((PANELS, 2, SUB, TILE), F32),
        in_specs=[SMEM] + [VMEM] * Z_GROUP,
        out_specs=VMEM,
        name="pick_top",
    )(idx, *got)


def eliminate(block):
    sub = lax.broadcasted_iota(jnp.int32, (8, 2 * NB), 0)
    lane = lax.broadcasted_iota(jnp.int32, (8, 2 * NB), 1)
    groups = NB // 8

    def spread(x):
        return jnp.broadcast_to(x, (8, 2 * NB))

    m = []
    for g in range(groups):
        eye = jnp.where(lane == sub + (8 * g + NB), F32(1), F32(0))
        m.append(jnp.concatenate([block[8 * g : 8 * g + 8], eye[:, NB:]], axis=1))
    scale = []
    for g0 in range(groups):
        j = g0 * PIV
        cols = [[spread(m[g][:, j + q : j + q + 1]) for g in range(g0, groups)] for q in range(PIV)]
        rows = [spread(m[g0][q : q + 1, :]) for q in range(PIV)]
        a = {}
        for q in range(PIV):
            for i in range(q, PIV):
                a[i, q] = spread(cols[q][0][i : i + 1, :])
        low = {}
        inv = []
        pivots = None
        for q in range(PIV):
            inv.append(1.0 / a[q, q])
            pivots = a[q, q] if pivots is None else jnp.where(sub >= q, a[q, q], pivots)
            for i in range(q + 1, PIV):
                low[i, q] = a[i, q] * inv[q]
            for jj in range(q + 1, PIV):
                for i in range(jj, PIV):
                    a[i, jj] = a[i, jj] - low[i, q] * a[jj, q]
        scale.append(lax.rsqrt(pivots))
        scaled = []
        for q in range(PIV):
            for i in range(q + 1, PIV):
                rows[i] = rows[i] - low[i, q] * rows[q]
            scaled.append(rows[q] * inv[q])
        for g in range(g0, groups):
            x = [cols[q][g - g0] for q in range(PIV)]
            updated = m[g]
            for q in range(PIV):
                for i in range(q + 1, PIV):
                    x[i] = x[i] - low[i, q] * x[q]
                part = x[q]
                if g == g0:
                    part = jnp.where(sub > q, part, F32(0))
                updated = updated - part * scaled[q]
            m[g] = updated
    return jnp.concatenate([m[g] * scale[g] for g in range(groups)], axis=0)


def factor_tile(tile, l_ref, it_ref, w):
    rows = lax.broadcasted_iota(jnp.int32, (TILE, TILE), 0)
    cols = lax.broadcasted_iota(jnp.int32, (TILE, TILE), 1)
    r64 = lax.broadcasted_iota(jnp.int32, (NB, NB), 0)
    c64 = lax.broadcasted_iota(jnp.int32, (NB, NB), 1)
    w[:TILE, :] = tile
    w[TILE:, :] = jnp.where(rows == cols, F32(1), F32(0))
    for lo in range(0, TILE, NB):
        hi = lo + NB
        below = TILE - hi
        m = eliminate(w[lo:hi, lo:hi]).T
        inv_t = jnp.where(r64 <= c64, m[NB:], F32(0))
        p = dot_nn(w[hi : TILE + hi, lo:hi], inv_t)
        l_ref[lo:hi, lo:hi] = jnp.where(r64 >= c64, m[:NB], F32(0))
        it_ref[:hi, lo:hi] = p[below:]
        if lo:
            l_ref[:lo, lo:hi] = jnp.zeros((lo, NB), F32)
        if below:
            l_ref[hi:, lo:hi] = p[:below]
            it_ref[hi:, lo:hi] = jnp.zeros((below, NB), F32)
            w[hi : TILE + hi, hi:] = w[hi : TILE + hi, hi:] - dot_nt(p, p[:below])
    return it_ref[...]


def factor0_kernel(idx, *rest):
    got = rest[:2]
    l_ref, it_ref, lb_ref, t11, t21, t22, top, w = rest[2:]
    core = idx[0] % 2
    for x in range(N_X):
        for other in range(2):
            base = pl.multiple_of((2 * x + (core + other) % 2) * SUB, SUB)
            top[:, :, pl.ds(base, SUB), :] = got[other][x]
    inv_t = factor_tile(top[0, 0], l_ref, it_ref, w)
    low1 = dot_nn(top[0, 1], inv_t).astype(BF16)
    low2 = dot_nn(top[2, 1].T, inv_t).astype(BF16)
    lb_ref[0] = low1
    lb_ref[1] = low2
    t11[...] = top[1, 0] - dot_bf(low1, low1)
    t21[...] = top[1, 1] - dot_bf(low2, low1)
    t22[...] = top[2, 0] - dot_bf(low2, low2)


def factor1_kernel(t11, t21, t22, l_ref, it_ref, lb_ref, rest_ref, w):
    inv_t = factor_tile(t11[...], l_ref, it_ref, w)
    low = dot_nn(t21[...], inv_t).astype(BF16)
    lb_ref[...] = low
    rest_ref[...] = t22[...] - dot_bf(low, low)


def factor2_kernel(t22, l_ref, it_ref, w):
    factor_tile(t22[...], l_ref, it_ref, w)


SQUARE = jax.ShapeDtypeStruct((TILE, TILE), F32)
FACTOR_COST = pl.CostEstimate(flops=15_000_000_000, transcendentals=0, bytes_accessed=2_000_000)
WORK = [pltpu.VMEM((2 * TILE, TILE), F32)]


def factor0(idx, got):
    return pl.pallas_call(
        factor0_kernel,
        out_shape=[SQUARE, SQUARE, jax.ShapeDtypeStruct((2, TILE, TILE), BF16), SQUARE, SQUARE, SQUARE],
        in_specs=[SMEM] + [VMEM] * 2,
        out_specs=[VMEM] * 6,
        scratch_shapes=[pltpu.VMEM((PANELS, 2, TILE, TILE), F32)] + WORK,
        cost_estimate=FACTOR_COST,
        name="factor0",
    )(idx, *got)


def factor1(t11, t21, t22):
    return pl.pallas_call(
        factor1_kernel,
        out_shape=[SQUARE, SQUARE, jax.ShapeDtypeStruct((TILE, TILE), BF16), SQUARE],
        in_specs=[VMEM] * 3,
        out_specs=[VMEM] * 4,
        scratch_shapes=WORK,
        cost_estimate=FACTOR_COST,
        name="factor1",
    )(t11, t21, t22)


def factor2(t22):
    return pl.pallas_call(
        factor2_kernel,
        out_shape=[SQUARE, SQUARE],
        in_specs=[VMEM],
        out_specs=[VMEM] * 2,
        scratch_shapes=WORK,
        cost_estimate=FACTOR_COST,
        name="factor2",
    )(t22)


def solve_kernel(idx, it0, it1, it2, lb0, lb1, *rest):
    got, out, rows = rest[:N_Z], rest[N_Z], rest[N_Z + 1]
    r, y, z = idx[0], idx[1], idx[2]
    for s in range(N_Z):
        source = (z + N_Z - s) % N_Z

        @pl.when(source < PANELS)
        def _():
            rows[source] = got[s][...]

    chunk = HALVES * SUB
    half = lax.broadcasted_iota(jnp.int32, (chunk, TILE), 0) // SUB
    tile_row = (half * N_Y + y) * N_ROW + r

    def keep(k, left, inverse):
        return jnp.where(tile_row > k, dot_nn(left, inverse[...]), F32(0)).astype(BF16)

    s0 = keep(0, rows[0].reshape(chunk, TILE), it0)
    s1 = keep(1, rows[1].reshape(chunk, TILE) - dot_bf(s0, lb0[0]), it1)
    s2 = keep(2, rows[2].reshape(chunk, TILE) - dot_bf(s0, lb0[1]) - dot_bf(s1, lb1[...]), it2)
    for k, done in enumerate((s0, s1, s2)):
        out[:, :, k * TILE : (k + 1) * TILE] = done.reshape(HALVES, SUB, TILE)


def solve(idx, inverses, lb0, lb1, got):
    return pl.pallas_call(
        solve_kernel,
        out_shape=jax.ShapeDtypeStruct((HALVES, SUB, PANELS * TILE), BF16),
        in_specs=[SMEM] + [VMEM] * (PANELS + 2 + N_Z),
        out_specs=VMEM,
        scratch_shapes=[pltpu.VMEM((PANELS, HALVES, SUB, TILE), F32)],
        name="solve",
    )(idx, *inverses, lb0, lb1, *got)


def join_z_kernel(idx, *rest):
    got, outs = rest[:N_Z], rest[N_Z:]
    for s in range(N_Z):
        base = pl.multiple_of((idx[2] + N_Z - s) % N_Z * SUB, SUB)
        for h in range(HALVES):
            outs[h][pl.ds(base, SUB), :] = got[s][h]


def join_z(idx, got):
    return pl.pallas_call(
        join_z_kernel,
        out_shape=[jax.ShapeDtypeStruct((TILE, PANELS * TILE), BF16)] * HALVES,
        in_specs=[SMEM] + [VMEM] * N_Z,
        out_specs=[VMEM] * HALVES,
        name="join_z",
    )(idx, *got)


def join_x_kernel(idx, *rest):
    got, out = rest[:-1], rest[-1]
    for s in range(N_X):
        out[(idx[0] // 2 + N_X - s) % N_X] = got[s][...]


def join_x(idx, got):
    return pl.pallas_call(
        join_x_kernel,
        out_shape=jax.ShapeDtypeStruct((N_X,) + got[0].shape, got[0].dtype),
        in_specs=[SMEM] + [VMEM] * N_X,
        out_specs=VMEM,
        name="join_x",
    )(idx, *got)


def join_cols_kernel(idx, own, other, out):
    core = idx[0] % 2
    for n, ref in enumerate((own, other)):
        for x in range(N_X):
            base = pl.multiple_of((2 * x + (core + n) % 2) * SUB, SUB)
            out[:, pl.ds(base, SUB), :] = ref[x]


def join_cols(idx, parts):
    return pl.pallas_call(
        join_cols_kernel,
        out_shape=jax.ShapeDtypeStruct((HALVES, TILE, PANELS * TILE), BF16),
        in_specs=[SMEM, VMEM, VMEM],
        out_specs=VMEM,
        name="join_cols",
    )(idx, *parts)


def part_tile(n, idx, shifts):
    shift = shifts[0] + (shifts[-1] - shifts[0]) * (n // HALVES)
    return n % HALVES * N_Y + (idx[1] + N_Y - shift) % N_Y


def update_kernel(shifts, idx, a_ref, c_all, *rest):
    count = HALVES * len(shifts)
    row_parts, rest = rest[:count], rest[count:]
    factors, inverses, rest = rest[:PANELS], rest[PANELS : 2 * PANELS], rest[2 * PANELS :]
    out, s_all, l_own, it_own, row_sem, own_sem = rest[-6:]
    r, c = idx[0], idx[3]
    n = pl.program_id(0)
    n_col = N_Y * N_Z

    def own_copies(k):
        return (
            pltpu.make_async_copy(factors[k], l_own, own_sem.at[0]),
            pltpu.make_async_copy(inverses[k], it_own, own_sem.at[1]),
        )

    @pl.when(n == 0)
    def _():
        for m in range(count):
            pltpu.make_async_copy(row_parts[m], s_all.at[m], row_sem.at[m]).start()
        for k in range(PANELS):

            @pl.when(c == k)
            def _():
                for copy in own_copies(k):
                    copy.start()
                for copy in own_copies(k):
                    copy.wait()

    pltpu.make_async_copy(row_parts[0], s_all.at[n], row_sem.at[n]).wait()
    i = part_tile(n, idx, shifts) * N_ROW + r
    for u in range(HALVES):
        lanes = slice(u * TILE, (u + 1) * TILE)
        j = c + u * n_col

        @pl.when(i >= j)
        def _():
            out[:, lanes] = a_ref[:, lanes] - dot_bf(s_all[n], c_all[u])

        @pl.when(i < j)
        def _():
            out[:, lanes] = a_ref[:, lanes]

    @pl.when(jnp.logical_and(c < PANELS, i > c))
    def _():
        out[:, :TILE] = dot_nn(out[:, :TILE], it_own[...])

    @pl.when(jnp.logical_and(c < PANELS, i == c))
    def _():
        out[:, :TILE] = l_own[...]


def update(idx, matrix, done, col_rows, row_parts, shifts, factors, inverses):
    count = HALVES * len(shifts)
    block = pl.BlockSpec((TILE, matrix.shape[1]), lambda n, idx: (part_tile(n, idx, shifts), 0))
    operands = [idx, matrix, col_rows, *row_parts, *factors, *inverses]
    in_specs = [block, VMEM] + [ANY] * (count + 2 * PANELS)
    aliases = {}
    if done is not None:
        aliases = {len(operands): 0}
        operands.append(done)
        in_specs.append(ANY)
    return pl.pallas_call(
        lambda *refs: update_kernel(shifts, *refs),
        grid_spec=pltpu.PrefetchScalarGridSpec(
            num_scalar_prefetch=1,
            grid=(count,),
            in_specs=in_specs,
            out_specs=block,
            scratch_shapes=[
                pltpu.VMEM((count, TILE, PANELS * TILE), BF16),
                pltpu.VMEM((TILE, TILE), F32),
                pltpu.VMEM((TILE, TILE), F32),
                pltpu.SemaphoreType.DMA((count,)),
                pltpu.SemaphoreType.DMA((2,)),
            ],
        ),
        out_shape=jax.ShapeDtypeStruct(matrix.shape, F32),
        input_output_aliases=aliases,
        name="update",
    )(*operands)


def on_device(matrix):
    row_index = lax.axis_index("row")
    col_index = lax.axis_index("col")
    y_index, z_index = col_index // N_Z, col_index % N_Z
    idx = jnp.stack([row_index, y_index, z_index, col_index]).astype(jnp.int32)
    barrier = lax.optimization_barrier

    sent = pack_top(idx, matrix)
    tiles = pack_y(matrix)
    slices = pick_row(idx, [sent[0]] + [row_shift(sent[s], s) for s in range(1, N_ROW)])
    slices = lax.select_n(y_index, slices, *[y_shift(slices, s) for s in range(1, N_Y)])
    slices, tiles = barrier((slices, tiles))
    slices = jnp.where(z_index < Z_GROUP, slices, z_shift(slices, Z_GROUP))
    top = pick_top(idx, [slices] + [z_group_shift(slices, s) for s in range(1, Z_GROUP)])
    top = join_x(idx, [top] + [x_shift(top, s) for s in range(1, N_X)])
    top_parts = [top, core_swap(top)]
    top_parts, tiles = barrier((top_parts, tiles))

    shifted = [y_shift(tiles[s], s) for s in range(1, N_Y)]
    l0, it0, lb0, t11, t21, t22 = factor0(idx, top_parts)
    l1, it1, lb1, t22 = factor1(t11, t21, t22)
    tiles, shifted, t22 = barrier((tiles, shifted, t22))
    sent = pack_z(idx, tiles[0], shifted)
    sent, t22 = barrier((sent, t22))
    l2, it2 = factor2(t22)
    scattered = [sent[0]] + [z_shift(sent[s], s) for s in range(1, N_Z)]
    solved = solve(idx, [it0, it1, it2], lb0, lb1, scattered)

    swapped = row_z_swap(solved)
    over_z = [solved] + [z_shift(solved, s) for s in range(1, N_Z) if s != N_Z // 2]
    over_z.insert(N_Z // 2, z_shift(over_z[N_Z // 2 - 1], 1))
    over_x = [swapped] + [x_shift(swapped, s) for s in range(1, N_X)]
    low, high = join_z(idx, over_z)
    col_half = join_x(idx, over_x)
    low, high, col_half = barrier((low, high, col_half))
    col_parts = [col_half, core_swap(col_half)]
    low_up, high_down = y_shift(low, 1), y_shift(high, N_Y - 1)
    high_up, low_down = y_shift(high, 1), y_shift(low, N_Y - 1)
    low_far, high_far = y_shift(low_up, 1), y_shift(high_down, N_Y - 1)

    own = ([l0, l1, l2], [it0, it1, it2])
    col_rows = join_cols(idx, col_parts)
    out = update(idx, matrix, None, col_rows, [low, high], (0,), *own)
    out = update(idx, matrix, out, col_rows, [low_up, high_up, low_down, high_down], (1, N_Y - 1), *own)
    return update(idx, matrix, out, col_rows, [low_far, high_far], (N_Y // 2,), *own)


def solution(mesh):
    return jax.shard_map(
        on_device, mesh=mesh, in_specs=(P("row", "col"),), out_specs=P("row", "col"), check_vma=False
    )
```

```python
import jax
import jax.numpy as jnp
from jax import lax
from jax.experimental import pallas as pl
from jax.experimental.pallas import tpu as pltpu
from jax.sharding import PartitionSpec as P

TILE = 256
PANELS = 3
NB = 64
PIV = 8
N_ROW = 8
N_Y = 4
N_Z = 8
SUB = TILE // 8
HALVES = 2
F32 = jnp.float32
BF16 = jnp.bfloat16
HIGHEST = lax.Precision.HIGHEST
N_X = 4
Z_GROUP = 4


def dot_nn(a, b):
    return lax.dot_general(a, b, (((1,), (0,)), ((), ())), precision=HIGHEST, preferred_element_type=F32)


def dot_nt(a, b):
    return lax.dot_general(a, b, (((1,), (1,)), ((), ())), precision=HIGHEST, preferred_element_type=F32)


def dot_bf(a, b):
    return lax.dot_general(a, b, (((1,), (1,)), ((), ())), preferred_element_type=F32)


def y_shift(x, s):
    pairs = [(y * N_Z + z, (y + s) % N_Y * N_Z + z) for y in range(N_Y) for z in range(N_Z)]
    return lax.ppermute(x, "col", pairs)


def z_shift(x, s):
    pairs = [(y * N_Z + z, y * N_Z + (z + s) % N_Z) for y in range(N_Y) for z in range(N_Z)]
    return lax.ppermute(x, "col", pairs)


def row_shift(x, s):
    return lax.ppermute(x, "row", [(r, (r + s) % N_ROW) for r in range(N_ROW)])


def z_group_shift(x, s):
    pairs = [
        (y * N_Z + z, y * N_Z + z // Z_GROUP * Z_GROUP + (z % Z_GROUP + s) % Z_GROUP)
        for y in range(N_Y)
        for z in range(N_Z)
    ]
    return lax.ppermute(x, "col", pairs)


def x_shift(x, s):
    return lax.ppermute(x, "row", [(r, (r + 2 * s) % N_ROW) for r in range(N_ROW)])


def core_swap(x):
    return lax.ppermute(x, "row", [(r, r ^ 1) for r in range(N_ROW)])


def row_z_swap(x):
    n_col = N_Y * N_Z
    pairs = [
        (r * n_col + y * N_Z + z, z * n_col + y * N_Z + r)
        for r in range(N_ROW)
        for y in range(N_Y)
        for z in range(N_Z)
    ]
    return lax.ppermute(x, ("row", "col"), pairs)


SMEM = pl.BlockSpec(memory_space=pltpu.SMEM)
ANY = pl.BlockSpec(memory_space=pl.ANY)
VMEM = pl.BlockSpec(memory_space=pltpu.VMEM)


def pack_top_kernel(idx, tile, *outs):
    r = idx[0]
    for s in range(N_ROW):
        base = pl.multiple_of((r + s) % N_ROW * SUB, SUB)
        outs[s][...] = tile[pl.ds(base, SUB), :]


def pack_top(idx, matrix):
    return pl.pallas_call(
        pack_top_kernel,
        grid=(1,),
        out_shape=[jax.ShapeDtypeStruct((SUB, TILE), F32)] * N_ROW,
        in_specs=[SMEM, pl.BlockSpec((TILE, TILE), lambda i: (0, 0))],
        out_specs=[pl.BlockSpec((SUB, TILE), lambda i: (0, 0))] * N_ROW,
        name="pack_top",
    )(idx, matrix)


def pack_y_kernel(*refs):
    for s in range(N_Y):
        refs[N_Y + s][...] = refs[s][...]


def pack_y(matrix):
    return pl.pallas_call(
        pack_y_kernel,
        grid=(HALVES,),
        out_shape=[jax.ShapeDtypeStruct((HALVES, TILE, TILE), F32)] * N_Y,
        in_specs=[pl.BlockSpec((TILE, TILE), lambda h, s=s: (h * N_Y + s, 0)) for s in range(N_Y)],
        out_specs=[pl.BlockSpec((None, TILE, TILE), lambda h: (h, 0, 0))] * N_Y,
        name="pack_y",
    )(*[matrix] * N_Y)


def pack_z_kernel(idx, own, *rest):
    got, outs = rest[: N_Y - 1], rest[N_Y - 1 :]
    y, z = idx[1], idx[2]
    for source, ref in enumerate((own,) + tuple(got)):

        @pl.when(y == source)
        def _():
            for s in range(N_Z):
                base = pl.multiple_of((z + s) % N_Z * SUB, SUB)
                outs[s][...] = ref[:, pl.ds(base, SUB), :]


def pack_z(idx, own, got):
    return pl.pallas_call(
        pack_z_kernel,
        out_shape=[jax.ShapeDtypeStruct((HALVES, SUB, TILE), F32)] * N_Z,
        in_specs=[SMEM] + [VMEM] * N_Y,
        out_specs=[VMEM] * N_Z,
        name="pack_z",
    )(idx, own, *got)


def pick_row_kernel(idx, *rest):
    got, out = rest[:-1], rest[-1]
    first = idx[3] % PANELS
    for s, ref in enumerate(got):
        source = (idx[0] + N_ROW - s) % N_ROW
        for n in range(2):

            @pl.when(source == (first + n) % PANELS)
            def _():
                out[n] = ref[...]


def pick_row(idx, got):
    return pl.pallas_call(
        pick_row_kernel,
        out_shape=jax.ShapeDtypeStruct((2, SUB, TILE), F32),
        in_specs=[SMEM] + [VMEM] * N_ROW,
        out_specs=VMEM,
        name="pick_row",
    )(idx, *got)


def pick_top_kernel(idx, *rest):
    got, out = rest[:-1], rest[-1]
    for s, ref in enumerate(got):
        source = (idx[2] % Z_GROUP + Z_GROUP - s) % Z_GROUP

        @pl.when(source < PANELS)
        def _():
            out[source] = ref[...]


def pick_top(idx, got):
    return pl.pallas_call(
        pick_top_kernel,
        out_shape=jax.ShapeDtypeStruct((PANELS, 2, SUB, TILE), F32),
        in_specs=[SMEM] + [VMEM] * Z_GROUP,
        out_specs=VMEM,
        name="pick_top",
    )(idx, *got)


def eliminate(block):
    sub = lax.broadcasted_iota(jnp.int32, (8, 2 * NB), 0)
    lane = lax.broadcasted_iota(jnp.int32, (8, 2 * NB), 1)
    groups = NB // 8

    def spread(x):
        return jnp.broadcast_to(x, (8, 2 * NB))

    m = []
    for g in range(groups):
        eye = jnp.where(lane == sub + (8 * g + NB), F32(1), F32(0))
        m.append(jnp.concatenate([block[8 * g : 8 * g + 8], eye[:, NB:]], axis=1))
    scale = []
    for g0 in range(groups):
        j = g0 * PIV
        cols = [[spread(m[g][:, j + q : j + q + 1]) for g in range(g0, groups)] for q in range(PIV)]
        rows = [spread(m[g0][q : q + 1, :]) for q in range(PIV)]
        a = {}
        for q in range(PIV):
            for i in range(q, PIV):
                a[i, q] = spread(cols[q][0][i : i + 1, :])
        low = {}
        inv = []
        pivots = None
        for q in range(PIV):
            inv.append(1.0 / a[q, q])
            pivots = a[q, q] if pivots is None else jnp.where(sub >= q, a[q, q], pivots)
            for i in range(q + 1, PIV):
                low[i, q] = a[i, q] * inv[q]
            for jj in range(q + 1, PIV):
                for i in range(jj, PIV):
                    a[i, jj] = a[i, jj] - low[i, q] * a[jj, q]
        scale.append(lax.rsqrt(pivots))
        scaled = []
        for q in range(PIV):
            for i in range(q + 1, PIV):
                rows[i] = rows[i] - low[i, q] * rows[q]
            scaled.append(rows[q] * inv[q])
        for g in range(g0, groups):
            x = [cols[q][g - g0] for q in range(PIV)]
            updated = m[g]
            for q in range(PIV):
                for i in range(q + 1, PIV):
                    x[i] = x[i] - low[i, q] * x[q]
                part = x[q]
                if g == g0:
                    part = jnp.where(sub > q, part, F32(0))
                updated = updated - part * scaled[q]
            m[g] = updated
    return jnp.concatenate([m[g] * scale[g] for g in range(groups)], axis=0)


def factor_tile(tile, l_ref, it_ref, w):
    rows = lax.broadcasted_iota(jnp.int32, (TILE, TILE), 0)
    cols = lax.broadcasted_iota(jnp.int32, (TILE, TILE), 1)
    r64 = lax.broadcasted_iota(jnp.int32, (NB, NB), 0)
    c64 = lax.broadcasted_iota(jnp.int32, (NB, NB), 1)
    w[:TILE, :] = tile
    w[TILE:, :] = jnp.where(rows == cols, F32(1), F32(0))
    for lo in range(0, TILE, NB):
        hi = lo + NB
        below = TILE - hi
        m = eliminate(w[lo:hi, lo:hi]).T
        inv_t = jnp.where(r64 <= c64, m[NB:], F32(0))
        p = dot_nn(w[hi : TILE + hi, lo:hi], inv_t)
        l_ref[lo:hi, lo:hi] = jnp.where(r64 >= c64, m[:NB], F32(0))
        it_ref[:hi, lo:hi] = p[below:]
        if lo:
            l_ref[:lo, lo:hi] = jnp.zeros((lo, NB), F32)
        if below:
            l_ref[hi:, lo:hi] = p[:below]
            it_ref[hi:, lo:hi] = jnp.zeros((below, NB), F32)
            w[hi : TILE + hi, hi:] = w[hi : TILE + hi, hi:] - dot_nt(p, p[:below])
    return it_ref[...]


def factor0_kernel(idx, *rest):
    got = rest[:2]
    l_ref, it_ref, lb_ref, t11, t21, t22, top, w = rest[2:]
    core = idx[0] % 2
    for x in range(N_X):
        for other in range(2):
            base = pl.multiple_of((2 * x + (core + other) % 2) * SUB, SUB)
            top[:, :, pl.ds(base, SUB), :] = got[other][x]
    inv_t = factor_tile(top[0, 0], l_ref, it_ref, w)
    low1 = dot_nn(top[0, 1], inv_t).astype(BF16)
    low2 = dot_nn(top[2, 1].T, inv_t).astype(BF16)
    lb_ref[0] = low1
    lb_ref[1] = low2
    t11[...] = top[1, 0] - dot_bf(low1, low1)
    t21[...] = top[1, 1] - dot_bf(low2, low1)
    t22[...] = top[2, 0] - dot_bf(low2, low2)


def factor1_kernel(t11, t21, t22, l_ref, it_ref, lb_ref, rest_ref, w):
    inv_t = factor_tile(t11[...], l_ref, it_ref, w)
    low = dot_nn(t21[...], inv_t).astype(BF16)
    lb_ref[...] = low
    rest_ref[...] = t22[...] - dot_bf(low, low)


def factor2_kernel(t22, l_ref, it_ref, w):
    factor_tile(t22[...], l_ref, it_ref, w)


SQUARE = jax.ShapeDtypeStruct((TILE, TILE), F32)
FACTOR_COST = pl.CostEstimate(flops=15_000_000_000, transcendentals=0, bytes_accessed=2_000_000)
WORK = [pltpu.VMEM((2 * TILE, TILE), F32)]


def factor0(idx, got):
    return pl.pallas_call(
        factor0_kernel,
        out_shape=[SQUARE, SQUARE, jax.ShapeDtypeStruct((2, TILE, TILE), BF16), SQUARE, SQUARE, SQUARE],
        in_specs=[SMEM] + [VMEM] * 2,
        out_specs=[VMEM] * 6,
        scratch_shapes=[pltpu.VMEM((PANELS, 2, TILE, TILE), F32)] + WORK,
        cost_estimate=FACTOR_COST,
        name="factor0",
    )(idx, *got)


def factor1(t11, t21, t22):
    return pl.pallas_call(
        factor1_kernel,
        out_shape=[SQUARE, SQUARE, jax.ShapeDtypeStruct((TILE, TILE), BF16), SQUARE],
        in_specs=[VMEM] * 3,
        out_specs=[VMEM] * 4,
        scratch_shapes=WORK,
        cost_estimate=FACTOR_COST,
        name="factor1",
    )(t11, t21, t22)


def factor2(t22):
    return pl.pallas_call(
        factor2_kernel,
        out_shape=[SQUARE, SQUARE],
        in_specs=[VMEM],
        out_specs=[VMEM] * 2,
        scratch_shapes=WORK,
        cost_estimate=FACTOR_COST,
        name="factor2",
    )(t22)


def solve_kernel(idx, it0, it1, it2, lb0, lb1, *rest):
    got, out, rows = rest[:N_Z], rest[N_Z], rest[N_Z + 1]
    r, y, z = idx[0], idx[1], idx[2]
    for s in range(N_Z):
        source = (z + N_Z - s) % N_Z

        @pl.when(source < PANELS)
        def _():
            rows[source] = got[s][...]

    chunk = HALVES * SUB
    half = lax.broadcasted_iota(jnp.int32, (chunk, TILE), 0) // SUB
    tile_row = (half * N_Y + y) * N_ROW + r

    def keep(k, left, inverse):
        return jnp.where(tile_row > k, dot_nn(left, inverse[...]), F32(0)).astype(BF16)

    s0 = keep(0, rows[0].reshape(chunk, TILE), it0)
    s1 = keep(1, rows[1].reshape(chunk, TILE) - dot_bf(s0, lb0[0]), it1)
    s2 = keep(2, rows[2].reshape(chunk, TILE) - dot_bf(s0, lb0[1]) - dot_bf(s1, lb1[...]), it2)
    for k, done in enumerate((s0, s1, s2)):
        out[:, :, k * TILE : (k + 1) * TILE] = done.reshape(HALVES, SUB, TILE)


def solve(idx, inverses, lb0, lb1, got):
    return pl.pallas_call(
        solve_kernel,
        out_shape=jax.ShapeDtypeStruct((HALVES, SUB, PANELS * TILE), BF16),
        in_specs=[SMEM] + [VMEM] * (PANELS + 2 + N_Z),
        out_specs=VMEM,
        scratch_shapes=[pltpu.VMEM((PANELS, HALVES, SUB, TILE), F32)],
        name="solve",
    )(idx, *inverses, lb0, lb1, *got)


def join_z_kernel(idx, *rest):
    got, outs = rest[:N_Z], rest[N_Z:]
    for s in range(N_Z):
        base = pl.multiple_of((idx[2] + N_Z - s) % N_Z * SUB, SUB)
        for h in range(HALVES):
            outs[h][pl.ds(base, SUB), :] = got[s][h]


def join_z(idx, got):
    return pl.pallas_call(
        join_z_kernel,
        out_shape=[jax.ShapeDtypeStruct((TILE, PANELS * TILE), BF16)] * HALVES,
        in_specs=[SMEM] + [VMEM] * N_Z,
        out_specs=[VMEM] * HALVES,
        name="join_z",
    )(idx, *got)


def join_x_kernel(idx, *rest):
    got, out = rest[:-1], rest[-1]
    for s in range(N_X):
        out[(idx[0] // 2 + N_X - s) % N_X] = got[s][...]


def join_x(idx, got):
    return pl.pallas_call(
        join_x_kernel,
        out_shape=jax.ShapeDtypeStruct((N_X,) + got[0].shape, got[0].dtype),
        in_specs=[SMEM] + [VMEM] * N_X,
        out_specs=VMEM,
        name="join_x",
    )(idx, *got)


def join_cols_kernel(idx, own, other, out):
    core = idx[0] % 2
    for n, ref in enumerate((own, other)):
        for x in range(N_X):
            base = pl.multiple_of((2 * x + (core + n) % 2) * SUB, SUB)
            out[:, pl.ds(base, SUB), :] = ref[x]


def join_cols(idx, parts):
    return pl.pallas_call(
        join_cols_kernel,
        out_shape=jax.ShapeDtypeStruct((HALVES, TILE, PANELS * TILE), BF16),
        in_specs=[SMEM, VMEM, VMEM],
        out_specs=VMEM,
        name="join_cols",
    )(idx, *parts)


def part_tile(n, idx, shifts):
    shift = shifts[0] + (shifts[-1] - shifts[0]) * (n // HALVES)
    return n % HALVES * N_Y + (idx[1] + N_Y - shift) % N_Y


def update_kernel(shifts, idx, a_ref, c_all, *rest):
    count = HALVES * len(shifts)
    row_parts, rest = rest[:count], rest[count:]
    factors, inverses, rest = rest[:PANELS], rest[PANELS : 2 * PANELS], rest[2 * PANELS :]
    out, s_all, l_own, it_own, row_sem, own_sem = rest[-6:]
    r, c = idx[0], idx[3]
    n = pl.program_id(0)
    n_col = N_Y * N_Z

    def own_copies(k):
        return (
            pltpu.make_async_copy(factors[k], l_own, own_sem.at[0]),
            pltpu.make_async_copy(inverses[k], it_own, own_sem.at[1]),
        )

    @pl.when(n == 0)
    def _():
        for m in range(count):
            pltpu.make_async_copy(row_parts[m], s_all.at[m], row_sem.at[m]).start()
        for k in range(PANELS):

            @pl.when(c == k)
            def _():
                for copy in own_copies(k):
                    copy.start()

    pltpu.make_async_copy(row_parts[0], s_all.at[n], row_sem.at[n]).wait()
    i = part_tile(n, idx, shifts) * N_ROW + r
    for u in range(HALVES):
        lanes = slice(u * TILE, (u + 1) * TILE)
        j = c + u * n_col

        @pl.when(i >= j)
        def _():
            out[:, lanes] = a_ref[:, lanes] - dot_bf(s_all[n], c_all[u])

        @pl.when(i < j)
        def _():
            out[:, lanes] = a_ref[:, lanes]

    @pl.when(jnp.logical_and(c < PANELS, n == 0))
    def _():
        for copy in own_copies(0):
            copy.wait()

    @pl.when(jnp.logical_and(c < PANELS, i > c))
    def _():
        out[:, :TILE] = dot_nn(out[:, :TILE], it_own[...])

    @pl.when(jnp.logical_and(c < PANELS, i == c))
    def _():
        out[:, :TILE] = l_own[...]


def update(idx, matrix, done, col_rows, row_parts, shifts, factors, inverses):
    count = HALVES * len(shifts)
    block = pl.BlockSpec((TILE, matrix.shape[1]), lambda n, idx: (part_tile(n, idx, shifts), 0))
    operands = [idx, matrix, col_rows, *row_parts, *factors, *inverses]
    in_specs = [block] + [VMEM] * (1 + count) + [ANY] * (2 * PANELS)
    aliases = {}
    if done is not None:
        aliases = {len(operands): 0}
        operands.append(done)
        in_specs.append(ANY)
    return pl.pallas_call(
        lambda *refs: update_kernel(shifts, *refs),
        grid_spec=pltpu.PrefetchScalarGridSpec(
            num_scalar_prefetch=1,
            grid=(count,),
            in_specs=in_specs,
            out_specs=block,
            scratch_shapes=[
                pltpu.VMEM((count, TILE, PANELS * TILE), BF16),
                pltpu.VMEM((TILE, TILE), F32),
                pltpu.VMEM((TILE, TILE), F32),
                pltpu.SemaphoreType.DMA((count,)),
                pltpu.SemaphoreType.DMA((2,)),
            ],
        ),
        out_shape=jax.ShapeDtypeStruct(matrix.shape, F32),
        input_output_aliases=aliases,
        name="update",
    )(*operands)


def on_device(matrix):
    row_index = lax.axis_index("row")
    col_index = lax.axis_index("col")
    y_index, z_index = col_index // N_Z, col_index % N_Z
    idx = jnp.stack([row_index, y_index, z_index, col_index]).astype(jnp.int32)
    barrier = lax.optimization_barrier

    sent = pack_top(idx, matrix)
    tiles = pack_y(matrix)
    slices = pick_row(idx, [sent[0]] + [row_shift(sent[s], s) for s in range(1, N_ROW)])
    slices = lax.select_n(y_index, slices, *[y_shift(slices, s) for s in range(1, N_Y)])
    slices, tiles = barrier((slices, tiles))
    slices = jnp.where(z_index < Z_GROUP, slices, z_shift(slices, Z_GROUP))
    top = pick_top(idx, [slices] + [z_group_shift(slices, s) for s in range(1, Z_GROUP)])
    top = join_x(idx, [top] + [x_shift(top, s) for s in range(1, N_X)])
    top_parts = [top, core_swap(top)]
    top_parts, tiles = barrier((top_parts, tiles))

    shifted = [y_shift(tiles[s], s) for s in range(1, N_Y)]
    l0, it0, lb0, t11, t21, t22 = factor0(idx, top_parts)
    l1, it1, lb1, t22 = factor1(t11, t21, t22)
    tiles, shifted, t22 = barrier((tiles, shifted, t22))
    sent = pack_z(idx, tiles[0], shifted)
    sent, t22 = barrier((sent, t22))
    l2, it2 = factor2(t22)
    early = [z_shift(sent[s], s) for s in range(2, N_Z - 1)]
    first, last, early, it2 = barrier((sent[1], sent[N_Z - 1], early, it2))
    scattered = [sent[0], z_shift(first, 1), *early, z_shift(last, N_Z - 1)]
    solved = solve(idx, [it0, it1, it2], lb0, lb1, scattered)

    swapped = row_z_swap(solved)
    over_z = [solved] + [z_shift(solved, s) for s in range(1, N_Z) if s != N_Z // 2]
    over_z.insert(N_Z // 2, z_shift(over_z[N_Z // 2 - 1], 1))
    over_x = [swapped] + [x_shift(swapped, s) for s in range(1, N_X)]
    low, high = join_z(idx, over_z)
    low, high, over_x = barrier((low, high, over_x))
    col_half = join_x(idx, over_x)
    col_parts = [col_half, core_swap(col_half)]
    low_up, high_down = y_shift(low, 1), y_shift(high, N_Y - 1)
    high_up, low_down = y_shift(high, 1), y_shift(low, N_Y - 1)
    low_far, high_far = y_shift(low_up, 1), y_shift(high_down, N_Y - 1)

    own = ([l0, l1, l2], [it0, it1, it2])
    col_rows = join_cols(idx, col_parts)
    out = update(idx, matrix, None, col_rows, [low, high], (0,), *own)
    out = update(idx, matrix, out, col_rows, [low_up, high_up, low_down, high_down], (1, N_Y - 1), *own)
    return update(idx, matrix, out, col_rows, [low_far, high_far], (N_Y // 2,), *own)


def solution(mesh):
    return jax.shard_map(
        on_device, mesh=mesh, in_specs=(P("row", "col"),), out_specs=P("row", "col"), check_vma=False
    )
```

```python
import jax
import jax.numpy as jnp
from jax import lax
from jax.experimental import pallas as pl
from jax.experimental.pallas import tpu as pltpu
from jax.sharding import PartitionSpec as P

TILE = 256
PANELS = 3
NB = 64
PIV = 8
N_ROW = 8
N_Y = 4
N_Z = 8
SUB = TILE // 8
HALVES = 2
F32 = jnp.float32
BF16 = jnp.bfloat16
HIGHEST = lax.Precision.HIGHEST
N_X = 4
Z_GROUP = 4


def dot_nn(a, b):
    return lax.dot_general(a, b, (((1,), (0,)), ((), ())), precision=HIGHEST, preferred_element_type=F32)


def dot_nt(a, b):
    return lax.dot_general(a, b, (((1,), (1,)), ((), ())), precision=HIGHEST, preferred_element_type=F32)


def dot_bf(a, b):
    return lax.dot_general(a, b, (((1,), (1,)), ((), ())), preferred_element_type=F32)


def y_shift(x, s):
    pairs = [(y * N_Z + z, (y + s) % N_Y * N_Z + z) for y in range(N_Y) for z in range(N_Z)]
    return lax.ppermute(x, "col", pairs)


def z_shift(x, s):
    pairs = [(y * N_Z + z, y * N_Z + (z + s) % N_Z) for y in range(N_Y) for z in range(N_Z)]
    return lax.ppermute(x, "col", pairs)


def row_shift(x, s):
    return lax.ppermute(x, "row", [(r, (r + s) % N_ROW) for r in range(N_ROW)])


def z_group_shift(x, s):
    pairs = [
        (y * N_Z + z, y * N_Z + z // Z_GROUP * Z_GROUP + (z % Z_GROUP + s) % Z_GROUP)
        for y in range(N_Y)
        for z in range(N_Z)
    ]
    return lax.ppermute(x, "col", pairs)


def x_shift(x, s):
    return lax.ppermute(x, "row", [(r, (r + 2 * s) % N_ROW) for r in range(N_ROW)])


def core_swap(x):
    return lax.ppermute(x, "row", [(r, r ^ 1) for r in range(N_ROW)])


def row_z_swap(x):
    n_col = N_Y * N_Z
    pairs = [
        (r * n_col + y * N_Z + z, z * n_col + y * N_Z + r)
        for r in range(N_ROW)
        for y in range(N_Y)
        for z in range(N_Z)
    ]
    return lax.ppermute(x, ("row", "col"), pairs)


SMEM = pl.BlockSpec(memory_space=pltpu.SMEM)
ANY = pl.BlockSpec(memory_space=pl.ANY)
VMEM = pl.BlockSpec(memory_space=pltpu.VMEM)
PARAMS = pltpu.CompilerParams(vmem_limit_bytes=16 * 2**20)


def pack_top_kernel(idx, tile, *outs):
    r = idx[0]
    for s in range(N_ROW):
        base = pl.multiple_of((r + s) % N_ROW * SUB, SUB)
        outs[s][...] = tile[pl.ds(base, SUB), :]


def pack_top(idx, matrix):
    return pl.pallas_call(
        pack_top_kernel,
        grid=(1,),
        out_shape=[jax.ShapeDtypeStruct((SUB, TILE), F32)] * N_ROW,
        in_specs=[SMEM, pl.BlockSpec((TILE, TILE), lambda i: (0, 0))],
        out_specs=[pl.BlockSpec((SUB, TILE), lambda i: (0, 0))] * N_ROW,
        compiler_params=PARAMS,
        name="pack_top",
    )(idx, matrix)


def pack_y_kernel(*refs):
    for s in range(N_Y):
        refs[N_Y + s][...] = refs[s][...]


def pack_y(matrix):
    return pl.pallas_call(
        pack_y_kernel,
        grid=(HALVES,),
        out_shape=[jax.ShapeDtypeStruct((HALVES, TILE, TILE), F32)] * N_Y,
        in_specs=[pl.BlockSpec((TILE, TILE), lambda h, s=s: (h * N_Y + s, 0)) for s in range(N_Y)],
        out_specs=[pl.BlockSpec((None, TILE, TILE), lambda h: (h, 0, 0))] * N_Y,
        compiler_params=PARAMS,
        name="pack_y",
    )(*[matrix] * N_Y)


def pack_z_kernel(idx, own, *rest):
    got, outs = rest[: N_Y - 1], rest[N_Y - 1 :]
    y, z = idx[1], idx[2]
    for source, ref in enumerate((own,) + tuple(got)):

        @pl.when(y == source)
        def _():
            for s in range(N_Z):
                base = pl.multiple_of((z + s) % N_Z * SUB, SUB)
                outs[s][...] = ref[:, pl.ds(base, SUB), :]


def pack_z(idx, own, got):
    return pl.pallas_call(
        pack_z_kernel,
        out_shape=[jax.ShapeDtypeStruct((HALVES, SUB, TILE), F32)] * N_Z,
        in_specs=[SMEM] + [VMEM] * N_Y,
        out_specs=[VMEM] * N_Z,
        compiler_params=PARAMS,
        name="pack_z",
    )(idx, own, *got)


def pick_row_kernel(idx, *rest):
    got, out = rest[:-1], rest[-1]
    first = idx[3] % PANELS
    for s, ref in enumerate(got):
        source = (idx[0] + N_ROW - s) % N_ROW
        for n in range(2):

            @pl.when(source == (first + n) % PANELS)
            def _():
                out[n] = ref[...]


def pick_row(idx, got):
    return pl.pallas_call(
        pick_row_kernel,
        out_shape=jax.ShapeDtypeStruct((2, SUB, TILE), F32),
        in_specs=[SMEM] + [VMEM] * N_ROW,
        out_specs=VMEM,
        compiler_params=PARAMS,
        name="pick_row",
    )(idx, *got)


def pick_top_kernel(idx, *rest):
    got, out = rest[:-1], rest[-1]
    for s, ref in enumerate(got):
        source = (idx[2] % Z_GROUP + Z_GROUP - s) % Z_GROUP

        @pl.when(source < PANELS)
        def _():
            out[source] = ref[...]


def pick_top(idx, got):
    return pl.pallas_call(
        pick_top_kernel,
        out_shape=jax.ShapeDtypeStruct((PANELS, 2, SUB, TILE), F32),
        in_specs=[SMEM] + [VMEM] * Z_GROUP,
        out_specs=VMEM,
        compiler_params=PARAMS,
        name="pick_top",
    )(idx, *got)


def eliminate(block):
    sub = lax.broadcasted_iota(jnp.int32, (8, 2 * NB), 0)
    lane = lax.broadcasted_iota(jnp.int32, (8, 2 * NB), 1)
    groups = NB // 8

    def spread(x):
        return jnp.broadcast_to(x, (8, 2 * NB))

    m = []
    for g in range(groups):
        eye = jnp.where(lane == sub + (8 * g + NB), F32(1), F32(0))
        m.append(jnp.concatenate([block[8 * g : 8 * g + 8], eye[:, NB:]], axis=1))
    scale = []
    for g0 in range(groups):
        j = g0 * PIV
        cols = [[spread(m[g][:, j + q : j + q + 1]) for g in range(g0, groups)] for q in range(PIV)]
        rows = [spread(m[g0][q : q + 1, :]) for q in range(PIV)]
        a = {}
        for q in range(PIV):
            for i in range(q, PIV):
                a[i, q] = spread(cols[q][0][i : i + 1, :])
        low = {}
        inv = []
        pivots = None
        for q in range(PIV):
            inv.append(1.0 / a[q, q])
            pivots = a[q, q] if pivots is None else jnp.where(sub >= q, a[q, q], pivots)
            for i in range(q + 1, PIV):
                low[i, q] = a[i, q] * inv[q]
            for jj in range(q + 1, PIV):
                for i in range(jj, PIV):
                    a[i, jj] = a[i, jj] - low[i, q] * a[jj, q]
        scale.append(lax.rsqrt(pivots))
        scaled = []
        for q in range(PIV):
            for i in range(q + 1, PIV):
                rows[i] = rows[i] - low[i, q] * rows[q]
            scaled.append(rows[q] * inv[q])
        for g in range(g0, groups):
            x = [cols[q][g - g0] for q in range(PIV)]
            updated = m[g]
            for q in range(PIV):
                for i in range(q + 1, PIV):
                    x[i] = x[i] - low[i, q] * x[q]
                part = x[q]
                if g == g0:
                    part = jnp.where(sub > q, part, F32(0))
                updated = updated - part * scaled[q]
            m[g] = updated
    return jnp.concatenate([m[g] * scale[g] for g in range(groups)], axis=0)


def chol_inv(w, lc):
    blocks = TILE // NB
    rows = lax.broadcasted_iota(jnp.int32, (2 * TILE, NB), 0)
    r64 = lax.broadcasted_iota(jnp.int32, (NB, NB), 0)
    c64 = lax.broadcasted_iota(jnp.int32, (NB, NB), 1)

    def step(b, carry):
        base = pl.multiple_of(b * NB, NB)
        m = eliminate(w[b, pl.ds(base, NB), :]).T
        lower = jnp.where(r64 >= c64, m[:NB], F32(0))
        inv_t = jnp.where(r64 <= c64, m[NB:], F32(0))
        p = jnp.where(rows >= base + NB, dot_nn(w[b], inv_t), F32(0))
        lc[b] = p
        lc[b, pl.ds(base, NB), :] = lower
        for bj in range(1, blocks):

            @pl.when(bj > b)
            def _():
                w[bj] = w[bj] - dot_nt(p, p[bj * NB : (bj + 1) * NB])

        return carry

    lax.fori_loop(0, blocks, step, 0)


def factor_tile(tile, l_ref, it_ref, w, lc):
    blocks = TILE // NB
    r = lax.broadcasted_iota(jnp.int32, (TILE, NB), 0)
    c = lax.broadcasted_iota(jnp.int32, (TILE, NB), 1)
    for b in range(blocks):
        w[b, :TILE, :] = tile[:, b * NB : (b + 1) * NB]
        w[b, TILE:, :] = jnp.where(r == c + b * NB, F32(1), F32(0))
    chol_inv(w, lc)
    l_ref[...] = jnp.concatenate([lc[b, :TILE, :] for b in range(blocks)], axis=1)
    inv_t = jnp.concatenate([lc[b, TILE:, :] for b in range(blocks)], axis=1)
    it_ref[...] = inv_t
    return inv_t


def factor0_kernel(idx, *rest):
    got = rest[:2]
    l_ref, it_ref, lb_ref, t11, t21, t22, top, w, lc = rest[2:]
    core = idx[0] % 2
    for x in range(N_X):
        for other in range(2):
            base = pl.multiple_of((2 * x + (core + other) % 2) * SUB, SUB)
            top[:, :, pl.ds(base, SUB), :] = got[other][x]
    inv_t = factor_tile(top[0, 0], l_ref, it_ref, w, lc)
    low1 = dot_nn(top[0, 1], inv_t).astype(BF16)
    low2 = dot_nn(top[2, 1].T, inv_t).astype(BF16)
    lb_ref[0] = low1
    lb_ref[1] = low2
    t11[...] = top[1, 0] - dot_bf(low1, low1)
    t21[...] = top[1, 1] - dot_bf(low2, low1)
    t22[...] = top[2, 0] - dot_bf(low2, low2)


def factor1_kernel(t11, t21, t22, l_ref, it_ref, lb_ref, rest_ref, w, lc):
    inv_t = factor_tile(t11[...], l_ref, it_ref, w, lc)
    low = dot_nn(t21[...], inv_t).astype(BF16)
    lb_ref[...] = low
    rest_ref[...] = t22[...] - dot_bf(low, low)


def factor2_kernel(t22, l_ref, it_ref, w, lc):
    factor_tile(t22[...], l_ref, it_ref, w, lc)


SQUARE = jax.ShapeDtypeStruct((TILE, TILE), F32)
FACTOR_COST = pl.CostEstimate(flops=15_000_000_000, transcendentals=0, bytes_accessed=2_000_000)
WORK = [pltpu.VMEM((TILE // NB, 2 * TILE, NB), F32)] * 2


def factor0(idx, got):
    return pl.pallas_call(
        factor0_kernel,
        out_shape=[SQUARE, SQUARE, jax.ShapeDtypeStruct((2, TILE, TILE), BF16), SQUARE, SQUARE, SQUARE],
        in_specs=[SMEM] + [VMEM] * 2,
        out_specs=[VMEM] * 6,
        scratch_shapes=[pltpu.VMEM((PANELS, 2, TILE, TILE), F32)] + WORK,
        cost_estimate=FACTOR_COST,
        compiler_params=PARAMS,
        name="factor0",
    )(idx, *got)


def factor1(t11, t21, t22):
    return pl.pallas_call(
        factor1_kernel,
        out_shape=[SQUARE, SQUARE, jax.ShapeDtypeStruct((TILE, TILE), BF16), SQUARE],
        in_specs=[VMEM] * 3,
        out_specs=[VMEM] * 4,
        scratch_shapes=WORK,
        cost_estimate=FACTOR_COST,
        compiler_params=PARAMS,
        name="factor1",
    )(t11, t21, t22)


def factor2(t22):
    return pl.pallas_call(
        factor2_kernel,
        out_shape=[SQUARE, SQUARE],
        in_specs=[VMEM],
        out_specs=[VMEM] * 2,
        scratch_shapes=WORK,
        cost_estimate=FACTOR_COST,
        compiler_params=PARAMS,
        name="factor2",
    )(t22)


def solve_kernel(idx, it0, it1, it2, lb0, lb1, *rest):
    got, out, rows = rest[:N_Z], rest[N_Z], rest[N_Z + 1]
    r, y, z = idx[0], idx[1], idx[2]
    for s in range(N_Z):
        source = (z + N_Z - s) % N_Z

        @pl.when(source < PANELS)
        def _():
            rows[source] = got[s][...]

    chunk = HALVES * SUB
    half = lax.broadcasted_iota(jnp.int32, (chunk, TILE), 0) // SUB
    tile_row = (half * N_Y + y) * N_ROW + r

    def keep(k, left, inverse):
        return jnp.where(tile_row > k, dot_nn(left, inverse[...]), F32(0)).astype(BF16)

    s0 = keep(0, rows[0].reshape(chunk, TILE), it0)
    s1 = keep(1, rows[1].reshape(chunk, TILE) - dot_bf(s0, lb0[0]), it1)
    s2 = keep(2, rows[2].reshape(chunk, TILE) - dot_bf(s0, lb0[1]) - dot_bf(s1, lb1[...]), it2)
    for k, done in enumerate((s0, s1, s2)):
        out[:, :, k * TILE : (k + 1) * TILE] = done.reshape(HALVES, SUB, TILE)


def solve(idx, inverses, lb0, lb1, got):
    return pl.pallas_call(
        solve_kernel,
        out_shape=jax.ShapeDtypeStruct((HALVES, SUB, PANELS * TILE), BF16),
        in_specs=[SMEM] + [VMEM] * (PANELS + 2 + N_Z),
        out_specs=VMEM,
        scratch_shapes=[pltpu.VMEM((PANELS, HALVES, SUB, TILE), F32)],
        compiler_params=PARAMS,
        name="solve",
    )(idx, *inverses, lb0, lb1, *got)


def join_z_kernel(idx, *rest):
    got, outs = rest[:N_Z], rest[N_Z:]
    for s in range(N_Z):
        base = pl.multiple_of((idx[2] + N_Z - s) % N_Z * SUB, SUB)
        for h in range(HALVES):
            outs[h][pl.ds(base, SUB), :] = got[s][h]


def join_z(idx, got):
    return pl.pallas_call(
        join_z_kernel,
        out_shape=[jax.ShapeDtypeStruct((TILE, PANELS * TILE), BF16)] * HALVES,
        in_specs=[SMEM] + [VMEM] * N_Z,
        out_specs=[VMEM] * HALVES,
        compiler_params=PARAMS,
        name="join_z",
    )(idx, *got)


def join_x_kernel(idx, *rest):
    got, out = rest[:-1], rest[-1]
    for s in range(N_X):
        out[(idx[0] // 2 + N_X - s) % N_X] = got[s][...]


def join_x(idx, got):
    return pl.pallas_call(
        join_x_kernel,
        out_shape=jax.ShapeDtypeStruct((N_X,) + got[0].shape, got[0].dtype),
        in_specs=[SMEM] + [VMEM] * N_X,
        out_specs=VMEM,
        compiler_params=PARAMS,
        name="join_x",
    )(idx, *got)


def update_kernel(idx, a_ref, *rest):
    row_parts = [rest[HALVES * s : HALVES * (s + 1)] for s in range(N_Y)]
    rest = rest[HALVES * N_Y :]
    col_parts, factors, inverses = rest[:2], rest[2 : 2 + PANELS], rest[2 + PANELS : 2 + 2 * PANELS]
    out, s_all, c_all, l_own, it_own, row_sem, own_sem = rest[2 + 2 * PANELS :]
    r, y, c = idx[0], idx[1], idx[3]
    core = r % 2
    t = pl.program_id(0)
    n_col = N_Y * N_Z

    def row_copy(s, h):
        slot = h * N_Y + (y + N_Y - s) % N_Y
        return pltpu.make_async_copy(row_parts[s][h], s_all.at[slot], row_sem.at[slot])

    def own_copies(k):
        return (
            pltpu.make_async_copy(factors[k], l_own, own_sem.at[0]),
            pltpu.make_async_copy(inverses[k], it_own, own_sem.at[1]),
        )

    @pl.when(t == 0)
    def _():
        for h in range(HALVES):
            for s in range(N_Y):
                row_copy(s, h).start()
        for k in range(PANELS):

            @pl.when(c == k)
            def _():
                for copy in own_copies(k):
                    copy.start()
                for copy in own_copies(k):
                    copy.wait()

        for other in range(2):
            for slot in range(N_X):
                base = pl.multiple_of((2 * slot + (core + other) % 2) * SUB, SUB)
                c_all[:, pl.ds(base, SUB), :] = col_parts[other][slot]

    pltpu.make_async_copy(row_parts[0][0], s_all.at[t], row_sem.at[t]).wait()
    i = t * N_ROW + r
    for u in range(HALVES):
        lanes = slice(u * TILE, (u + 1) * TILE)
        j = c + u * n_col

        @pl.when(i >= j)
        def _():
            out[:, lanes] = a_ref[:, lanes] - dot_bf(s_all[t], c_all[u])

        @pl.when(i < j)
        def _():
            out[:, lanes] = a_ref[:, lanes]

    @pl.when(jnp.logical_and(c < PANELS, i > c))
    def _():
        out[:, :TILE] = dot_nn(out[:, :TILE], it_own[...])

    @pl.when(jnp.logical_and(c < PANELS, i == c))
    def _():
        out[:, :TILE] = l_own[...]


def update(idx, matrix, row_parts, col_parts, factors, inverses):
    rows, cols = matrix.shape
    width = PANELS * TILE
    block = pl.BlockSpec((TILE, cols), lambda t: (t, 0))
    return pl.pallas_call(
        update_kernel,
        grid=(rows // TILE,),
        out_shape=jax.ShapeDtypeStruct(matrix.shape, F32),
        in_specs=[SMEM, block] + [ANY] * (HALVES * N_Y) + [VMEM] * 2 + [ANY] * (2 * PANELS),
        out_specs=block,
        scratch_shapes=[
            pltpu.VMEM((rows // TILE, TILE, width), BF16),
            pltpu.VMEM((HALVES, TILE, width), BF16),
            pltpu.VMEM((TILE, TILE), F32),
            pltpu.VMEM((TILE, TILE), F32),
            pltpu.SemaphoreType.DMA((rows // TILE,)),
            pltpu.SemaphoreType.DMA((2,)),
        ],
        compiler_params=PARAMS,
        name="update",
    )(idx, matrix, *row_parts, *col_parts, *factors, *inverses)


def on_device(matrix):
    row_index = lax.axis_index("row")
    col_index = lax.axis_index("col")
    y_index, z_index = col_index // N_Z, col_index % N_Z
    idx = jnp.stack([row_index, y_index, z_index, col_index]).astype(jnp.int32)
    barrier = lax.optimization_barrier

    sent = pack_top(idx, matrix)
    tiles = pack_y(matrix)
    slices = pick_row(idx, [sent[0]] + [row_shift(sent[s], s) for s in range(1, N_ROW)])
    slices = lax.select_n(y_index, slices, *[y_shift(slices, s) for s in range(1, N_Y)])
    slices, tiles = barrier((slices, tiles))
    slices = jnp.where(z_index < Z_GROUP, slices, z_shift(slices, Z_GROUP))
    top = pick_top(idx, [slices] + [z_group_shift(slices, s) for s in range(1, Z_GROUP)])
    top = join_x(idx, [top] + [x_shift(top, s) for s in range(1, N_X)])
    top_parts = [top, core_swap(top)]
    top_parts, tiles = barrier((top_parts, tiles))

    shifted = [y_shift(tiles[s], s) for s in range(1, N_Y)]
    l0, it0, lb0, t11, t21, t22 = factor0(idx, top_parts)
    l1, it1, lb1, t22 = factor1(t11, t21, t22)
    tiles, shifted, t22 = barrier((tiles, shifted, t22))
    sent = pack_z(idx, tiles[0], shifted)
    sent, t22 = barrier((sent, t22))
    scattered = [sent[0]] + [z_shift(sent[s], s) for s in range(1, N_Z)]
    l2, it2 = factor2(t22)
    solved = solve(idx, [it0, it1, it2], lb0, lb1, scattered)

    swapped = row_z_swap(solved)
    over_z = [solved] + [z_shift(solved, s) for s in range(1, N_Z) if s != N_Z // 2]
    over_z.insert(N_Z // 2, z_shift(over_z[N_Z // 2 - 1], 1))
    over_x = [swapped] + [x_shift(swapped, s) for s in range(1, N_X)]
    low, high = join_z(idx, over_z)
    low, high, over_x = barrier((low, high, over_x))
    col_half = join_x(idx, over_x)
    low_up, high_down = y_shift(low, 1), y_shift(high, N_Y - 1)
    high_up, low_down = y_shift(high, 1), y_shift(low, N_Y - 1)
    low_far, high_far = y_shift(low_up, 1), y_shift(high_down, N_Y - 1)
    row_parts = [low, high, low_up, high_up, low_far, high_far, low_down, high_down]
    col_parts = [col_half, core_swap(col_half)]
    return update(idx, matrix, row_parts, col_parts, [l0, l1, l2], [it0, it1, it2])


def solution(mesh):
    return jax.shard_map(
        on_device, mesh=mesh, in_specs=(P("row", "col"),), out_specs=P("row", "col"), check_vma=False
    )
```

```python
import jax
import jax.numpy as jnp
from jax import lax
from jax.experimental import pallas as pl
from jax.experimental.pallas import tpu as pltpu
from jax.sharding import PartitionSpec as P

TILE = 256
PANELS = 3
NB = 64
PIV = 8
N_ROW = 8
N_Y = 4
N_Z = 8
SUB = TILE // 8
HALVES = 2
F32 = jnp.float32
BF16 = jnp.bfloat16
HIGHEST = lax.Precision.HIGHEST
N_X = 4
Z_GROUP = 4


def dot_nn(a, b):
    return lax.dot_general(a, b, (((1,), (0,)), ((), ())), precision=HIGHEST, preferred_element_type=F32)


def dot_nt(a, b):
    return lax.dot_general(a, b, (((1,), (1,)), ((), ())), precision=HIGHEST, preferred_element_type=F32)


def dot_bf(a, b):
    return lax.dot_general(a, b, (((1,), (1,)), ((), ())), preferred_element_type=F32)


def y_shift(x, s):
    pairs = [(y * N_Z + z, (y + s) % N_Y * N_Z + z) for y in range(N_Y) for z in range(N_Z)]
    return lax.ppermute(x, "col", pairs)


def z_shift(x, s):
    pairs = [(y * N_Z + z, y * N_Z + (z + s) % N_Z) for y in range(N_Y) for z in range(N_Z)]
    return lax.ppermute(x, "col", pairs)


def row_shift(x, s):
    return lax.ppermute(x, "row", [(r, (r + s) % N_ROW) for r in range(N_ROW)])


def z_group_shift(x, s):
    pairs = [
        (y * N_Z + z, y * N_Z + z // Z_GROUP * Z_GROUP + (z % Z_GROUP + s) % Z_GROUP)
        for y in range(N_Y)
        for z in range(N_Z)
    ]
    return lax.ppermute(x, "col", pairs)


def x_shift(x, s):
    return lax.ppermute(x, "row", [(r, (r + 2 * s) % N_ROW) for r in range(N_ROW)])


def core_swap(x):
    return lax.ppermute(x, "row", [(r, r ^ 1) for r in range(N_ROW)])


def row_z_swap(x):
    n_col = N_Y * N_Z
    pairs = [
        (r * n_col + y * N_Z + z, z * n_col + y * N_Z + r)
        for r in range(N_ROW)
        for y in range(N_Y)
        for z in range(N_Z)
    ]
    return lax.ppermute(x, ("row", "col"), pairs)


SMEM = pl.BlockSpec(memory_space=pltpu.SMEM)
ANY = pl.BlockSpec(memory_space=pl.ANY)
VMEM = pl.BlockSpec(memory_space=pltpu.VMEM)
PARAMS = pltpu.CompilerParams(vmem_limit_bytes=16 * 2**20)


def pack_top_kernel(idx, matrix, *rest):
    outs, sem = rest[:N_ROW], rest[N_ROW]
    copies = []
    for s in range(N_ROW):
        base = pl.multiple_of((idx[0] + s) % N_ROW * SUB, SUB)
        source = matrix.at[pl.ds(base, SUB), pl.ds(0, TILE)]
        copies.append(pltpu.make_async_copy(source, outs[s], sem.at[s]))
    for copy in copies:
        copy.start()
    for copy in copies:
        copy.wait()


def pack_top(idx, matrix):
    return pl.pallas_call(
        pack_top_kernel,
        out_shape=[jax.ShapeDtypeStruct((SUB, TILE), F32)] * N_ROW,
        in_specs=[SMEM, pl.BlockSpec(memory_space=pltpu.HBM)],
        out_specs=[VMEM] * N_ROW,
        scratch_shapes=[pltpu.SemaphoreType.DMA((N_ROW,))],
        compiler_params=PARAMS,
        name="pack_top",
    )(idx, matrix)


def pack_y_kernel(*refs):
    for s in range(N_Y):
        refs[N_Y + s][...] = refs[s][...]


def pack_y(matrix):
    return pl.pallas_call(
        pack_y_kernel,
        grid=(HALVES,),
        out_shape=[jax.ShapeDtypeStruct((HALVES, TILE, TILE), F32)] * N_Y,
        in_specs=[pl.BlockSpec((TILE, TILE), lambda h, s=s: (h * N_Y + s, 0)) for s in range(N_Y)],
        out_specs=[pl.BlockSpec((None, TILE, TILE), lambda h: (h, 0, 0))] * N_Y,
        compiler_params=PARAMS,
        name="pack_y",
    )(*[matrix] * N_Y)


def pack_z_kernel(idx, own, *rest):
    got, outs = rest[: N_Y - 1], rest[N_Y - 1 :]
    y, z = idx[1], idx[2]
    for source, ref in enumerate((own,) + tuple(got)):

        @pl.when(y == source)
        def _():
            for s in range(N_Z):
                base = pl.multiple_of((z + s) % N_Z * SUB, SUB)
                outs[s][...] = ref[:, pl.ds(base, SUB), :]


def pack_z(idx, own, got):
    return pl.pallas_call(
        pack_z_kernel,
        out_shape=[jax.ShapeDtypeStruct((HALVES, SUB, TILE), F32)] * N_Z,
        in_specs=[SMEM] + [VMEM] * N_Y,
        out_specs=[VMEM] * N_Z,
        compiler_params=PARAMS,
        name="pack_z",
    )(idx, own, *got)


def pick_row_kernel(idx, *rest):
    got, out = rest[:-1], rest[-1]
    first = idx[3] % PANELS
    for s, ref in enumerate(got):
        source = (idx[0] + N_ROW - s) % N_ROW
        for n in range(2):

            @pl.when(source == (first + n) % PANELS)
            def _():
                out[n] = ref[...]


def pick_row(idx, got):
    return pl.pallas_call(
        pick_row_kernel,
        out_shape=jax.ShapeDtypeStruct((2, SUB, TILE), F32),
        in_specs=[SMEM] + [VMEM] * N_ROW,
        out_specs=VMEM,
        compiler_params=PARAMS,
        name="pick_row",
    )(idx, *got)


def pick_top_kernel(idx, *rest):
    got, out = rest[:-1], rest[-1]
    for s, ref in enumerate(got):
        source = (idx[2] % Z_GROUP + Z_GROUP - s) % Z_GROUP

        @pl.when(source < PANELS)
        def _():
            out[source] = ref[...]


def pick_top(idx, got):
    return pl.pallas_call(
        pick_top_kernel,
        out_shape=jax.ShapeDtypeStruct((PANELS, 2, SUB, TILE), F32),
        in_specs=[SMEM] + [VMEM] * Z_GROUP,
        out_specs=VMEM,
        compiler_params=PARAMS,
        name="pick_top",
    )(idx, *got)


def eliminate(block):
    sub = lax.broadcasted_iota(jnp.int32, (8, 2 * NB), 0)
    lane = lax.broadcasted_iota(jnp.int32, (8, 2 * NB), 1)
    groups = NB // 8

    def spread(x):
        return jnp.broadcast_to(x, (8, 2 * NB))

    m = []
    for g in range(groups):
        eye = jnp.where(lane == sub + (8 * g + NB), F32(1), F32(0))
        m.append(jnp.concatenate([block[8 * g : 8 * g + 8], eye[:, NB:]], axis=1))
    scale = []
    for g0 in range(groups):
        j = g0 * PIV
        cols = [[spread(m[g][:, j + q : j + q + 1]) for g in range(g0, groups)] for q in range(PIV)]
        rows = [spread(m[g0][q : q + 1, :]) for q in range(PIV)]
        a = {}
        for q in range(PIV):
            for i in range(q, PIV):
                a[i, q] = spread(cols[q][0][i : i + 1, :])
        low = {}
        inv = []
        pivots = None
        for q in range(PIV):
            inv.append(1.0 / a[q, q])
            pivots = a[q, q] if pivots is None else jnp.where(sub >= q, a[q, q], pivots)
            for i in range(q + 1, PIV):
                low[i, q] = a[i, q] * inv[q]
            for jj in range(q + 1, PIV):
                for i in range(jj, PIV):
                    a[i, jj] = a[i, jj] - low[i, q] * a[jj, q]
        scale.append(lax.rsqrt(pivots))
        scaled = []
        for q in range(PIV):
            for i in range(q + 1, PIV):
                rows[i] = rows[i] - low[i, q] * rows[q]
            scaled.append(rows[q] * inv[q])
        for g in range(g0, groups):
            x = [cols[q][g - g0] for q in range(PIV)]
            updated = m[g]
            for q in range(PIV):
                for i in range(q + 1, PIV):
                    x[i] = x[i] - low[i, q] * x[q]
                part = x[q]
                if g == g0:
                    part = jnp.where(sub > q, part, F32(0))
                updated = updated - part * scaled[q]
            m[g] = updated
    return jnp.concatenate([m[g] * scale[g] for g in range(groups)], axis=0)


def chol_inv(w, lc):
    blocks = TILE // NB
    rows = lax.broadcasted_iota(jnp.int32, (2 * TILE, NB), 0)
    r64 = lax.broadcasted_iota(jnp.int32, (NB, NB), 0)
    c64 = lax.broadcasted_iota(jnp.int32, (NB, NB), 1)

    def step(b, carry):
        base = pl.multiple_of(b * NB, NB)
        m = eliminate(w[b, pl.ds(base, NB), :]).T
        lower = jnp.where(r64 >= c64, m[:NB], F32(0))
        inv_t = jnp.where(r64 <= c64, m[NB:], F32(0))
        p = jnp.where(rows >= base + NB, dot_nn(w[b], inv_t), F32(0))
        lc[b] = p
        lc[b, pl.ds(base, NB), :] = lower
        for bj in range(1, blocks):

            @pl.when(bj > b)
            def _():
                w[bj] = w[bj] - dot_nt(p, p[bj * NB : (bj + 1) * NB])

        return carry

    lax.fori_loop(0, blocks, step, 0)


def factor_tile(tile, l_ref, it_ref, w, lc):
    blocks = TILE // NB
    r = lax.broadcasted_iota(jnp.int32, (TILE, NB), 0)
    c = lax.broadcasted_iota(jnp.int32, (TILE, NB), 1)
    for b in range(blocks):
        w[b, :TILE, :] = tile[:, b * NB : (b + 1) * NB]
        w[b, TILE:, :] = jnp.where(r == c + b * NB, F32(1), F32(0))
    chol_inv(w, lc)
    l_ref[...] = jnp.concatenate([lc[b, :TILE, :] for b in range(blocks)], axis=1)
    inv_t = jnp.concatenate([lc[b, TILE:, :] for b in range(blocks)], axis=1)
    it_ref[...] = inv_t
    return inv_t


def factor0_kernel(idx, *rest):
    got = rest[:2]
    l_ref, it_ref, lb_ref, t11, t21, t22, top, w, lc = rest[2:]
    core = idx[0] % 2
    for x in range(N_X):
        for other in range(2):
            base = pl.multiple_of((2 * x + (core + other) % 2) * SUB, SUB)
            top[:, :, pl.ds(base, SUB), :] = got[other][x]
    inv_t = factor_tile(top[0, 0], l_ref, it_ref, w, lc)
    low1 = dot_nn(top[0, 1], inv_t).astype(BF16)
    low2 = dot_nn(top[2, 1].T, inv_t).astype(BF16)
    lb_ref[0] = low1
    lb_ref[1] = low2
    t11[...] = top[1, 0] - dot_bf(low1, low1)
    t21[...] = top[1, 1] - dot_bf(low2, low1)
    t22[...] = top[2, 0] - dot_bf(low2, low2)


def factor1_kernel(t11, t21, t22, l_ref, it_ref, lb_ref, rest_ref, w, lc):
    inv_t = factor_tile(t11[...], l_ref, it_ref, w, lc)
    low = dot_nn(t21[...], inv_t).astype(BF16)
    lb_ref[...] = low
    rest_ref[...] = t22[...] - dot_bf(low, low)


def factor2_kernel(t22, l_ref, it_ref, w, lc):
    factor_tile(t22[...], l_ref, it_ref, w, lc)


SQUARE = jax.ShapeDtypeStruct((TILE, TILE), F32)
FACTOR_COST = pl.CostEstimate(flops=15_000_000_000, transcendentals=0, bytes_accessed=2_000_000)
WORK = [pltpu.VMEM((TILE // NB, 2 * TILE, NB), F32)] * 2


def factor0(idx, got):
    return pl.pallas_call(
        factor0_kernel,
        out_shape=[SQUARE, SQUARE, jax.ShapeDtypeStruct((2, TILE, TILE), BF16), SQUARE, SQUARE, SQUARE],
        in_specs=[SMEM] + [VMEM] * 2,
        out_specs=[VMEM] * 6,
        scratch_shapes=[pltpu.VMEM((PANELS, 2, TILE, TILE), F32)] + WORK,
        cost_estimate=FACTOR_COST,
        compiler_params=PARAMS,
        name="factor0",
    )(idx, *got)


def factor1(t11, t21, t22):
    return pl.pallas_call(
        factor1_kernel,
        out_shape=[SQUARE, SQUARE, jax.ShapeDtypeStruct((TILE, TILE), BF16), SQUARE],
        in_specs=[VMEM] * 3,
        out_specs=[VMEM] * 4,
        scratch_shapes=WORK,
        cost_estimate=FACTOR_COST,
        compiler_params=PARAMS,
        name="factor1",
    )(t11, t21, t22)


def factor2(t22):
    return pl.pallas_call(
        factor2_kernel,
        out_shape=[SQUARE, SQUARE],
        in_specs=[VMEM],
        out_specs=[VMEM] * 2,
        scratch_shapes=WORK,
        cost_estimate=FACTOR_COST,
        compiler_params=PARAMS,
        name="factor2",
    )(t22)


def solve_kernel(idx, it0, it1, it2, lb0, lb1, *rest):
    got, out, rows = rest[:N_Z], rest[N_Z], rest[N_Z + 1]
    r, y, z = idx[0], idx[1], idx[2]
    for s in range(N_Z):
        source = (z + N_Z - s) % N_Z

        @pl.when(source < PANELS)
        def _():
            rows[source] = got[s][...]

    chunk = HALVES * SUB
    half = lax.broadcasted_iota(jnp.int32, (chunk, TILE), 0) // SUB
    tile_row = (half * N_Y + y) * N_ROW + r

    def keep(k, left, inverse):
        return jnp.where(tile_row > k, dot_nn(left, inverse[...]), F32(0)).astype(BF16)

    s0 = keep(0, rows[0].reshape(chunk, TILE), it0)
    s1 = keep(1, rows[1].reshape(chunk, TILE) - dot_bf(s0, lb0[0]), it1)
    s2 = keep(2, rows[2].reshape(chunk, TILE) - dot_bf(s0, lb0[1]) - dot_bf(s1, lb1[...]), it2)
    for k, done in enumerate((s0, s1, s2)):
        out[:, :, k * TILE : (k + 1) * TILE] = done.reshape(HALVES, SUB, TILE)


def solve(idx, inverses, lb0, lb1, got):
    return pl.pallas_call(
        solve_kernel,
        out_shape=jax.ShapeDtypeStruct((HALVES, SUB, PANELS * TILE), BF16),
        in_specs=[SMEM] + [VMEM] * (PANELS + 2 + N_Z),
        out_specs=VMEM,
        scratch_shapes=[pltpu.VMEM((PANELS, HALVES, SUB, TILE), F32)],
        compiler_params=PARAMS,
        name="solve",
    )(idx, *inverses, lb0, lb1, *got)


def join_z_kernel(idx, *rest):
    got, outs = rest[:N_Z], rest[N_Z:]
    for s in range(N_Z):
        base = pl.multiple_of((idx[2] + N_Z - s) % N_Z * SUB, SUB)
        for h in range(HALVES):
            outs[h][pl.ds(base, SUB), :] = got[s][h]


def join_z(idx, got):
    return pl.pallas_call(
        join_z_kernel,
        out_shape=[jax.ShapeDtypeStruct((TILE, PANELS * TILE), BF16)] * HALVES,
        in_specs=[SMEM] + [VMEM] * N_Z,
        out_specs=[VMEM] * HALVES,
        compiler_params=PARAMS,
        name="join_z",
    )(idx, *got)


def join_x_kernel(idx, *rest):
    got, out = rest[:-1], rest[-1]
    for s in range(N_X):
        out[(idx[0] // 2 + N_X - s) % N_X] = got[s][...]


def join_x(idx, got):
    return pl.pallas_call(
        join_x_kernel,
        out_shape=jax.ShapeDtypeStruct((N_X,) + got[0].shape, got[0].dtype),
        in_specs=[SMEM] + [VMEM] * N_X,
        out_specs=VMEM,
        compiler_params=PARAMS,
        name="join_x",
    )(idx, *got)


def join_cols_kernel(idx, own, other, out):
    core = idx[0] % 2
    for n, ref in enumerate((own, other)):
        for x in range(N_X):
            base = pl.multiple_of((2 * x + (core + n) % 2) * SUB, SUB)
            out[:, pl.ds(base, SUB), :] = ref[x]


def join_cols(idx, parts):
    return pl.pallas_call(
        join_cols_kernel,
        out_shape=jax.ShapeDtypeStruct((HALVES, TILE, PANELS * TILE), BF16),
        in_specs=[SMEM, VMEM, VMEM],
        out_specs=VMEM,
        compiler_params=PARAMS,
        name="join_cols",
    )(idx, *parts)


def part_tile(n, idx, shifts):
    shift = shifts[0] + (shifts[-1] - shifts[0]) * (n // HALVES)
    return n % HALVES * N_Y + (idx[1] + N_Y - shift) % N_Y


def update_kernel(shifts, idx, a_ref, c_all, *rest):
    count = HALVES * len(shifts)
    row_parts, rest = rest[:count], rest[count:]
    factors, inverses, rest = rest[:PANELS], rest[PANELS : 2 * PANELS], rest[2 * PANELS :]
    out, s_all, l_own, it_own, row_sem, own_sem = rest[-6:]
    r, c = idx[0], idx[3]
    n = pl.program_id(0)
    n_col = N_Y * N_Z

    def own_copies(k):
        return (
            pltpu.make_async_copy(factors[k], l_own, own_sem.at[0]),
            pltpu.make_async_copy(inverses[k], it_own, own_sem.at[1]),
        )

    @pl.when(n == 0)
    def _():
        for m in range(count):
            pltpu.make_async_copy(row_parts[m], s_all.at[m], row_sem.at[m]).start()
        for k in range(PANELS):

            @pl.when(c == k)
            def _():
                for copy in own_copies(k):
                    copy.start()

    pltpu.make_async_copy(row_parts[0], s_all.at[n], row_sem.at[n]).wait()
    i = part_tile(n, idx, shifts) * N_ROW + r
    for u in range(HALVES):
        lanes = slice(u * TILE, (u + 1) * TILE)
        j = c + u * n_col

        @pl.when(i >= j)
        def _():
            out[:, lanes] = a_ref[:, lanes] - dot_bf(s_all[n], c_all[u])

        @pl.when(i < j)
        def _():
            out[:, lanes] = a_ref[:, lanes]

    @pl.when(jnp.logical_and(c < PANELS, n == 0))
    def _():
        for copy in own_copies(0):
            copy.wait()

    @pl.when(jnp.logical_and(c < PANELS, i > c))
    def _():
        out[:, :TILE] = dot_nn(out[:, :TILE], it_own[...])

    @pl.when(jnp.logical_and(c < PANELS, i == c))
    def _():
        out[:, :TILE] = l_own[...]


def update(idx, matrix, done, col_rows, row_parts, shifts, factors, inverses):
    count = HALVES * len(shifts)
    block = pl.BlockSpec((TILE, matrix.shape[1]), lambda n, idx: (part_tile(n, idx, shifts), 0))
    operands = [idx, matrix, col_rows, *row_parts, *factors, *inverses]
    in_specs = [block] + [VMEM] * (1 + count) + [ANY] * (2 * PANELS)
    aliases = {}
    if done is not None:
        aliases = {len(operands): 0}
        operands.append(done)
        in_specs.append(ANY)
    return pl.pallas_call(
        lambda *refs: update_kernel(shifts, *refs),
        grid_spec=pltpu.PrefetchScalarGridSpec(
            num_scalar_prefetch=1,
            grid=(count,),
            in_specs=in_specs,
            out_specs=block,
            scratch_shapes=[
                pltpu.VMEM((count, TILE, PANELS * TILE), BF16),
                pltpu.VMEM((TILE, TILE), F32),
                pltpu.VMEM((TILE, TILE), F32),
                pltpu.SemaphoreType.DMA((count,)),
                pltpu.SemaphoreType.DMA((2,)),
            ],
        ),
        out_shape=jax.ShapeDtypeStruct(matrix.shape, F32),
        input_output_aliases=aliases,
        compiler_params=PARAMS,
        name="update",
    )(*operands)


def on_device(matrix):
    row_index = lax.axis_index("row")
    col_index = lax.axis_index("col")
    y_index, z_index = col_index // N_Z, col_index % N_Z
    idx = jnp.stack([row_index, y_index, z_index, col_index]).astype(jnp.int32)
    barrier = lax.optimization_barrier

    sent = pack_top(idx, matrix)
    tiles = pack_y(matrix)
    slices = pick_row(idx, [sent[0]] + [row_shift(sent[s], s) for s in range(1, N_ROW)])
    slices = lax.select_n(y_index, slices, *[y_shift(slices, s) for s in range(1, N_Y)])
    slices, tiles = barrier((slices, tiles))
    slices = jnp.where(z_index < Z_GROUP, slices, z_shift(slices, Z_GROUP))
    top = pick_top(idx, [slices] + [z_group_shift(slices, s) for s in range(1, Z_GROUP)])
    top = join_x(idx, [top] + [x_shift(top, s) for s in range(1, N_X)])
    top_parts = [top, core_swap(top)]
    top_parts, tiles = barrier((top_parts, tiles))

    shifted = [y_shift(tiles[s], s) for s in range(1, N_Y)]
    l0, it0, lb0, t11, t21, t22 = factor0(idx, top_parts)
    l1, it1, lb1, t22 = factor1(t11, t21, t22)
    tiles, shifted, t22 = barrier((tiles, shifted, t22))
    sent = pack_z(idx, tiles[0], shifted)
    sent, t22 = barrier((sent, t22))
    scattered = [sent[0]] + [z_shift(sent[s], s) for s in range(1, N_Z)]
    l2, it2 = factor2(t22)
    solved = solve(idx, [it0, it1, it2], lb0, lb1, scattered)

    swapped = row_z_swap(solved)
    over_z = [solved] + [z_shift(solved, s) for s in range(1, N_Z) if s != N_Z // 2]
    over_z.insert(N_Z // 2, z_shift(over_z[N_Z // 2 - 1], 1))
    over_x = [swapped] + [x_shift(swapped, s) for s in range(1, N_X)]
    low, high = join_z(idx, over_z)
    low, high, over_x = barrier((low, high, over_x))
    col_half = join_x(idx, over_x)
    low_up, high_down = y_shift(low, 1), y_shift(high, N_Y - 1)
    high_up, low_down = y_shift(high, 1), y_shift(low, N_Y - 1)
    low_far, high_far = y_shift(low_up, 1), y_shift(high_down, N_Y - 1)
    own = ([l0, l1, l2], [it0, it1, it2])
    col_rows = join_cols(idx, [col_half, core_swap(col_half)])
    out = update(idx, matrix, None, col_rows, [low, high], (0,), *own)
    out = update(idx, matrix, out, col_rows, [low_up, high_up, low_down, high_down], (1, N_Y - 1), *own)
    return update(idx, matrix, out, col_rows, [low_far, high_far], (N_Y // 2,), *own)


def solution(mesh):
    return jax.shard_map(
        on_device, mesh=mesh, in_specs=(P("row", "col"),), out_specs=P("row", "col"), check_vma=False
    )
```

```python
import jax
import jax.numpy as jnp
from jax import lax
from jax.experimental import pallas as pl
from jax.experimental.pallas import tpu as pltpu
from jax.sharding import PartitionSpec as P

TILE = 256
PANELS = 3
NB = 64
PIV = 8
N_ROW = 8
N_Y = 4
N_Z = 8
SUB = TILE // 8
HALVES = 2
F32 = jnp.float32
BF16 = jnp.bfloat16
HIGHEST = lax.Precision.HIGHEST
N_X = 4
Z_GROUP = 4


def dot_nn(a, b):
    return lax.dot_general(a, b, (((1,), (0,)), ((), ())), precision=HIGHEST, preferred_element_type=F32)


def dot_nt(a, b):
    return lax.dot_general(a, b, (((1,), (1,)), ((), ())), precision=HIGHEST, preferred_element_type=F32)


def dot_bf(a, b):
    return lax.dot_general(a, b, (((1,), (1,)), ((), ())), preferred_element_type=F32)


def y_shift(x, s):
    pairs = [(y * N_Z + z, (y + s) % N_Y * N_Z + z) for y in range(N_Y) for z in range(N_Z)]
    return lax.ppermute(x, "col", pairs)


def z_shift(x, s):
    pairs = [(y * N_Z + z, y * N_Z + (z + s) % N_Z) for y in range(N_Y) for z in range(N_Z)]
    return lax.ppermute(x, "col", pairs)


def row_shift(x, s):
    return lax.ppermute(x, "row", [(r, (r + s) % N_ROW) for r in range(N_ROW)])


def z_group_shift(x, s):
    pairs = [
        (y * N_Z + z, y * N_Z + z // Z_GROUP * Z_GROUP + (z % Z_GROUP + s) % Z_GROUP)
        for y in range(N_Y)
        for z in range(N_Z)
    ]
    return lax.ppermute(x, "col", pairs)


def x_shift(x, s):
    return lax.ppermute(x, "row", [(r, (r + 2 * s) % N_ROW) for r in range(N_ROW)])


def core_swap(x):
    return lax.ppermute(x, "row", [(r, r ^ 1) for r in range(N_ROW)])


def row_z_swap(x):
    n_col = N_Y * N_Z
    pairs = [
        (r * n_col + y * N_Z + z, z * n_col + y * N_Z + r)
        for r in range(N_ROW)
        for y in range(N_Y)
        for z in range(N_Z)
    ]
    return lax.ppermute(x, ("row", "col"), pairs)


SMEM = pl.BlockSpec(memory_space=pltpu.SMEM)
ANY = pl.BlockSpec(memory_space=pl.ANY)
VMEM = pl.BlockSpec(memory_space=pltpu.VMEM)
PARAMS = pltpu.CompilerParams(vmem_limit_bytes=16 * 2**20)


def pack_top_kernel(idx, tile, *outs):
    for s in range(N_ROW):
        base = pl.multiple_of((idx[0] + s) % N_ROW * SUB, SUB)
        outs[s][...] = tile[pl.ds(base, SUB), :]


def pack_top(idx, tile):
    return pl.pallas_call(
        pack_top_kernel,
        out_shape=[jax.ShapeDtypeStruct((SUB, TILE), F32)] * N_ROW,
        in_specs=[SMEM, VMEM],
        out_specs=[VMEM] * N_ROW,
        compiler_params=PARAMS,
        name="pack_top",
    )(idx, tile)


def pack_y_kernel(*refs):
    for s in range(N_Y):
        refs[N_Y + s][...] = refs[s][...]


def pack_y(matrix):
    return pl.pallas_call(
        pack_y_kernel,
        grid=(HALVES,),
        out_shape=[jax.ShapeDtypeStruct((HALVES, TILE, TILE), F32)] * N_Y,
        in_specs=[pl.BlockSpec((TILE, TILE), lambda h, s=s: (h * N_Y + s, 0)) for s in range(N_Y)],
        out_specs=[pl.BlockSpec((None, TILE, TILE), lambda h: (h, 0, 0))] * N_Y,
        compiler_params=PARAMS,
        name="pack_y",
    )(*[matrix] * N_Y)


def pack_z_kernel(idx, own, *rest):
    got, outs = rest[: N_Y - 1], rest[N_Y - 1 :]
    y, z = idx[1], idx[2]
    for source, ref in enumerate((own,) + tuple(got)):

        @pl.when(y == source)
        def _():
            for s in range(N_Z):
                base = pl.multiple_of((z + s) % N_Z * SUB, SUB)
                outs[s][...] = ref[:, pl.ds(base, SUB), :]


def pack_z(idx, own, got):
    return pl.pallas_call(
        pack_z_kernel,
        out_shape=[jax.ShapeDtypeStruct((HALVES, SUB, TILE), F32)] * N_Z,
        in_specs=[SMEM] + [VMEM] * N_Y,
        out_specs=[VMEM] * N_Z,
        compiler_params=PARAMS,
        name="pack_z",
    )(idx, own, *got)


def pick_row_kernel(idx, *rest):
    got, out = rest[:-1], rest[-1]
    first = idx[3] % PANELS
    for s, ref in enumerate(got):
        source = (idx[0] + N_ROW - s) % N_ROW
        for n in range(2):

            @pl.when(source == (first + n) % PANELS)
            def _():
                out[n] = ref[...]


def pick_row(idx, got):
    return pl.pallas_call(
        pick_row_kernel,
        out_shape=jax.ShapeDtypeStruct((2, SUB, TILE), F32),
        in_specs=[SMEM] + [VMEM] * N_ROW,
        out_specs=VMEM,
        compiler_params=PARAMS,
        name="pick_row",
    )(idx, *got)


def pick_top_kernel(idx, *rest):
    got, out = rest[:-1], rest[-1]
    for s, ref in enumerate(got):
        source = (idx[2] % Z_GROUP + Z_GROUP - s) % Z_GROUP

        @pl.when(source < PANELS)
        def _():
            out[source] = ref[...]


def pick_top(idx, got):
    return pl.pallas_call(
        pick_top_kernel,
        out_shape=jax.ShapeDtypeStruct((PANELS, 2, SUB, TILE), F32),
        in_specs=[SMEM] + [VMEM] * Z_GROUP,
        out_specs=VMEM,
        compiler_params=PARAMS,
        name="pick_top",
    )(idx, *got)


def eliminate(block):
    sub = lax.broadcasted_iota(jnp.int32, (8, 2 * NB), 0)
    lane = lax.broadcasted_iota(jnp.int32, (8, 2 * NB), 1)
    groups = NB // 8

    def spread(x):
        return jnp.broadcast_to(x, (8, 2 * NB))

    m = []
    for g in range(groups):
        eye = jnp.where(lane == sub + (8 * g + NB), F32(1), F32(0))
        m.append(jnp.concatenate([block[8 * g : 8 * g + 8], eye[:, NB:]], axis=1))
    scale = []
    for g0 in range(groups):
        j = g0 * PIV
        cols = [[spread(m[g][:, j + q : j + q + 1]) for g in range(g0, groups)] for q in range(PIV)]
        rows = [spread(m[g0][q : q + 1, :]) for q in range(PIV)]
        a = {}
        for q in range(PIV):
            for i in range(q, PIV):
                a[i, q] = spread(cols[q][0][i : i + 1, :])
        low = {}
        inv = []
        pivots = None
        for q in range(PIV):
            inv.append(1.0 / a[q, q])
            pivots = a[q, q] if pivots is None else jnp.where(sub >= q, a[q, q], pivots)
            for i in range(q + 1, PIV):
                low[i, q] = a[i, q] * inv[q]
            for jj in range(q + 1, PIV):
                for i in range(jj, PIV):
                    a[i, jj] = a[i, jj] - low[i, q] * a[jj, q]
        scale.append(lax.rsqrt(pivots))
        scaled = []
        for q in range(PIV):
            for i in range(q + 1, PIV):
                rows[i] = rows[i] - low[i, q] * rows[q]
            scaled.append(rows[q] * inv[q])
        for g in range(g0, groups):
            x = [cols[q][g - g0] for q in range(PIV)]
            updated = m[g]
            for q in range(PIV):
                for i in range(q + 1, PIV):
                    x[i] = x[i] - low[i, q] * x[q]
                part = x[q]
                if g == g0:
                    part = jnp.where(sub > q, part, F32(0))
                updated = updated - part * scaled[q]
            m[g] = updated
    return jnp.concatenate([m[g] * scale[g] for g in range(groups)], axis=0)


def factor_tile(tile, l_ref, it_ref, w):
    rows = lax.broadcasted_iota(jnp.int32, (TILE, TILE), 0)
    cols = lax.broadcasted_iota(jnp.int32, (TILE, TILE), 1)
    r64 = lax.broadcasted_iota(jnp.int32, (NB, NB), 0)
    c64 = lax.broadcasted_iota(jnp.int32, (NB, NB), 1)
    w[:TILE, :] = tile
    w[TILE:, :] = jnp.where(rows == cols, F32(1), F32(0))
    for lo in range(0, TILE, NB):
        hi = lo + NB
        below = TILE - hi
        m = eliminate(w[lo:hi, lo:hi]).T
        inv_t = jnp.where(r64 <= c64, m[NB:], F32(0))
        p = dot_nn(w[hi : TILE + hi, lo:hi], inv_t)
        l_ref[lo:hi, lo:hi] = jnp.where(r64 >= c64, m[:NB], F32(0))
        it_ref[:hi, lo:hi] = p[below:]
        if lo:
            l_ref[:lo, lo:hi] = jnp.zeros((lo, NB), F32)
        if below:
            l_ref[hi:, lo:hi] = p[:below]
            it_ref[hi:, lo:hi] = jnp.zeros((below, NB), F32)
            w[hi : TILE + hi, hi:] = w[hi : TILE + hi, hi:] - dot_nt(p, p[:below])
    return it_ref[...]


def factor0_kernel(idx, *rest):
    got = rest[:2]
    l_ref, it_ref, lb_ref, t11, t21, t22, top, w = rest[2:]
    core = idx[0] % 2
    for x in range(N_X):
        for other in range(2):
            base = pl.multiple_of((2 * x + (core + other) % 2) * SUB, SUB)
            top[:, :, pl.ds(base, SUB), :] = got[other][x]
    inv_t = factor_tile(top[0, 0], l_ref, it_ref, w)
    low1 = dot_nn(top[0, 1], inv_t).astype(BF16)
    low2 = dot_nn(top[2, 1].T, inv_t).astype(BF16)
    lb_ref[0] = low1
    lb_ref[1] = low2
    t11[...] = top[1, 0] - dot_bf(low1, low1)
    t21[...] = top[1, 1] - dot_bf(low2, low1)
    t22[...] = top[2, 0] - dot_bf(low2, low2)


def factor1_kernel(t11, t21, t22, l_ref, it_ref, lb_ref, rest_ref, w):
    inv_t = factor_tile(t11[...], l_ref, it_ref, w)
    low = dot_nn(t21[...], inv_t).astype(BF16)
    lb_ref[...] = low
    rest_ref[...] = t22[...] - dot_bf(low, low)


def factor2_kernel(t22, l_ref, it_ref, w):
    factor_tile(t22[...], l_ref, it_ref, w)


SQUARE = jax.ShapeDtypeStruct((TILE, TILE), F32)
FACTOR_COST = pl.CostEstimate(flops=15_000_000_000, transcendentals=0, bytes_accessed=2_000_000)
WORK = [pltpu.VMEM((2 * TILE, TILE), F32)]


def factor0(idx, got):
    return pl.pallas_call(
        factor0_kernel,
        out_shape=[SQUARE, SQUARE, jax.ShapeDtypeStruct((2, TILE, TILE), BF16), SQUARE, SQUARE, SQUARE],
        in_specs=[SMEM] + [VMEM] * 2,
        out_specs=[VMEM] * 6,
        scratch_shapes=[pltpu.VMEM((PANELS, 2, TILE, TILE), F32)] + WORK,
        cost_estimate=FACTOR_COST,
        compiler_params=PARAMS,
        name="factor0",
    )(idx, *got)


def factor1(t11, t21, t22):
    return pl.pallas_call(
        factor1_kernel,
        out_shape=[SQUARE, SQUARE, jax.ShapeDtypeStruct((TILE, TILE), BF16), SQUARE],
        in_specs=[VMEM] * 3,
        out_specs=[VMEM] * 4,
        scratch_shapes=WORK,
        cost_estimate=FACTOR_COST,
        compiler_params=PARAMS,
        name="factor1",
    )(t11, t21, t22)


def factor2(t22):
    return pl.pallas_call(
        factor2_kernel,
        out_shape=[SQUARE, SQUARE],
        in_specs=[VMEM],
        out_specs=[VMEM] * 2,
        scratch_shapes=WORK,
        cost_estimate=FACTOR_COST,
        compiler_params=PARAMS,
        name="factor2",
    )(t22)


def solve_kernel(idx, it0, it1, it2, lb0, lb1, *rest):
    got, out, rows = rest[:N_Z], rest[N_Z], rest[N_Z + 1]
    r, y, z = idx[0], idx[1], idx[2]
    for s in range(N_Z):
        source = (z + N_Z - s) % N_Z

        @pl.when(source < PANELS)
        def _():
            rows[source] = got[s][...]

    chunk = HALVES * SUB
    half = lax.broadcasted_iota(jnp.int32, (chunk, TILE), 0) // SUB
    tile_row = (half * N_Y + y) * N_ROW + r

    def keep(k, left, inverse):
        return jnp.where(tile_row > k, dot_nn(left, inverse[...]), F32(0)).astype(BF16)

    s0 = keep(0, rows[0].reshape(chunk, TILE), it0)
    s1 = keep(1, rows[1].reshape(chunk, TILE) - dot_bf(s0, lb0[0]), it1)
    s2 = keep(2, rows[2].reshape(chunk, TILE) - dot_bf(s0, lb0[1]) - dot_bf(s1, lb1[...]), it2)
    for k, done in enumerate((s0, s1, s2)):
        out[:, :, k * TILE : (k + 1) * TILE] = done.reshape(HALVES, SUB, TILE)


def solve(idx, inverses, lb0, lb1, got):
    return pl.pallas_call(
        solve_kernel,
        out_shape=jax.ShapeDtypeStruct((HALVES, SUB, PANELS * TILE), BF16),
        in_specs=[SMEM] + [VMEM] * (PANELS + 2 + N_Z),
        out_specs=VMEM,
        scratch_shapes=[pltpu.VMEM((PANELS, HALVES, SUB, TILE), F32)],
        compiler_params=PARAMS,
        name="solve",
    )(idx, *inverses, lb0, lb1, *got)


def join_z_kernel(idx, *rest):
    got, outs = rest[:N_Z], rest[N_Z:]
    for s in range(N_Z):
        base = pl.multiple_of((idx[2] + N_Z - s) % N_Z * SUB, SUB)
        for h in range(HALVES):
            outs[h][pl.ds(base, SUB), :] = got[s][h]


def join_z(idx, got):
    return pl.pallas_call(
        join_z_kernel,
        out_shape=[jax.ShapeDtypeStruct((TILE, PANELS * TILE), BF16)] * HALVES,
        in_specs=[SMEM] + [VMEM] * N_Z,
        out_specs=[VMEM] * HALVES,
        compiler_params=PARAMS,
        name="join_z",
    )(idx, *got)


def join_x_kernel(idx, *rest):
    got, out = rest[:-1], rest[-1]
    for s in range(N_X):
        out[(idx[0] // 2 + N_X - s) % N_X] = got[s][...]


def join_x(idx, got):
    return pl.pallas_call(
        join_x_kernel,
        out_shape=jax.ShapeDtypeStruct((N_X,) + got[0].shape, got[0].dtype),
        in_specs=[SMEM] + [VMEM] * N_X,
        out_specs=VMEM,
        compiler_params=PARAMS,
        name="join_x",
    )(idx, *got)


def join_cols_kernel(idx, own, other, out):
    core = idx[0] % 2
    for n, ref in enumerate((own, other)):
        for x in range(N_X):
            base = pl.multiple_of((2 * x + (core + n) % 2) * SUB, SUB)
            out[:, pl.ds(base, SUB), :] = ref[x]


def join_cols(idx, parts):
    return pl.pallas_call(
        join_cols_kernel,
        out_shape=jax.ShapeDtypeStruct((HALVES, TILE, PANELS * TILE), BF16),
        in_specs=[SMEM, VMEM, VMEM],
        out_specs=VMEM,
        compiler_params=PARAMS,
        name="join_cols",
    )(idx, *parts)


def part_tile(n, idx, shifts):
    shift = shifts[0] + (shifts[-1] - shifts[0]) * (n // HALVES)
    return n % HALVES * N_Y + (idx[1] + N_Y - shift) % N_Y


def update_kernel(shifts, idx, a_ref, c_all, *rest):
    count = HALVES * len(shifts)
    row_parts, rest = rest[:count], rest[count:]
    factors, inverses, rest = rest[:PANELS], rest[PANELS : 2 * PANELS], rest[2 * PANELS :]
    out, s_all, l_own, it_own, row_sem, own_sem = rest[-6:]
    r, c = idx[0], idx[3]
    n = pl.program_id(0)
    n_col = N_Y * N_Z

    def own_copies(k):
        return (
            pltpu.make_async_copy(factors[k], l_own, own_sem.at[0]),
            pltpu.make_async_copy(inverses[k], it_own, own_sem.at[1]),
        )

    @pl.when(n == 0)
    def _():
        for m in range(count):
            pltpu.make_async_copy(row_parts[m], s_all.at[m], row_sem.at[m]).start()
        for k in range(PANELS):

            @pl.when(c == k)
            def _():
                for copy in own_copies(k):
                    copy.start()

    pltpu.make_async_copy(row_parts[0], s_all.at[n], row_sem.at[n]).wait()
    i = part_tile(n, idx, shifts) * N_ROW + r
    for u in range(HALVES):
        lanes = slice(u * TILE, (u + 1) * TILE)
        j = c + u * n_col

        @pl.when(i >= j)
        def _():
            out[:, lanes] = a_ref[:, lanes] - dot_bf(s_all[n], c_all[u])

        @pl.when(i < j)
        def _():
            out[:, lanes] = a_ref[:, lanes]

    @pl.when(jnp.logical_and(c < PANELS, n == 0))
    def _():
        for copy in own_copies(0):
            copy.wait()

    @pl.when(jnp.logical_and(c < PANELS, i > c))
    def _():
        out[:, :TILE] = dot_nn(out[:, :TILE], it_own[...])

    @pl.when(jnp.logical_and(c < PANELS, i == c))
    def _():
        out[:, :TILE] = l_own[...]


def update(idx, matrix, done, col_rows, row_parts, shifts, factors, inverses):
    count = HALVES * len(shifts)
    block = pl.BlockSpec((TILE, matrix.shape[1]), lambda n, idx: (part_tile(n, idx, shifts), 0))
    operands = [idx, matrix, col_rows, *row_parts, *factors, *inverses]
    in_specs = [block] + [VMEM] * (1 + count) + [ANY] * (2 * PANELS)
    aliases = {}
    if done is not None:
        aliases = {len(operands): 0}
        operands.append(done)
        in_specs.append(ANY)
    return pl.pallas_call(
        lambda *refs: update_kernel(shifts, *refs),
        grid_spec=pltpu.PrefetchScalarGridSpec(
            num_scalar_prefetch=1,
            grid=(count,),
            in_specs=in_specs,
            out_specs=block,
            scratch_shapes=[
                pltpu.VMEM((count, TILE, PANELS * TILE), BF16),
                pltpu.VMEM((TILE, TILE), F32),
                pltpu.VMEM((TILE, TILE), F32),
                pltpu.SemaphoreType.DMA((count,)),
                pltpu.SemaphoreType.DMA((2,)),
            ],
        ),
        out_shape=jax.ShapeDtypeStruct(matrix.shape, F32),
        input_output_aliases=aliases,
        compiler_params=PARAMS,
        name="update",
    )(*operands)


def on_device(matrix):
    row_index = lax.axis_index("row")
    col_index = lax.axis_index("col")
    y_index, z_index = col_index // N_Z, col_index % N_Z
    idx = jnp.stack([row_index, y_index, z_index, col_index]).astype(jnp.int32)
    barrier = lax.optimization_barrier

    sent = pack_top(idx, matrix[:TILE, :TILE])
    tiles = pack_y(matrix)
    slices = pick_row(idx, [sent[0]] + [row_shift(sent[s], s) for s in range(1, N_ROW)])
    slices = lax.select_n(y_index, slices, *[y_shift(slices, s) for s in range(1, N_Y)])
    slices, tiles = barrier((slices, tiles))
    slices = jnp.where(z_index < Z_GROUP, slices, z_shift(slices, Z_GROUP))
    top = pick_top(idx, [slices] + [z_group_shift(slices, s) for s in range(1, Z_GROUP)])
    top = join_x(idx, [top] + [x_shift(top, s) for s in range(1, N_X)])
    top_parts = [top, core_swap(top)]
    top_parts, tiles = barrier((top_parts, tiles))

    shifted = [y_shift(tiles[s], s) for s in range(1, N_Y)]
    l0, it0, lb0, t11, t21, t22 = factor0(idx, top_parts)
    l1, it1, lb1, t22 = factor1(t11, t21, t22)
    tiles, shifted, t22 = barrier((tiles, shifted, t22))
    sent = pack_z(idx, tiles[0], shifted)
    sent, t22 = barrier((sent, t22))
    scattered = [sent[0]] + [z_shift(sent[s], s) for s in range(1, N_Z)]
    l2, it2 = factor2(t22)
    solved = solve(idx, [it0, it1, it2], lb0, lb1, scattered)

    swapped = row_z_swap(solved)
    over_z = [solved] + [z_shift(solved, s) for s in range(1, N_Z) if s != N_Z // 2]
    over_z.insert(N_Z // 2, z_shift(over_z[N_Z // 2 - 1], 1))
    over_x = [swapped] + [x_shift(swapped, s) for s in range(1, N_X)]
    low, high = join_z(idx, over_z)
    low, high, over_x = barrier((low, high, over_x))
    col_half = join_x(idx, over_x)
    low_up, high_down = y_shift(low, 1), y_shift(high, N_Y - 1)
    high_up, low_down = y_shift(high, 1), y_shift(low, N_Y - 1)
    low_far, high_far = y_shift(low_up, 1), y_shift(high_down, N_Y - 1)
    own = ([l0, l1, l2], [it0, it1, it2])
    col_rows = join_cols(idx, [col_half, core_swap(col_half)])
    out = update(idx, matrix, None, col_rows, [low, high], (0,), *own)
    out = update(idx, matrix, out, col_rows, [low_up, high_up, low_down, high_down], (1, N_Y - 1), *own)
    return update(idx, matrix, out, col_rows, [low_far, high_far], (N_Y // 2,), *own)


def solution(mesh):
    return jax.shard_map(
        on_device, mesh=mesh, in_specs=(P("row", "col"),), out_specs=P("row", "col"), check_vma=False
    )
```

```python
import jax
import jax.numpy as jnp
from jax import lax
from jax.experimental import pallas as pl
from jax.experimental.pallas import tpu as pltpu
from jax.sharding import PartitionSpec as P

TILE = 256
PANELS = 3
NB = 64
PIV = 8
N_ROW = 8
N_Y = 4
N_Z = 8
SUB = TILE // 8
HALVES = 2
F32 = jnp.float32
BF16 = jnp.bfloat16
HIGHEST = lax.Precision.HIGHEST
N_X = 4
Z_GROUP = 4


def dot_nn(a, b):
    return lax.dot_general(a, b, (((1,), (0,)), ((), ())), precision=HIGHEST, preferred_element_type=F32)


def dot_nt(a, b):
    return lax.dot_general(a, b, (((1,), (1,)), ((), ())), precision=HIGHEST, preferred_element_type=F32)


def dot_bf(a, b):
    return lax.dot_general(a, b, (((1,), (1,)), ((), ())), preferred_element_type=F32)


def y_shift(x, s):
    pairs = [(y * N_Z + z, (y + s) % N_Y * N_Z + z) for y in range(N_Y) for z in range(N_Z)]
    return lax.ppermute(x, "col", pairs)


def z_shift(x, s):
    pairs = [(y * N_Z + z, y * N_Z + (z + s) % N_Z) for y in range(N_Y) for z in range(N_Z)]
    return lax.ppermute(x, "col", pairs)


def row_shift(x, s):
    return lax.ppermute(x, "row", [(r, (r + s) % N_ROW) for r in range(N_ROW)])


def z_group_shift(x, s):
    pairs = [
        (y * N_Z + z, y * N_Z + z // Z_GROUP * Z_GROUP + (z % Z_GROUP + s) % Z_GROUP)
        for y in range(N_Y)
        for z in range(N_Z)
    ]
    return lax.ppermute(x, "col", pairs)


def x_shift(x, s):
    return lax.ppermute(x, "row", [(r, (r + 2 * s) % N_ROW) for r in range(N_ROW)])


def core_swap(x):
    return lax.ppermute(x, "row", [(r, r ^ 1) for r in range(N_ROW)])


def row_z_swap(x):
    n_col = N_Y * N_Z
    pairs = [
        (r * n_col + y * N_Z + z, z * n_col + y * N_Z + r)
        for r in range(N_ROW)
        for y in range(N_Y)
        for z in range(N_Z)
    ]
    return lax.ppermute(x, ("row", "col"), pairs)


SMEM = pl.BlockSpec(memory_space=pltpu.SMEM)
ANY = pl.BlockSpec(memory_space=pl.ANY)
VMEM = pl.BlockSpec(memory_space=pltpu.VMEM)
PARAMS = pltpu.CompilerParams(vmem_limit_bytes=16 * 2**20)


def pack_top_kernel(idx, tile, *outs):
    for s in range(N_ROW):
        base = pl.multiple_of((idx[0] + s) % N_ROW * SUB, SUB)
        outs[s][...] = tile[pl.ds(base, SUB), :]


def pack_top(idx, tile):
    return pl.pallas_call(
        pack_top_kernel,
        out_shape=[jax.ShapeDtypeStruct((SUB, TILE), F32)] * N_ROW,
        in_specs=[SMEM, VMEM],
        out_specs=[VMEM] * N_ROW,
        compiler_params=PARAMS,
        name="pack_top",
    )(idx, tile)


def pack_y_kernel(*refs):
    for s in range(N_Y):
        refs[N_Y + s][...] = refs[s][...]


def pack_y(matrix):
    return pl.pallas_call(
        pack_y_kernel,
        grid=(HALVES,),
        out_shape=[jax.ShapeDtypeStruct((HALVES, TILE, TILE), F32)] * N_Y,
        in_specs=[pl.BlockSpec((TILE, TILE), lambda h, s=s: (h * N_Y + s, 0)) for s in range(N_Y)],
        out_specs=[pl.BlockSpec((None, TILE, TILE), lambda h: (h, 0, 0))] * N_Y,
        compiler_params=PARAMS,
        name="pack_y",
    )(*[matrix] * N_Y)


def pack_z_kernel(idx, own, *rest):
    got, outs = rest[: N_Y - 1], rest[N_Y - 1 :]
    y, z = idx[1], idx[2]
    for source, ref in enumerate((own,) + tuple(got)):

        @pl.when(y == source)
        def _():
            for s in range(N_Z):
                base = pl.multiple_of((z + s) % N_Z * SUB, SUB)
                outs[s][...] = ref[:, pl.ds(base, SUB), :]


def pack_z(idx, own, got):
    return pl.pallas_call(
        pack_z_kernel,
        out_shape=[jax.ShapeDtypeStruct((HALVES, SUB, TILE), F32)] * N_Z,
        in_specs=[SMEM] + [VMEM] * N_Y,
        out_specs=[VMEM] * N_Z,
        compiler_params=PARAMS,
        name="pack_z",
    )(idx, own, *got)


def pick_row_kernel(idx, *rest):
    got, out = rest[:-1], rest[-1]
    first = idx[3] % PANELS
    for s, ref in enumerate(got):
        source = (idx[0] + N_ROW - s) % N_ROW
        for n in range(2):

            @pl.when(source == (first + n) % PANELS)
            def _():
                out[n] = ref[...]


def pick_row(idx, got):
    return pl.pallas_call(
        pick_row_kernel,
        out_shape=jax.ShapeDtypeStruct((2, SUB, TILE), F32),
        in_specs=[SMEM] + [VMEM] * N_ROW,
        out_specs=VMEM,
        compiler_params=PARAMS,
        name="pick_row",
    )(idx, *got)


def pick_top_kernel(idx, *rest):
    got, out = rest[:-1], rest[-1]
    for s, ref in enumerate(got):
        source = (idx[2] % Z_GROUP + Z_GROUP - s) % Z_GROUP

        @pl.when(source < PANELS)
        def _():
            out[source] = ref[...]


def pick_top(idx, got):
    return pl.pallas_call(
        pick_top_kernel,
        out_shape=jax.ShapeDtypeStruct((PANELS, 2, SUB, TILE), F32),
        in_specs=[SMEM] + [VMEM] * Z_GROUP,
        out_specs=VMEM,
        compiler_params=PARAMS,
        name="pick_top",
    )(idx, *got)


def eliminate(block):
    sub = lax.broadcasted_iota(jnp.int32, (8, 2 * NB), 0)
    lane = lax.broadcasted_iota(jnp.int32, (8, 2 * NB), 1)
    groups = NB // 8

    def spread(x):
        return jnp.broadcast_to(x, (8, 2 * NB))

    m = []
    for g in range(groups):
        eye = jnp.where(lane == sub + (8 * g + NB), F32(1), F32(0))
        m.append(jnp.concatenate([block[8 * g : 8 * g + 8], eye[:, NB:]], axis=1))
    scale = []
    for g0 in range(groups):
        j = g0 * PIV
        cols = [[spread(m[g][:, j + q : j + q + 1]) for g in range(g0, groups)] for q in range(PIV)]
        rows = [spread(m[g0][q : q + 1, :]) for q in range(PIV)]
        a = {}
        for q in range(PIV):
            for i in range(q, PIV):
                a[i, q] = spread(cols[q][0][i : i + 1, :])
        low = {}
        inv = []
        pivots = None
        for q in range(PIV):
            inv.append(1.0 / a[q, q])
            pivots = a[q, q] if pivots is None else jnp.where(sub >= q, a[q, q], pivots)
            for i in range(q + 1, PIV):
                low[i, q] = a[i, q] * inv[q]
            for jj in range(q + 1, PIV):
                for i in range(jj, PIV):
                    a[i, jj] = a[i, jj] - low[i, q] * a[jj, q]
        scale.append(lax.rsqrt(pivots))
        scaled = []
        for q in range(PIV):
            for i in range(q + 1, PIV):
                rows[i] = rows[i] - low[i, q] * rows[q]
            scaled.append(rows[q] * inv[q])
        for g in range(g0, groups):
            x = [cols[q][g - g0] for q in range(PIV)]
            updated = m[g]
            for q in range(PIV):
                for i in range(q + 1, PIV):
                    x[i] = x[i] - low[i, q] * x[q]
                part = x[q]
                if g == g0:
                    part = jnp.where(sub > q, part, F32(0))
                updated = updated - part * scaled[q]
            m[g] = updated
    return jnp.concatenate([m[g] * scale[g] for g in range(groups)], axis=0)


def factor_tile(tile, l_ref, it_ref, w):
    rows = lax.broadcasted_iota(jnp.int32, (TILE, TILE), 0)
    cols = lax.broadcasted_iota(jnp.int32, (TILE, TILE), 1)
    r64 = lax.broadcasted_iota(jnp.int32, (NB, NB), 0)
    c64 = lax.broadcasted_iota(jnp.int32, (NB, NB), 1)
    w[:TILE, :] = tile
    w[TILE:, :] = jnp.where(rows == cols, F32(1), F32(0))
    for lo in range(0, TILE, NB):
        hi = lo + NB
        below = TILE - hi
        m = eliminate(w[lo:hi, lo:hi]).T
        inv_t = jnp.where(r64 <= c64, m[NB:], F32(0))
        p = dot_nn(w[hi : TILE + hi, lo:hi], inv_t)
        l_ref[lo:hi, lo:hi] = jnp.where(r64 >= c64, m[:NB], F32(0))
        it_ref[:hi, lo:hi] = p[below:]
        if lo:
            l_ref[:lo, lo:hi] = jnp.zeros((lo, NB), F32)
        if below:
            l_ref[hi:, lo:hi] = p[:below]
            it_ref[hi:, lo:hi] = jnp.zeros((below, NB), F32)
            w[hi : TILE + hi, hi:] = w[hi : TILE + hi, hi:] - dot_nt(p, p[:below])
    return it_ref[...]


def factor0_kernel(idx, *rest):
    got = rest[:2]
    l_ref, it_ref, lb_ref, t11, t21, t22, top, w = rest[2:]
    core = idx[0] % 2
    for x in range(N_X):
        for other in range(2):
            base = pl.multiple_of((2 * x + (core + other) % 2) * SUB, SUB)
            top[:, :, pl.ds(base, SUB), :] = got[other][x]
    inv_t = factor_tile(top[0, 0], l_ref, it_ref, w)
    low1 = dot_nn(top[0, 1], inv_t).astype(BF16)
    low2 = dot_nn(top[2, 1].T, inv_t).astype(BF16)
    lb_ref[0] = low1
    lb_ref[1] = low2
    t11[...] = top[1, 0] - dot_bf(low1, low1)
    t21[...] = top[1, 1] - dot_bf(low2, low1)
    t22[...] = top[2, 0] - dot_bf(low2, low2)


def factor1_kernel(t11, t21, t22, l_ref, it_ref, lb_ref, rest_ref, w):
    inv_t = factor_tile(t11[...], l_ref, it_ref, w)
    low = dot_nn(t21[...], inv_t).astype(BF16)
    lb_ref[...] = low
    rest_ref[...] = t22[...] - dot_bf(low, low)


def factor2_kernel(t22, l_ref, it_ref, w):
    factor_tile(t22[...], l_ref, it_ref, w)


SQUARE = jax.ShapeDtypeStruct((TILE, TILE), F32)
FACTOR_COST = pl.CostEstimate(flops=15_000_000_000, transcendentals=0, bytes_accessed=2_000_000)
WORK = [pltpu.VMEM((2 * TILE, TILE), F32)]


def factor0(idx, got):
    return pl.pallas_call(
        factor0_kernel,
        out_shape=[SQUARE, SQUARE, jax.ShapeDtypeStruct((2, TILE, TILE), BF16), SQUARE, SQUARE, SQUARE],
        in_specs=[SMEM] + [VMEM] * 2,
        out_specs=[VMEM] * 6,
        scratch_shapes=[pltpu.VMEM((PANELS, 2, TILE, TILE), F32)] + WORK,
        cost_estimate=FACTOR_COST,
        compiler_params=PARAMS,
        name="factor0",
    )(idx, *got)


def factor1(t11, t21, t22):
    return pl.pallas_call(
        factor1_kernel,
        out_shape=[SQUARE, SQUARE, jax.ShapeDtypeStruct((TILE, TILE), BF16), SQUARE],
        in_specs=[VMEM] * 3,
        out_specs=[VMEM] * 4,
        scratch_shapes=WORK,
        cost_estimate=FACTOR_COST,
        compiler_params=PARAMS,
        name="factor1",
    )(t11, t21, t22)


def factor2(t22):
    return pl.pallas_call(
        factor2_kernel,
        out_shape=[SQUARE, SQUARE],
        in_specs=[VMEM],
        out_specs=[VMEM] * 2,
        scratch_shapes=WORK,
        cost_estimate=FACTOR_COST,
        compiler_params=PARAMS,
        name="factor2",
    )(t22)


def solve_kernel(idx, it0, it1, it2, lb0, lb1, *rest):
    got, out, rows = rest[:N_Z], rest[N_Z], rest[N_Z + 1]
    r, y, z = idx[0], idx[1], idx[2]
    for s in range(N_Z):
        source = (z + N_Z - s) % N_Z

        @pl.when(source < PANELS)
        def _():
            rows[source] = got[s][...]

    chunk = HALVES * SUB
    half = lax.broadcasted_iota(jnp.int32, (chunk, TILE), 0) // SUB
    tile_row = (half * N_Y + y) * N_ROW + r

    def keep(k, left, inverse):
        return jnp.where(tile_row > k, dot_nn(left, inverse[...]), F32(0)).astype(BF16)

    s0 = keep(0, rows[0].reshape(chunk, TILE), it0)
    s1 = keep(1, rows[1].reshape(chunk, TILE) - dot_bf(s0, lb0[0]), it1)
    s2 = keep(2, rows[2].reshape(chunk, TILE) - dot_bf(s0, lb0[1]) - dot_bf(s1, lb1[...]), it2)
    for k, done in enumerate((s0, s1, s2)):
        out[:, :, k * TILE : (k + 1) * TILE] = done.reshape(HALVES, SUB, TILE)


def solve(idx, inverses, lb0, lb1, got):
    return pl.pallas_call(
        solve_kernel,
        out_shape=jax.ShapeDtypeStruct((HALVES, SUB, PANELS * TILE), BF16),
        in_specs=[SMEM] + [VMEM] * (PANELS + 2 + N_Z),
        out_specs=VMEM,
        scratch_shapes=[pltpu.VMEM((PANELS, HALVES, SUB, TILE), F32)],
        compiler_params=PARAMS,
        name="solve",
    )(idx, *inverses, lb0, lb1, *got)


def join_z_kernel(idx, *rest):
    got, outs = rest[:N_Z], rest[N_Z:]
    for s in range(N_Z):
        base = pl.multiple_of((idx[2] + N_Z - s) % N_Z * SUB, SUB)
        for h in range(HALVES):
            outs[h][pl.ds(base, SUB), :] = got[s][h]


def join_z(idx, got):
    return pl.pallas_call(
        join_z_kernel,
        out_shape=[jax.ShapeDtypeStruct((TILE, PANELS * TILE), BF16)] * HALVES,
        in_specs=[SMEM] + [VMEM] * N_Z,
        out_specs=[VMEM] * HALVES,
        compiler_params=PARAMS,
        name="join_z",
    )(idx, *got)


def join_x_kernel(idx, *rest):
    got, out = rest[:-1], rest[-1]
    for s in range(N_X):
        out[(idx[0] // 2 + N_X - s) % N_X] = got[s][...]


def join_x(idx, got):
    return pl.pallas_call(
        join_x_kernel,
        out_shape=jax.ShapeDtypeStruct((N_X,) + got[0].shape, got[0].dtype),
        in_specs=[SMEM] + [VMEM] * N_X,
        out_specs=VMEM,
        compiler_params=PARAMS,
        name="join_x",
    )(idx, *got)


def join_cols_kernel(idx, own, other, out):
    core = idx[0] % 2
    for n, ref in enumerate((own, other)):
        for x in range(N_X):
            base = pl.multiple_of((2 * x + (core + n) % 2) * SUB, SUB)
            out[:, pl.ds(base, SUB), :] = ref[x]


def join_cols(idx, parts):
    return pl.pallas_call(
        join_cols_kernel,
        out_shape=jax.ShapeDtypeStruct((HALVES, TILE, PANELS * TILE), BF16),
        in_specs=[SMEM, VMEM, VMEM],
        out_specs=VMEM,
        compiler_params=PARAMS,
        name="join_cols",
    )(idx, *parts)


def part_tile(n, idx, shifts):
    shift = shifts[0] + (shifts[-1] - shifts[0]) * (n // HALVES)
    return n % HALVES * N_Y + (idx[1] + N_Y - shift) % N_Y


def update_kernel(shifts, idx, a_ref, c_all, *rest):
    count = HALVES * len(shifts)
    row_parts, rest = rest[:count], rest[count:]
    factors, inverses, rest = rest[:PANELS], rest[PANELS : 2 * PANELS], rest[2 * PANELS :]
    out, s_all, l_own, it_own, row_sem, own_sem = rest[-6:]
    r, c = idx[0], idx[3]
    n = pl.program_id(0)
    n_col = N_Y * N_Z

    def own_copies(k):
        return (
            pltpu.make_async_copy(factors[k], l_own, own_sem.at[0]),
            pltpu.make_async_copy(inverses[k], it_own, own_sem.at[1]),
        )

    @pl.when(n == 0)
    def _():
        for m in range(count):
            pltpu.make_async_copy(row_parts[m], s_all.at[m], row_sem.at[m]).start()
        for k in range(PANELS):

            @pl.when(c == k)
            def _():
                for copy in own_copies(k):
                    copy.start()

    pltpu.make_async_copy(row_parts[0], s_all.at[n], row_sem.at[n]).wait()
    i = part_tile(n, idx, shifts) * N_ROW + r
    for u in range(HALVES):
        lanes = slice(u * TILE, (u + 1) * TILE)
        j = c + u * n_col

        @pl.when(i >= j)
        def _():
            out[:, lanes] = a_ref[:, lanes] - dot_bf(s_all[n], c_all[u])

        @pl.when(i < j)
        def _():
            out[:, lanes] = a_ref[:, lanes]

    @pl.when(jnp.logical_and(c < PANELS, n == 0))
    def _():
        for copy in own_copies(0):
            copy.wait()

    @pl.when(jnp.logical_and(c < PANELS, i > c))
    def _():
        out[:, :TILE] = dot_nn(out[:, :TILE], it_own[...])

    @pl.when(jnp.logical_and(c < PANELS, i == c))
    def _():
        out[:, :TILE] = l_own[...]


def update(idx, matrix, done, col_rows, row_parts, shifts, factors, inverses):
    count = HALVES * len(shifts)
    block = pl.BlockSpec((TILE, matrix.shape[1]), lambda n, idx: (part_tile(n, idx, shifts), 0))
    operands = [idx, matrix, col_rows, *row_parts, *factors, *inverses]
    in_specs = [block] + [VMEM] * (1 + count) + [ANY] * (2 * PANELS)
    aliases = {}
    if done is not None:
        aliases = {len(operands): 0}
        operands.append(done)
        in_specs.append(ANY)
    return pl.pallas_call(
        lambda *refs: update_kernel(shifts, *refs),
        grid_spec=pltpu.PrefetchScalarGridSpec(
            num_scalar_prefetch=1,
            grid=(count,),
            in_specs=in_specs,
            out_specs=block,
            scratch_shapes=[
                pltpu.VMEM((count, TILE, PANELS * TILE), BF16),
                pltpu.VMEM((TILE, TILE), F32),
                pltpu.VMEM((TILE, TILE), F32),
                pltpu.SemaphoreType.DMA((count,)),
                pltpu.SemaphoreType.DMA((2,)),
            ],
        ),
        out_shape=jax.ShapeDtypeStruct(matrix.shape, F32),
        input_output_aliases=aliases,
        compiler_params=PARAMS,
        name="update",
    )(*operands)


def on_device(matrix):
    row_index = lax.axis_index("row")
    col_index = lax.axis_index("col")
    y_index, z_index = col_index // N_Z, col_index % N_Z
    idx = jnp.stack([row_index, y_index, z_index, col_index]).astype(jnp.int32)
    barrier = lax.optimization_barrier

    sent = pack_top(idx, matrix[:TILE, :TILE])
    tiles = pack_y(matrix[:, :TILE])
    slices = pick_row(idx, [sent[0]] + [row_shift(sent[s], s) for s in range(1, N_ROW)])
    slices = lax.select_n(y_index, slices, *[y_shift(slices, s) for s in range(1, N_Y)])
    slices, tiles = barrier((slices, tiles))
    slices = jnp.where(z_index < Z_GROUP, slices, z_shift(slices, Z_GROUP))
    top = pick_top(idx, [slices] + [z_group_shift(slices, s) for s in range(1, Z_GROUP)])
    top = join_x(idx, [top] + [x_shift(top, s) for s in range(1, N_X)])
    top_parts = [top, core_swap(top)]
    top_parts, tiles = barrier((top_parts, tiles))

    shifted = [y_shift(tiles[s], s) for s in range(1, N_Y)]
    l0, it0, lb0, t11, t21, t22 = factor0(idx, top_parts)
    l1, it1, lb1, t22 = factor1(t11, t21, t22)
    tiles, shifted, t22 = barrier((tiles, shifted, t22))
    sent = pack_z(idx, tiles[0], shifted)
    sent, t22 = barrier((sent, t22))
    scattered = [sent[0]] + [z_shift(sent[s], s) for s in range(1, N_Z)]
    l2, it2 = factor2(t22)
    solved = solve(idx, [it0, it1, it2], lb0, lb1, scattered)

    swapped = row_z_swap(solved)
    over_z = [solved] + [z_shift(solved, s) for s in range(1, N_Z) if s != N_Z // 2]
    over_z.insert(N_Z // 2, z_shift(over_z[N_Z // 2 - 1], 1))
    over_x = [swapped] + [x_shift(swapped, s) for s in range(1, N_X)]
    low, high = join_z(idx, over_z)
    low, high, over_x = barrier((low, high, over_x))
    col_half = join_x(idx, over_x)
    low_up, high_down = y_shift(low, 1), y_shift(high, N_Y - 1)
    high_up, low_down = y_shift(high, 1), y_shift(low, N_Y - 1)
    low_far, high_far = y_shift(low_up, 1), y_shift(high_down, N_Y - 1)
    own = ([l0, l1, l2], [it0, it1, it2])
    col_rows = join_cols(idx, [col_half, core_swap(col_half)])
    out = update(idx, matrix, None, col_rows, [low, high], (0,), *own)
    out = update(idx, matrix, out, col_rows, [low_up, high_up, low_down, high_down], (1, N_Y - 1), *own)
    return update(idx, matrix, out, col_rows, [low_far, high_far], (N_Y // 2,), *own)


def solution(mesh):
    return jax.shard_map(
        on_device, mesh=mesh, in_specs=(P("row", "col"),), out_specs=P("row", "col"), check_vma=False
    )
```
